32 devices in a mesh: rep: 2 (over core), shard: 16 (over z, y, x).
Axes of the slice: x: 2, y: 2, z: 4, core: 2. Of those that a mesh axis runs over, the one named last changes fastest.
Arguments:
- tokens: bfloat16 [32, 1024, 768], P('rep', 'shard'), may hold values from -6 to 6
- cotangent: bfloat16 [32, 1024, 768], P('rep', 'shard'), may hold values from -6 to 6
- lengths: int32 [2, 16], P('rep'), may hold values from 512 to 1024, as said below
- order: int32 [2, 16], P('rep'), may hold values from 0 to 15, each once within a row
- norm_weight: bfloat16 [768], P('shard'), may hold values from 0.099609375 to 1.8984375
- in_weight: bfloat16 [768, 3352], P('shard'), may hold values from -0.21875 to 0.21875
- conv_weight: bfloat16 [1792, 4], P('shard'), may hold values from -3 to 3
- conv_bias: bfloat16 [1792], P('shard'), may hold values from -3 to 3
- step_bias: float32 [24], replicated, may hold values from -5.5 to -2.5
- decay_log: float32 [24], replicated, may hold values from 0 to 2.77
- skip_gain: float32 [24], replicated, may hold values from 0.5 to 1.5
- gate_norm_weight: bfloat16 [1536], P('shard'), may hold values from 0.099609375 to 1.8984375
- out_weight: bfloat16 [1536, 768], P('shard'), may hold values from -0.15625 to 0.15625
Outputs:
- output: bfloat16 [32, 1024, 768], P('rep', 'shard')
- input_grad: bfloat16 [32, 1024, 768], P('rep', 'shard')
- grad_norm: float32 [768], P('shard')
- grad_in: float32 [768, 3352], P('shard')
- grad_conv: float32 [1792, 4], P('shard')
- grad_conv_bias: float32 [1792], P('shard')
- grad_step_bias: float32 [24], replicated
- grad_decay_log: float32 [24], replicated
- grad_skip: float32 [24], replicated
- grad_gate_norm: float32 [1536], P('shard')
- grad_out: float32 [1536, 768], P('shard')
The draws below stay inside these ranges and needn't reach their ends.
Inputs may be any that keep to these rules, and one draw needn't show every extreme that they name: Each row of order holds every number from 0 to 15 once: slot k of group r holds sequence order[r, k]. lengths[r, s] counts the valid leading positions of sequence s of group r; each row has one entry equal to 1024 and one equal to 512.
All inputs are finite; a program needn't handle non-finite values.
Results may differ from the reference program's by a relative error of at most 0.012.
The reference program's roundings to bfloat16 on the way count: a program that leaves them out, or rounds other values in their place, can miss the bound.
Values may be sent and summed in bfloat16 or wider, within the bound.
A program may use at most 192 MiB of HBM per device.

```python
import jax
import jax.numpy as jnp
from jax import lax

D = 768
HEADS = 24
HEADDIM = 64
STATE = 128
CONV = 4
SPAN = 256
SEQ_LEN = 1024
DI = 1536
XBC = 1792
PROJ = 3352
SEQS = 32
N_REP = 2
N_SHARD = 16


def draw_lengths(key, part):
    first_key, second_key = jax.random.split(key, 2)
    spread = jax.random.randint(first_key, (N_REP, N_SHARD), SEQ_LEN // 2, SEQ_LEN + 1)
    picked = jax.random.randint(second_key, (N_REP,), 0, N_SHARD)
    column = jnp.arange(N_SHARD)[None, :]
    spread = jnp.where(column == picked[:, None], SEQ_LEN, spread)
    spread = jnp.where(column == (picked[:, None] + 1) % N_SHARD, SEQ_LEN // 2, spread)
    return spread.astype(jnp.int32)


def shard_levels(own_key, shape, cuts, least, top_value):
    level, own = 1.0, jax.random.fold_in(own_key, 6)
    for position, shards_of in cuts:
        heights = jnp.exp(jax.random.uniform(jax.random.fold_in(own, position), (shards_of,), jnp.float32, least / len(cuts), top_value / len(cuts)))
        level = level * jnp.repeat(heights, shape[position] // shards_of).reshape([-1 if axis == position else 1 for axis in range(len(shape))])
    return level


def centred(own_key, shape, width, most, pieces=(), held_as=jnp.bfloat16):
    drawn = jax.random.normal(own_key, shape, jnp.float32) * width
    if len(pieces) > 0:
        drawn = shard_levels(own_key, shape, pieces, -0.22, 0.18) * drawn
    return jnp.clip(drawn, min=-most, max=most).astype(held_as)


def setup_inputs(seed: int = 0) -> dict:
    streams_of = jax.random.split(jax.random.key(seed), 14)
    tokens = centred(streams_of[0], (SEQS, SEQ_LEN, D), 1.0, 6.0, ((0, 2), (1, 16)))
    cotangent = centred(streams_of[1], (SEQS, SEQ_LEN, D), 1.0, 6.0, ((0, 2), (1, 16)))
    lengths = draw_lengths(jax.random.fold_in(streams_of[13], 71), 0)
    order = jax.vmap(lambda own: jax.random.permutation(own, N_SHARD))(jax.random.split(streams_of[3], N_REP)).reshape((N_REP, N_SHARD)).astype(jnp.int32)
    norm_weight = jnp.clip(1.0 + 0.18 * jax.random.normal(streams_of[4], (D,), jnp.float32), 0.099609375, 1.8984375).astype(jnp.bfloat16)
    in_weight = centred(streams_of[5], (D, PROJ), D ** -0.5, 0.21875, ((0, 16),))
    conv_weight = centred(streams_of[6], (XBC, CONV), CONV ** -0.5, 3.0, ((0, 16),))
    conv_bias = centred(streams_of[7], (XBC,), 0.5, 3.0, ((0, 16),))
    step_bias = jnp.clip(jax.random.uniform(streams_of[8], (HEADS,), jnp.float32, -5.5, -2.5), -5.5, -2.5)
    decay_log = jnp.clip(jax.random.uniform(streams_of[9], (HEADS,), jnp.float32, 0.0, 2.77), 0.0, 2.77)
    skip_gain = jnp.clip(jax.random.uniform(streams_of[10], (HEADS,), jnp.float32, 0.5, 1.5), 0.5, 1.5)
    gate_norm_weight = jnp.clip(1.0 + 0.18 * jax.random.normal(streams_of[11], (DI,), jnp.float32), 0.099609375, 1.8984375).astype(jnp.bfloat16)
    out_weight = centred(streams_of[12], (DI, D), DI ** -0.5, 0.15625, ((0, 16),))
    return dict(tokens=tokens, cotangent=cotangent, lengths=lengths, order=order, norm_weight=norm_weight, in_weight=in_weight, conv_weight=conv_weight, conv_bias=conv_bias, step_bias=step_bias, decay_log=decay_log, skip_gain=skip_gain, gate_norm_weight=gate_norm_weight, out_weight=out_weight)


epsilon = 1e-05
highest = lax.Precision.HIGHEST

@jax.custom_vjp
def low(v):
    return lax.optimization_barrier(v.astype(jnp.bfloat16)).astype(jnp.float32)

@jax.custom_vjp
def low_back(v):
    return v

def low_keep(v):
    return (low(v), None)

def low_pass(kept, grad):
    return (grad,)

def back_keep(v):
    return (v, None)

def back_low(kept, grad):
    return (low(grad),)
low.defvjp(low_keep, low_pass)
low_back.defvjp(back_keep, back_low)

def decay_terms(log_block, step_block):
    cumul = jnp.cumsum(log_block, axis=0)
    cumul_heads = cumul.T
    positions = log_block.shape[0]
    causal = jnp.arange(positions)[:, None] >= jnp.arange(positions)[None, :]
    spread = jnp.where(causal[None], cumul_heads[:, :, None] - cumul_heads[:, None, :], 0.0)
    factor = jnp.where(causal[None], jnp.exp(spread), 0.0) * step_block.T[:, None, :]
    carry_weight = jnp.exp(cumul[-1][None, :] - cumul) * step_block
    return (factor, carry_weight, jnp.exp(cumul), jnp.exp(cumul[-1]))

def norm_part(tok_float, norm_gain):
    return tok_float * lax.rsqrt(lax.optimization_barrier(jnp.mean(tok_float * tok_float, axis=-1, keepdims=True)) + epsilon) * norm_gain

def conv_part(conv_in, conv_taps, conv_shift):
    length = conv_in.shape[0]
    padded = jnp.concatenate([jnp.zeros((CONV - 1, conv_in.shape[1]), jnp.float32), conv_in], axis=0)
    total = conv_shift[None, :] + jnp.zeros_like(conv_in)
    for tap in range(CONV):
        total = total + conv_taps[:, tap][None, :] * padded[tap:tap + length]
    return jax.nn.silu(total)

def step_part(step_raw, step_bias, decay_log):
    step_size = jax.nn.softplus(step_raw + step_bias[None, :])
    return (step_size, -jnp.exp(decay_log)[None, :] * step_size)

def gate_part(scan_out, heads_in, skip_gain, gate_raw, gate_gain):
    mixed = scan_out + jnp.repeat(skip_gain, HEADDIM)[None, :] * heads_in
    gated = mixed * jax.nn.silu(gate_raw)
    return gated * lax.rsqrt(lax.optimization_barrier(jnp.mean(gated * gated, axis=-1, keepdims=True)) + epsilon) * gate_gain

def ref_block(state, inputs):
    heads_blk, keys_blk, query_blk, step_blk, log_blk = inputs
    factor, carry_weight, growth, growth_last = decay_terms(log_blk, step_blk)
    scores = low_back(jnp.dot(query_blk, keys_blk.T, precision=highest))
    mixing = low(scores[None] * factor)
    within = low_back(jnp.einsum('hts,shp->thp', mixing, heads_blk, precision=highest))
    across = low_back(jnp.einsum('tn,hpn->thp', query_blk, low(state), precision=highest))
    result = within + growth[:, :, None] * across
    weighted = low(heads_blk * carry_weight[:, :, None])
    contrib = low_back(jnp.einsum('sn,shp->hpn', keys_blk, weighted, precision=highest))
    return (growth_last[:, None, None] * state + contrib, result)

def mixer(tok_float, keep_row, norm_gain, in_matrix, conv_taps, conv_shift, step_bias, decay_log, skip_gain, gate_gain, out_matrix):
    normed = norm_part(tok_float, norm_gain)
    projected = low_back(jnp.dot(low(normed), in_matrix, precision=highest))
    gate_raw = projected[:, :DI]
    conv_in = projected[:, DI:DI + XBC]
    step_raw = projected[:, DI + XBC:]
    convolved = conv_part(conv_in, conv_taps, conv_shift)
    heads_in = convolved[:, :DI]
    heads_low = low(heads_in)
    key_low = low(convolved[:, DI:DI + STATE])
    query_low = low(convolved[:, DI + STATE:])
    step_size, log_decay = step_part(step_raw, step_bias, decay_log)
    count = SEQ_LEN // SPAN
    inputs = (heads_low.reshape(count, SPAN, HEADS, HEADDIM), key_low.reshape(count, SPAN, STATE), query_low.reshape(count, SPAN, STATE), step_size.reshape(count, SPAN, HEADS), log_decay.reshape(count, SPAN, HEADS))
    start = jnp.zeros((HEADS, HEADDIM, STATE), jnp.float32)
    final_state, blocks = lax.scan(jax.checkpoint(ref_block), start, inputs)
    scan_out = blocks.reshape(SEQ_LEN, DI)
    gate_value = gate_part(scan_out, heads_in, skip_gain, gate_raw, gate_gain)
    branch = low_back(jnp.dot(low(gate_value), out_matrix, precision=highest))
    return tok_float + keep_row[:, None] * branch

def reference(tokens, cotangent, lengths, order, norm_weight, in_weight, conv_weight, conv_bias, step_bias, decay_log, skip_gain, gate_norm_weight, out_weight):
    params = (norm_weight.astype(jnp.float32), in_weight.astype(jnp.float32), conv_weight.astype(jnp.float32), conv_bias.astype(jnp.float32), step_bias.astype(jnp.float32), decay_log.astype(jnp.float32), skip_gain.astype(jnp.float32), gate_norm_weight.astype(jnp.float32), out_weight.astype(jnp.float32))
    slot_length = jnp.take_along_axis(lengths, order, axis=1).reshape(SEQS)
    keep = (jnp.arange(SEQ_LEN, dtype=jnp.int32)[None, :] < slot_length[:, None]).astype(jnp.float32)

    def one_seq(totals, item):
        tok_seq, cot_seq, keep_row = item

        def forward(tok_float, norm_gain, in_matrix, conv_taps, conv_shift, bias_heads, log_heads, skip_heads, gate_gain, out_matrix):
            return mixer(tok_float, keep_row, norm_gain, in_matrix, conv_taps, conv_shift, bias_heads, log_heads, skip_heads, gate_gain, out_matrix)
        result, pull = jax.vjp(forward, tok_seq.astype(jnp.float32), *params)
        grads = pull(cot_seq.astype(jnp.float32))
        summed = tuple((total + grad for total, grad in zip(totals, grads[1:])))
        return (summed, (result.astype(jnp.bfloat16), grads[0].astype(jnp.bfloat16)))
    zeros = tuple((jnp.zeros_like(param) for param in params))
    totals, stacked = lax.scan(one_seq, zeros, (tokens, cotangent, keep))
    return (stacked[0], stacked[1], totals[0], totals[1], totals[2], totals[3], totals[4], totals[5], totals[6], totals[7], totals[8])
```

```python
import functools

import jax
import jax.numpy as jnp
from jax import lax
from jax.experimental import pallas as pl
from jax.experimental.pallas import tpu as pltpu
from jax.sharding import PartitionSpec as P

HEADS = 24
HEADDIM = 64
STATE = 128
CONV = 4
SPAN = 256
DI = 1536
XBC = 1792
TILE = 128
PAIRS = DI // TILE
HALF = SPAN // 2
EDGE = 8
epsilon = 1e-05
F32 = jnp.float32
BF16 = jnp.bfloat16
FULL = lax.Precision.HIGHEST


def mul(a, b):
    return jnp.dot(a, b, preferred_element_type=F32)


def mul_nt(a, b):
    return lax.dot_general(a, b, (((1,), (1,)), ((), ())), preferred_element_type=F32)


def mul_tn(a, b):
    return lax.dot_general(a, b, (((0,), (0,)), ((), ())), preferred_element_type=F32)


def sigmoid(v):
    return 0.5 * jnp.tanh(0.5 * v) + 0.5


def softplus(v):
    return jnp.maximum(v, 0.0) + jnp.log1p(jnp.exp(-jnp.abs(v)))


def fold(v):
    return jnp.sum(v.reshape(v.shape[0] // EDGE, EDGE, v.shape[1]), axis=0)


def tile_at(j, base=0):
    return pl.ds(pl.multiple_of(base + j * TILE, TILE), TILE)


def lane_low(shape):
    return lax.broadcasted_iota(jnp.int32, shape, 1) < HEADDIM


def spread(column, h):
    return jnp.broadcast_to(column[:, h : h + 1], (column.shape[0], TILE))


def conv_argument(cin_ref, cw_ref, cb_ref, cols):
    total = cb_ref[:, cols]
    for tap in range(CONV):
        start = EDGE - CONV + 1 + tap
        total = total + cw_ref[tap : tap + 1, cols] * cin_ref[0, start : start + SPAN, cols]
    return total


def head_times(step_raw, step_bias, decay_log):
    shifted = step_raw + step_bias
    step = softplus(shifted)
    log_decay = -jnp.exp(decay_log) * step
    rows = lax.broadcasted_iota(jnp.int32, (SPAN, SPAN), 0)
    columns = lax.broadcasted_iota(jnp.int32, (SPAN, SPAN), 1)
    lower = (rows >= columns).astype(F32)
    cumul = jnp.dot(lower, log_decay, precision=FULL, preferred_element_type=F32)
    return shifted, step, cumul, cumul - jnp.log(step)


def causal_mask(flip):
    rows = lax.broadcasted_iota(jnp.int32, (HALF, HALF), 0)
    columns = lax.broadcasted_iota(jnp.int32, (HALF, HALF), 1)
    return columns >= rows if flip else rows >= columns


def forward_kernel(
    len_ref, tok_ref, w_ref, ow_ref, nw_ref, cw_ref, cb_ref, sb_ref, dl_ref, sk_ref, gn_ref,
    out_ref, cin_ref, gr_ref, mx_ref, st_ref, sr_ref, nl_ref, gl_ref,
    ws, col_t, pair_s, row_s, state, scores, gated,
):
    block = pl.program_id(0)
    offset = block * SPAN

    @pl.when(block == 0)
    def _():
        ws[...] = jnp.zeros_like(ws)
        ws[:, :HEADS] = w_ref[:, DI + XBC : DI + XBC + HEADS]
        state[...] = jnp.zeros_like(state)
        cin_ref[0, :EDGE, :] = jnp.zeros((EDGE, XBC), F32)

    @pl.when(block > 0)
    def _():
        cin_ref[0, :EDGE, :] = gated[:EDGE, :]

    for r in range(0, SPAN, 64):
        tok = tok_ref[r : r + 64, :].astype(F32)
        nrm = lax.rsqrt(jnp.mean(tok * tok, axis=-1, keepdims=True) + epsilon)
        nl_ref[r : r + 64, :] = (tok * nrm * nw_ref[...]).astype(BF16)
    low = nl_ref[...]
    sr_ref[...] = mul(low, ws[...])
    for n in range(0, XBC, 256):
        cin_ref[0, EDGE:, n : n + 256] = mul(low, w_ref[:, DI + n : DI + n + 256])
    for n in range(0, DI, 256):
        gr_ref[:, n : n + 256] = mul(low, w_ref[:, n : n + 256])

    _, _, cumul, shift = head_times(sr_ref[...], sb_ref[...], dl_ref[...])
    row_s[...] = shift.T
    low_lanes = lane_low((SPAN, TILE))
    for h in range(HEADS):
        col_t[h] = spread(cumul, h)
    for j in range(PAIRS):
        pair_s[j] = jnp.where(low_lanes, spread(shift, 2 * j), spread(shift, 2 * j + 1))

    def act(jt):
        arg = conv_argument(cin_ref, cw_ref, cb_ref, tile_at(jt))
        return arg * sigmoid(arg)

    key = act(PAIRS).astype(BF16)
    query = act(PAIRS + 1).astype(BF16)
    key_t = key.astype(F32).T.astype(BF16)
    scores[...] = mul_nt(query, key)
    st_ref[0] = state[...]
    mask = causal_mask(False)

    def pair(j, total):
        cols = tile_at(j)
        heads_in = act(j)
        heads_low = heads_in.astype(BF16)
        cum0, cum1 = col_t[2 * j], col_t[2 * j + 1]
        cum = jnp.where(low_lanes, cum0, cum1)
        last = cum[SPAN - 1 : SPAN, :]
        old = state[:, cols]
        across = mul(query, old.astype(BF16))
        weighted = (heads_low.astype(F32) * jnp.exp(last - pair_s[j])).astype(BF16)
        state[:, cols] = jnp.exp(last) * old + mul(key_t, weighted)
        zero = jnp.zeros_like(heads_low)
        parts = (jnp.where(low_lanes, heads_low, zero), jnp.where(low_lanes, zero, heads_low))
        top, bottom = [], []
        for h in range(2):
            col = (cum0, cum1)[h]
            row = row_s[pl.ds(2 * j + h, 1), :]
            first = jnp.where(mask, col[:HALF] - row[:, :HALF], -jnp.inf)
            top.append((scores[:HALF, :HALF] * jnp.exp(first)).astype(BF16))
            full = col[HALF:] - row[:, :HALF]
            bottom.append((scores[HALF:, :HALF] * jnp.exp(full)).astype(BF16))
            second = jnp.where(mask, col[HALF:] - row[:, HALF:], -jnp.inf)
            bottom.append((scores[HALF:, HALF:] * jnp.exp(second)).astype(BF16))
        tops = jnp.concatenate([p[:HALF] for p in parts], axis=0)
        within = jnp.concatenate(
            [
                mul(jnp.concatenate(top, axis=1), tops),
                mul(jnp.concatenate(bottom, axis=1), jnp.concatenate(parts, axis=0)),
            ],
            axis=0,
        )
        mixed = within + jnp.exp(cum) * across + sk_ref[:, cols] * heads_in
        mx_ref[:, cols] = mixed
        gate = gr_ref[:, cols]
        value = mixed * (gate * sigmoid(gate))
        gated[:, cols] = value
        return total + value * value

    total = lax.fori_loop(0, PAIRS, pair, jnp.zeros((SPAN, TILE), F32))
    rms = lax.rsqrt(jnp.sum(total, axis=-1, keepdims=True) * (1.0 / DI) + epsilon)

    def finish(j, carry):
        cols = tile_at(j)
        gl_ref[:, cols] = (gated[:, cols] * rms * gn_ref[:, cols]).astype(BF16)
        return carry

    lax.fori_loop(0, PAIRS, finish, 0)
    positions = offset + lax.broadcasted_iota(jnp.int32, (SPAN, 256), 0)
    valid = positions < len_ref[0]
    for n in range(0, tok_ref.shape[1], 256):
        branch = mul(gl_ref[...], ow_ref[:, n : n + 256])
        tok = tok_ref[:, n : n + 256].astype(F32)
        out_ref[:, n : n + 256] = (tok + jnp.where(valid, branch, 0.0)).astype(BF16)
    gated[:EDGE, :] = cin_ref[0, SPAN:, :]


def backward_kernel(
    len_ref, cot_ref, tok_ref, w_ref, ow_ref, nw_ref, cw_ref, cb_ref, sb_ref, dl_ref, sk_ref, gn_ref,
    cin_ref, gr_ref, mx_ref, st_ref, sr_ref,
    ig_ref, gp_ref, taps_ref, gcb_ref, ggn_ref, gsk_ref, gnw_ref, ghd_ref,
    ws, col_s, pair_t, row_t, later, scores, grad_scores, gg, sig, gpre, args, acc_q, acc_k, acc_u, acc_v, acc_l,
):
    step_id = pl.program_id(0)
    count = pl.num_programs(0)
    offset = (count - 1 - step_id) * SPAN

    @pl.when(step_id == 0)
    def _():
        ws[...] = jnp.zeros_like(ws)
        ws[:, :HEADS] = w_ref[:, DI + XBC : DI + XBC + HEADS]
        later[...] = jnp.zeros_like(later)
        gpre[SPAN:, :] = jnp.zeros((EDGE, XBC), F32)
        for ref in (taps_ref, gcb_ref, ggn_ref, gsk_ref, gnw_ref, ghd_ref):
            ref[...] = jnp.zeros_like(ref)

    width = cot_ref.shape[1]
    positions = offset + lax.broadcasted_iota(jnp.int32, (SPAN, width), 0)
    grad_branch = jnp.where(positions < len_ref[0], cot_ref[...].astype(F32), 0.0).astype(BF16)
    for n in range(0, DI, 256):
        gg[:, n : n + 256] = mul_nt(grad_branch, ow_ref[n : n + 256, :])

    shifted, step, cumul, shift = head_times(sr_ref[...], sb_ref[...], dl_ref[...])
    row_t[...] = cumul.T
    low_lanes = lane_low((SPAN, TILE))
    for h in range(HEADS):
        col_s[h] = spread(shift, h)
    for j in range(PAIRS):
        pair_t[j] = jnp.where(low_lanes, spread(cumul, 2 * j), spread(cumul, 2 * j + 1))

    def sums(j, carry):
        squares, crossed = carry
        cols = tile_at(j)
        gate = gr_ref[:, cols]
        part = sigmoid(gate)
        sig[:, cols] = part
        value = mx_ref[:, cols] * (gate * part)
        return squares + value * value, crossed + (gg[:, cols] * gn_ref[:, cols]) * value

    nothing = jnp.zeros((SPAN, TILE), F32)
    squares, crossed = lax.fori_loop(0, PAIRS, sums, (nothing, nothing))
    rms = lax.rsqrt(jnp.sum(squares, axis=-1, keepdims=True) * (1.0 / DI) + epsilon)
    coef = rms * rms * (jnp.sum(crossed, axis=-1, keepdims=True) * (1.0 / DI))
    rms = jnp.broadcast_to(rms, (SPAN, TILE))
    coef = jnp.broadcast_to(coef, (SPAN, TILE))

    def act(jt, slot):
        arg = conv_argument(cin_ref, cw_ref, cb_ref, tile_at(jt))
        args[:, slot * TILE : (slot + 1) * TILE] = arg
        return (arg * sigmoid(arg)).astype(BF16)

    key = act(PAIRS, 0)
    query = act(PAIRS + 1, 1)
    query_t = query.astype(F32).T.astype(BF16)
    scores[...] = mul_nt(key, query)
    grad_scores[...] = jnp.zeros_like(grad_scores)
    for ref in (acc_q, acc_k, acc_u, acc_v, acc_l):
        ref[...] = jnp.zeros_like(ref)
    mask = causal_mask(True)
    lane = lax.broadcasted_iota(jnp.int32, (2 * TILE, TILE), 0) % TILE
    head = lax.broadcasted_iota(jnp.int32, (2 * TILE, TILE), 1)

    def by_head(value, pick):
        high = value.astype(BF16)
        rest = (value - high.astype(F32)).astype(BF16)
        return mul(jnp.concatenate([high, rest], axis=1), pick)

    def pair(j, carry):
        cols = tile_at(j)
        arg = conv_argument(cin_ref, cw_ref, cb_ref, cols)
        part_x = sigmoid(arg)
        heads_in = arg * part_x
        heads_low = heads_in.astype(BF16)
        heads_float = heads_low.astype(F32)
        gate, mixed, part, gain, back = (
            gr_ref[:, cols], mx_ref[:, cols], sig[:, cols], gn_ref[:, cols], gg[:, cols]
        )
        silu = gate * part
        value = mixed * silu
        ggn_ref[:, cols] += fold(back * value * rms)
        grad_gated = rms * (back * gain - value * coef)
        grad_scan = grad_gated * silu
        gp_ref[:, cols] = (grad_gated * mixed * (part * (1.0 + gate * (1.0 - part)))).astype(BF16)
        gsk_ref[:, cols] += fold(grad_scan * heads_in)
        cum = pair_t[j]
        growth = jnp.exp(cum)
        last = cum[SPAN - 1 : SPAN, :]
        grad_low = grad_scan.astype(BF16)
        scaled = growth * grad_scan
        grad_across = scaled.astype(BF16)
        col0, col1 = col_s[2 * j], col_s[2 * j + 1]
        carry_weight = jnp.exp(last - jnp.where(low_lanes, col0, col1))
        weighted = (heads_float * carry_weight).astype(BF16)
        after = later[:, cols]
        after_low = after.astype(BF16)
        before = st_ref[0, :, cols]
        before_low = before.astype(BF16)
        across = mul(query, before_low)
        acc_k[...] += mul_nt(weighted, after_low)
        acc_q[...] += mul_nt(grad_across, before_low)
        grow_last = jnp.exp(last)
        carried = mul(key, after_low) * carry_weight
        last_sum = fold(carried * heads_float) + fold(after * before) * grow_last
        later[:, cols] = mul(query_t, grad_across) + grow_last * after
        zero = jnp.zeros_like(grad_low)
        parts = (jnp.where(low_lanes, grad_low, zero), jnp.where(low_lanes, zero, grad_low))
        top, bottom = [], []
        for h in range(2):
            col = (col0, col1)[h]
            row = row_t[pl.ds(2 * j + h, 1), :]
            mixed_top = mul_nt(heads_low[:HALF], parts[h])
            mixed_low = mul_nt(heads_low[HALF:], parts[h][HALF:])
            factor = jnp.exp(jnp.where(mask, row[:, :HALF] - col[:HALF], -jnp.inf))
            top.append((scores[:HALF, :HALF] * factor).astype(BF16))
            grad_scores[:HALF, :HALF] += mixed_top[:, :HALF] * factor
            factor = jnp.exp(row[:, HALF:] - col[:HALF])
            top.append((scores[:HALF, HALF:] * factor).astype(BF16))
            grad_scores[:HALF, HALF:] += mixed_top[:, HALF:] * factor
            factor = jnp.exp(jnp.where(mask, row[:, HALF:] - col[HALF:], -jnp.inf))
            bottom.append((scores[HALF:, HALF:] * factor).astype(BF16))
            grad_scores[HALF:, HALF:] += mixed_low * factor
        lows = jnp.concatenate([p[HALF:] for p in parts], axis=0)
        grad_heads = carried + jnp.concatenate(
            [
                mul(jnp.concatenate(top, axis=1), jnp.concatenate(parts, axis=0)),
                mul(jnp.concatenate(bottom, axis=1), lows),
            ],
            axis=0,
        )
        gain_skip = sk_ref[:, cols]
        spanned = growth * across
        within = mixed - gain_skip * heads_in - spanned
        pick = (head == 2 * j + lane // HEADDIM).astype(F32)
        pick_low = pick.astype(BF16)
        acc_u[...] += by_head(grad_low.astype(F32) * within + grad_scan * spanned, pick_low)
        acc_v[...] += by_head(heads_float * grad_heads, pick_low)
        acc_l[...] += jnp.dot(last_sum, pick[:TILE], precision=FULL, preferred_element_type=F32)
        grad_conv = grad_heads + gain_skip * grad_scan
        gpre[:SPAN, cols] = grad_conv * (part_x * (1.0 + arg * (1.0 - part_x)))
        return carry

    lax.fori_loop(0, PAIRS, pair, 0)

    rows = lax.broadcasted_iota(jnp.int32, (SPAN, SPAN), 0)
    columns = lax.broadcasted_iota(jnp.int32, (SPAN, SPAN), 1)
    upper = (columns >= rows).astype(F32)
    at_end = lax.broadcasted_iota(jnp.int32, (SPAN, TILE), 0) == SPAN - 1
    to_step = acc_v[...]
    ends = jnp.sum(acc_l[...], axis=0, keepdims=True)
    grad_cumul = acc_u[...] - to_step + jnp.where(at_end, ends, 0.0)
    grad_log = jnp.dot(upper, grad_cumul, precision=FULL, preferred_element_type=F32)
    rate = jnp.exp(dl_ref[...])
    safe = jnp.where(step > 0.0, step, 1.0)
    grad_step = jnp.where(step > 0.0, to_step / safe, 0.0)
    grad_raw = (grad_step - rate * grad_log) * sigmoid(shifted)
    ghd_ref[:EDGE, :] += fold(grad_raw)
    ghd_ref[EDGE:, :] -= fold(rate * step * grad_log)
    raw_low = grad_raw.astype(BF16)
    gp_ref[:, DI + XBC :] = raw_low[:, :HEADS]

    scores_low = grad_scores[...].astype(BF16)
    scores_t = grad_scores[...].T.astype(BF16)
    for slot, grad in (
        (0, acc_k[...] + mul(scores_low, query)),
        (1, acc_q[...] + mul(scores_t, key)),
    ):
        arg = args[:, slot * TILE : (slot + 1) * TILE]
        part = sigmoid(arg)
        gpre[:SPAN, DI + slot * TILE : DI + (slot + 1) * TILE] = grad * (part * (1.0 + arg * (1.0 - part)))

    def through_conv(j, carry):
        cols = tile_at(j)
        here = gpre[:SPAN, cols]
        gcb_ref[:, cols] += fold(here)
        total = jnp.zeros_like(here)
        for tap in range(CONV):
            start = EDGE - CONV + 1 + tap
            taps_ref[tap, :, cols] += fold(here * cin_ref[0, start : start + SPAN, cols])
            ahead = CONV - 1 - tap
            total = total + cw_ref[tap : tap + 1, cols] * gpre[ahead : ahead + SPAN, cols]
        gp_ref[:, tile_at(j, DI)] = total.astype(BF16)
        return carry

    lax.fori_loop(0, PAIRS + 2, through_conv, 0)
    gpre[SPAN:, :] = gpre[:EDGE, :]

    for n in range(0, width, 256):
        grad = mul_nt(gp_ref[:, : DI + XBC], w_ref[n : n + 256, : DI + XBC])
        gg[:, n : n + 256] = grad + mul_nt(raw_low, ws[n : n + 256, :])
    for r in range(0, SPAN, 64):
        tok = tok_ref[r : r + 64, :].astype(F32)
        nrm = lax.rsqrt(jnp.mean(tok * tok, axis=-1, keepdims=True) + epsilon)
        grad = gg[r : r + 64, :width]
        gnw_ref[...] += fold(grad * tok * nrm)
        value = grad * nw_ref[...]
        centre = jnp.mean(value * tok, axis=-1, keepdims=True) * (nrm * nrm)
        grad_tok = nrm * (value - tok * centre)
        ig_ref[r : r + 64, :] = (cot_ref[r : r + 64, :].astype(F32) + grad_tok).astype(BF16)


def whole(shape):
    return pl.BlockSpec(shape, lambda i: (0,) * len(shape), pipeline_mode=pl.Buffered(1))


def rows_of(width, last=None):
    if last is None:
        return pl.BlockSpec((SPAN, width), lambda i: (i, 0))
    return pl.BlockSpec((SPAN, width), lambda i: (last - i, 0))


def params_specs(width):
    proj = DI + XBC + HEADS
    return [
        whole((width, proj)), whole((DI, width)), whole((1, width)), whole((CONV, XBC)), whole((1, XBC)),
        whole((1, TILE)), whole((1, TILE)), whole((1, DI)), whole((1, DI)),
    ]


LIMIT = 60 * 2**20


def run_forward(valid, tok, params):
    length, width = tok.shape
    count = length // SPAN
    shapes = [
        ((length, width), BF16), ((count, SPAN + EDGE, XBC), F32), ((length, DI), F32), ((length, DI), F32),
        ((count, STATE, DI), F32), ((length, TILE), F32), ((length, width), BF16), ((length, DI), BF16),
    ]
    out_specs = [
        rows_of(width), pl.BlockSpec((1, SPAN + EDGE, XBC), lambda i: (i, 0, 0)), rows_of(DI), rows_of(DI),
        pl.BlockSpec((1, STATE, DI), lambda i: (i, 0, 0)), rows_of(TILE), rows_of(width), rows_of(DI),
    ]
    return pl.pallas_call(
        forward_kernel,
        grid=(count,),
        out_shape=[jax.ShapeDtypeStruct(s, d) for s, d in shapes],
        in_specs=[pl.BlockSpec(memory_space=pltpu.SMEM), rows_of(width), *params_specs(width)],
        out_specs=out_specs,
        scratch_shapes=[
            pltpu.VMEM((width, TILE), BF16), pltpu.VMEM((HEADS, SPAN, TILE), F32), pltpu.VMEM((PAIRS, SPAN, TILE), F32),
            pltpu.VMEM((TILE, SPAN), F32), pltpu.VMEM((STATE, DI), F32), pltpu.VMEM((SPAN, SPAN), F32), pltpu.VMEM((SPAN, XBC), F32),
        ],
        compiler_params=pltpu.CompilerParams(dimension_semantics=("arbitrary",), vmem_limit_bytes=LIMIT),
        cost_estimate=pl.CostEstimate(flops=20 * 10**9, bytes_accessed=60 * 10**6, transcendentals=10**7),
    )(valid, tok, *params)


def run_backward(valid, cot, tok, params, kept):
    length, width = tok.shape
    count = length // SPAN
    proj = DI + XBC + HEADS
    last = count - 1
    shapes = [
        ((length, width), BF16), ((length, proj), BF16), ((CONV, EDGE, XBC), F32), ((EDGE, XBC), F32), ((EDGE, DI), F32),
        ((EDGE, DI), F32), ((EDGE, width), F32), ((2 * EDGE, TILE), F32),
    ]
    out_specs = [rows_of(width, last), rows_of(proj, last), *(whole(s) for s, _ in shapes[2:])]
    kept_specs = [
        pl.BlockSpec((1, SPAN + EDGE, XBC), lambda i: (last - i, 0, 0)), rows_of(DI, last), rows_of(DI, last),
        pl.BlockSpec((1, STATE, DI), lambda i: (last - i, 0, 0)), rows_of(TILE, last),
    ]
    square, wide = pltpu.VMEM((SPAN, SPAN), F32), pltpu.VMEM((SPAN, DI), F32)
    narrow = pltpu.VMEM((SPAN, TILE), F32)
    return pl.pallas_call(
        backward_kernel,
        grid=(count,),
        out_shape=[jax.ShapeDtypeStruct(s, d) for s, d in shapes],
        in_specs=[pl.BlockSpec(memory_space=pltpu.SMEM), rows_of(width, last), rows_of(width, last), *params_specs(width), *kept_specs],
        out_specs=out_specs,
        scratch_shapes=[
            pltpu.VMEM((width, TILE), BF16), pltpu.VMEM((HEADS, SPAN, TILE), F32), pltpu.VMEM((PAIRS, SPAN, TILE), F32),
            pltpu.VMEM((TILE, SPAN), F32), pltpu.VMEM((STATE, DI), F32), square, square, wide, wide,
            pltpu.VMEM((SPAN + EDGE, XBC), F32), pltpu.VMEM((SPAN, 2 * TILE), F32),
            narrow, narrow, narrow, narrow, pltpu.VMEM((EDGE, TILE), F32),
        ],
        compiler_params=pltpu.CompilerParams(dimension_semantics=("arbitrary",), vmem_limit_bytes=LIMIT),
        cost_estimate=pl.CostEstimate(flops=40 * 10**9, bytes_accessed=60 * 10**6, transcendentals=2 * 10**7),
    )(valid, cot, tok, *params, *kept)


def prepare(norm_full, in_full, conv_full, shift_full, gate_full, out_full, step_bias, decay_log, skip_gain):
    pad = ((0, 0), (0, TILE - HEADS))
    return (
        in_full,
        out_full,
        norm_full.astype(F32)[None],
        conv_full.astype(F32).T,
        shift_full.astype(F32)[None],
        jnp.pad(step_bias[None], pad),
        jnp.pad(decay_log[None], pad),
        jnp.repeat(skip_gain, HEADDIM)[None],
        gate_full.astype(F32)[None],
    )


def on_device(
    tokens, cotangent, lengths, order, norm_weight, in_weight, conv_weight, conv_bias,
    step_bias, decay_log, skip_gain, gate_norm_weight, out_weight,
):
    peers = lax.axis_size("shard")
    rank = lax.axis_index("shard")
    piece, width = tokens.shape[1:]

    def gather(x):
        return lax.all_gather(x, "shard", axis=0, tiled=True)

    def to_sequences(x):
        parts = x.reshape(peers, 1, piece, width)
        return lax.all_to_all(parts, "shard", split_axis=0, concat_axis=2, tiled=True).reshape(peers * piece, width)

    def to_slots(x):
        parts = x.reshape(1, peers * piece, width)
        return lax.all_to_all(parts, "shard", split_axis=1, concat_axis=0, tiled=True)

    slots = jnp.arange(peers, dtype=jnp.int32)
    sequence = jnp.sum(jnp.where(slots == rank, order[0], 0))
    valid = jnp.sum(jnp.where(slots == sequence, lengths[0], 0))[None]
    tok = to_sequences(tokens)
    cot = to_sequences(cotangent)
    params = prepare(
        gather(norm_weight), gather(in_weight), gather(conv_weight), gather(conv_bias),
        gather(gate_norm_weight), gather(out_weight), step_bias, decay_log, skip_gain,
    )
    out, cin, gr, mx, st, sr, normed, gate_low = run_forward(valid, tok, params)
    output = to_slots(out)
    ig, gp, taps, gcb, ggn, gsk, gnw, ghd = run_backward(valid, cot, tok, params, (cin, gr, mx, st, sr))
    input_grad = to_slots(ig)
    keep = jnp.arange(peers * piece, dtype=jnp.int32)[:, None] < valid[0]
    grad_branch = jnp.where(keep, cot, jnp.zeros_like(cot))
    grad_out = mul_tn(gate_low, grad_branch)
    grad_in = mul_tn(normed, gp)

    def scatter(x):
        return lax.psum(lax.psum_scatter(x, "shard", scatter_dimension=0, tiled=True), "rep")

    heads = jnp.stack([
        jnp.sum(ghd[:EDGE], axis=0)[:HEADS], jnp.sum(ghd[EDGE:], axis=0)[:HEADS],
        jnp.sum(gsk.reshape(EDGE, HEADS, HEADDIM), axis=(0, 2)),
    ])
    heads = lax.psum(heads, ("rep", "shard"))
    return (
        output, input_grad, scatter(jnp.sum(gnw, axis=0)), scatter(grad_in), scatter(jnp.sum(taps, axis=1).T),
        scatter(jnp.sum(gcb, axis=0)), heads[0], heads[1], heads[2], scatter(jnp.sum(ggn, axis=0)), scatter(grad_out),
    )


def solution(mesh):
    placed = (
        P("rep", "shard", None), P("rep", "shard", None), P("rep", None), P("rep", None), P("shard"),
        P("shard", None), P("shard", None), P("shard"), P(), P(), P(), P("shard"), P("shard", None),
    )
    outs = (
        P("rep", "shard", None), P("rep", "shard", None), P("shard"), P("shard", None), P("shard", None),
        P("shard"), P(), P(), P(), P("shard"), P("shard", None),
    )
    return jax.shard_map(on_device, mesh=mesh, in_specs=placed, out_specs=outs, check_vma=False)
```

```python
import functools

import jax
import jax.numpy as jnp
from jax import lax
from jax.experimental import pallas as pl
from jax.experimental.pallas import tpu as pltpu
from jax.sharding import PartitionSpec as P

HEADS = 24
HEADDIM = 64
STATE = 128
CONV = 4
SPAN = 256
DI = 1536
XBC = 1792
TILE = 128
PAIRS = DI // TILE
HALF = SPAN // 2
EDGE = 8
epsilon = 1e-05
F32 = jnp.float32
BF16 = jnp.bfloat16
FULL = lax.Precision.HIGHEST


def mul(a, b):
    return jnp.dot(a, b, preferred_element_type=F32)


def mul_nt(a, b):
    return lax.dot_general(a, b, (((1,), (1,)), ((), ())), preferred_element_type=F32)


def mul_tn(a, b):
    return lax.dot_general(a, b, (((0,), (0,)), ((), ())), preferred_element_type=F32)


def sigmoid(v):
    return 0.5 * jnp.tanh(0.5 * v) + 0.5


def softplus(v):
    return jnp.maximum(v, 0.0) + jnp.log1p(jnp.exp(-jnp.abs(v)))


def fold(v):
    return jnp.sum(v.reshape(v.shape[0] // EDGE, EDGE, v.shape[1]), axis=0)


def tile_at(j, base=0):
    return pl.ds(pl.multiple_of(base + j * TILE, TILE), TILE)


def lane_low(shape):
    return lax.broadcasted_iota(jnp.int32, shape, 1) < HEADDIM


def spread(column, h):
    return jnp.broadcast_to(column[:, h : h + 1], (column.shape[0], TILE))


def conv_argument(cin_ref, cw_ref, cb_ref, cols):
    total = cb_ref[:, cols]
    for tap in range(CONV):
        start = EDGE - CONV + 1 + tap
        total = total + cw_ref[tap : tap + 1, cols] * cin_ref[0, start : start + SPAN, cols]
    return total


def head_times(step_raw, step_bias, decay_log):
    shifted = step_raw + step_bias
    step = softplus(shifted)
    log_decay = -jnp.exp(decay_log) * step
    rows = lax.broadcasted_iota(jnp.int32, (SPAN, SPAN), 0)
    columns = lax.broadcasted_iota(jnp.int32, (SPAN, SPAN), 1)
    lower = (rows >= columns).astype(F32)
    cumul = jnp.dot(lower, log_decay, precision=FULL, preferred_element_type=F32)
    return shifted, step, cumul, cumul - jnp.log(step)


def causal_mask(flip):
    rows = lax.broadcasted_iota(jnp.int32, (HALF, HALF), 0)
    columns = lax.broadcasted_iota(jnp.int32, (HALF, HALF), 1)
    return columns >= rows if flip else rows >= columns


def forward_kernel(
    len_ref, tok_ref, w_ref, ow_ref, nw_ref, cw_ref, cb_ref, sb_ref, dl_ref, sk_ref, gn_ref,
    out_ref, cin_ref, gr_ref, mx_ref, st_ref, sr_ref, nl_ref, gl_ref,
    ws, col_t, pair_s, row_s, state, scores, gated,
):
    block = pl.program_id(0)
    offset = block * SPAN

    @pl.when(block == 0)
    def _():
        ws[...] = jnp.zeros_like(ws)
        ws[:, :HEADS] = w_ref[:, DI + XBC : DI + XBC + HEADS]
        state[...] = jnp.zeros_like(state)
        cin_ref[0, :EDGE, :] = jnp.zeros((EDGE, XBC), F32)

    @pl.when(block > 0)
    def _():
        cin_ref[0, :EDGE, :] = gated[:EDGE, :]

    for r in range(0, SPAN, 64):
        tok = tok_ref[r : r + 64, :].astype(F32)
        nrm = lax.rsqrt(jnp.mean(tok * tok, axis=-1, keepdims=True) + epsilon)
        nl_ref[r : r + 64, :] = (tok * nrm * nw_ref[...]).astype(BF16)
    low = nl_ref[...]
    sr_ref[...] = mul(low, ws[...])
    for n in range(0, XBC, 256):
        cin_ref[0, EDGE:, n : n + 256] = mul(low, w_ref[:, DI + n : DI + n + 256])
    for n in range(0, DI, 256):
        gr_ref[:, n : n + 256] = mul(low, w_ref[:, n : n + 256])

    _, _, cumul, shift = head_times(sr_ref[...], sb_ref[...], dl_ref[...])
    row_s[...] = shift.T
    low_lanes = lane_low((SPAN, TILE))
    for h in range(HEADS):
        col_t[h] = spread(cumul, h)
    for j in range(PAIRS):
        pair_s[j] = jnp.where(low_lanes, spread(shift, 2 * j), spread(shift, 2 * j + 1))

    def act(jt):
        arg = conv_argument(cin_ref, cw_ref, cb_ref, tile_at(jt))
        return arg * sigmoid(arg)

    key = act(PAIRS).astype(BF16)
    query = act(PAIRS + 1).astype(BF16)
    key_t = key.astype(F32).T.astype(BF16)
    scores[...] = mul_nt(query, key)
    st_ref[0] = state[...]
    mask = causal_mask(False)

    def pair(j, total):
        cols = tile_at(j)
        heads_in = act(j)
        heads_low = heads_in.astype(BF16)
        cum0, cum1 = col_t[2 * j], col_t[2 * j + 1]
        cum = jnp.where(low_lanes, cum0, cum1)
        last = cum[SPAN - 1 : SPAN, :]
        old = state[:, cols]
        across = mul(query, old.astype(BF16))
        weighted = (heads_low.astype(F32) * jnp.exp(last - pair_s[j])).astype(BF16)
        state[:, cols] = jnp.exp(last) * old + mul(key_t, weighted)
        zero = jnp.zeros_like(heads_low)
        parts = (jnp.where(low_lanes, heads_low, zero), jnp.where(low_lanes, zero, heads_low))
        top, bottom = [], []
        for h in range(2):
            col = (cum0, cum1)[h]
            row = row_s[pl.ds(2 * j + h, 1), :]
            first = jnp.where(mask, col[:HALF] - row[:, :HALF], -jnp.inf)
            top.append((scores[:HALF, :HALF] * jnp.exp(first)).astype(BF16))
            full = col[HALF:] - row[:, :HALF]
            bottom.append((scores[HALF:, :HALF] * jnp.exp(full)).astype(BF16))
            second = jnp.where(mask, col[HALF:] - row[:, HALF:], -jnp.inf)
            bottom.append((scores[HALF:, HALF:] * jnp.exp(second)).astype(BF16))
        tops = jnp.concatenate([p[:HALF] for p in parts], axis=0)
        within = jnp.concatenate(
            [
                mul(jnp.concatenate(top, axis=1), tops),
                mul(jnp.concatenate(bottom, axis=1), jnp.concatenate(parts, axis=0)),
            ],
            axis=0,
        )
        mixed = within + jnp.exp(cum) * across + sk_ref[:, cols] * heads_in
        mx_ref[:, cols] = mixed
        gate = gr_ref[:, cols]
        value = mixed * (gate * sigmoid(gate))
        gated[:, cols] = value
        return total + value * value

    total = lax.fori_loop(0, PAIRS, pair, jnp.zeros((SPAN, TILE), F32))
    rms = lax.rsqrt(jnp.sum(total, axis=-1, keepdims=True) * (1.0 / DI) + epsilon)

    def finish(j, carry):
        cols = tile_at(j)
        gl_ref[:, cols] = (gated[:, cols] * rms * gn_ref[:, cols]).astype(BF16)
        return carry

    lax.fori_loop(0, PAIRS, finish, 0)
    positions = offset + lax.broadcasted_iota(jnp.int32, (SPAN, 256), 0)
    valid = positions < len_ref[0]
    for n in range(0, tok_ref.shape[1], 256):
        branch = mul(gl_ref[...], ow_ref[:, n : n + 256])
        tok = tok_ref[:, n : n + 256].astype(F32)
        out_ref[:, n : n + 256] = (tok + jnp.where(valid, branch, 0.0)).astype(BF16)
    gated[:EDGE, :] = cin_ref[0, SPAN:, :]


def backward_kernel(
    len_ref, cot_ref, tok_ref, w_ref, ow_ref, nw_ref, cw_ref, cb_ref, sb_ref, dl_ref, sk_ref, gn_ref,
    cin_ref, gr_ref, mx_ref, st_ref, sr_ref,
    ig_ref, gp_ref, gb_ref, taps_ref, gcb_ref, ggn_ref, gsk_ref, gnw_ref, ghd_ref,
    ws, col_s, pair_t, row_t, later, scores, grad_scores, gg, sig, gpre, args, acc_q, acc_k, acc_u, acc_v, acc_l,
):
    step_id = pl.program_id(0)
    count = pl.num_programs(0)
    offset = (count - 1 - step_id) * SPAN

    @pl.when(step_id == 0)
    def _():
        ws[...] = jnp.zeros_like(ws)
        ws[:, :HEADS] = w_ref[:, DI + XBC : DI + XBC + HEADS]
        later[...] = jnp.zeros_like(later)
        gpre[SPAN:, :] = jnp.zeros((EDGE, XBC), F32)
        for ref in (taps_ref, gcb_ref, ggn_ref, gsk_ref, gnw_ref, ghd_ref):
            ref[...] = jnp.zeros_like(ref)

    width = cot_ref.shape[1]
    positions = offset + lax.broadcasted_iota(jnp.int32, (SPAN, width), 0)
    grad_branch = jnp.where(positions < len_ref[0], cot_ref[...].astype(F32), 0.0).astype(BF16)
    gb_ref[...] = grad_branch
    for n in range(0, DI, 256):
        gg[:, n : n + 256] = mul_nt(grad_branch, ow_ref[n : n + 256, :])

    shifted, step, cumul, shift = head_times(sr_ref[...], sb_ref[...], dl_ref[...])
    row_t[...] = cumul.T
    low_lanes = lane_low((SPAN, TILE))
    for h in range(HEADS):
        col_s[h] = spread(shift, h)
    for j in range(PAIRS):
        pair_t[j] = jnp.where(low_lanes, spread(cumul, 2 * j), spread(cumul, 2 * j + 1))

    def sums(j, carry):
        squares, crossed = carry
        cols = tile_at(j)
        gate = gr_ref[:, cols]
        part = sigmoid(gate)
        sig[:, cols] = part
        value = mx_ref[:, cols] * (gate * part)
        return squares + value * value, crossed + (gg[:, cols] * gn_ref[:, cols]) * value

    nothing = jnp.zeros((SPAN, TILE), F32)
    squares, crossed = lax.fori_loop(0, PAIRS, sums, (nothing, nothing))
    rms = lax.rsqrt(jnp.sum(squares, axis=-1, keepdims=True) * (1.0 / DI) + epsilon)
    coef = rms * rms * (jnp.sum(crossed, axis=-1, keepdims=True) * (1.0 / DI))
    rms = jnp.broadcast_to(rms, (SPAN, TILE))
    coef = jnp.broadcast_to(coef, (SPAN, TILE))

    def act(jt, slot):
        arg = conv_argument(cin_ref, cw_ref, cb_ref, tile_at(jt))
        args[:, slot * TILE : (slot + 1) * TILE] = arg
        return (arg * sigmoid(arg)).astype(BF16)

    key = act(PAIRS, 0)
    query = act(PAIRS + 1, 1)
    query_t = query.astype(F32).T.astype(BF16)
    scores[...] = mul_nt(key, query)
    grad_scores[...] = jnp.zeros_like(grad_scores)
    for ref in (acc_q, acc_k, acc_u, acc_v, acc_l):
        ref[...] = jnp.zeros_like(ref)
    mask = causal_mask(True)
    lane = lax.broadcasted_iota(jnp.int32, (2 * TILE, TILE), 0) % TILE
    head = lax.broadcasted_iota(jnp.int32, (2 * TILE, TILE), 1)

    def by_head(value, pick):
        high = value.astype(BF16)
        rest = (value - high.astype(F32)).astype(BF16)
        return mul(jnp.concatenate([high, rest], axis=1), pick)

    def pair(j, carry):
        cols = tile_at(j)
        arg = conv_argument(cin_ref, cw_ref, cb_ref, cols)
        part_x = sigmoid(arg)
        heads_in = arg * part_x
        heads_low = heads_in.astype(BF16)
        heads_float = heads_low.astype(F32)
        gate, mixed, part, gain, back = (
            gr_ref[:, cols], mx_ref[:, cols], sig[:, cols], gn_ref[:, cols], gg[:, cols]
        )
        silu = gate * part
        value = mixed * silu
        ggn_ref[:, cols] += fold(back * value * rms)
        grad_gated = rms * (back * gain - value * coef)
        grad_scan = grad_gated * silu
        gp_ref[:, cols] = (grad_gated * mixed * (part * (1.0 + gate * (1.0 - part)))).astype(BF16)
        gsk_ref[:, cols] += fold(grad_scan * heads_in)
        cum = pair_t[j]
        growth = jnp.exp(cum)
        last = cum[SPAN - 1 : SPAN, :]
        grad_low = grad_scan.astype(BF16)
        scaled = growth * grad_scan
        grad_across = scaled.astype(BF16)
        col0, col1 = col_s[2 * j], col_s[2 * j + 1]
        carry_weight = jnp.exp(last - jnp.where(low_lanes, col0, col1))
        weighted = (heads_float * carry_weight).astype(BF16)
        after = later[:, cols]
        after_low = after.astype(BF16)
        before = st_ref[0, :, cols]
        before_low = before.astype(BF16)
        across = mul(query, before_low)
        acc_k[...] += mul_nt(weighted, after_low)
        acc_q[...] += mul_nt(grad_across, before_low)
        grow_last = jnp.exp(last)
        carried = mul(key, after_low) * carry_weight
        last_sum = fold(carried * heads_float) + fold(after * before) * grow_last
        later[:, cols] = mul(query_t, grad_across) + grow_last * after
        zero = jnp.zeros_like(grad_low)
        parts = (jnp.where(low_lanes, grad_low, zero), jnp.where(low_lanes, zero, grad_low))
        top, bottom = [], []
        for h in range(2):
            col = (col0, col1)[h]
            row = row_t[pl.ds(2 * j + h, 1), :]
            mixed_top = mul_nt(heads_low[:HALF], parts[h])
            mixed_low = mul_nt(heads_low[HALF:], parts[h][HALF:])
            factor = jnp.exp(jnp.where(mask, row[:, :HALF] - col[:HALF], -jnp.inf))
            top.append((scores[:HALF, :HALF] * factor).astype(BF16))
            grad_scores[:HALF, :HALF] += mixed_top[:, :HALF] * factor
            factor = jnp.exp(row[:, HALF:] - col[:HALF])
            top.append((scores[:HALF, HALF:] * factor).astype(BF16))
            grad_scores[:HALF, HALF:] += mixed_top[:, HALF:] * factor
            factor = jnp.exp(jnp.where(mask, row[:, HALF:] - col[HALF:], -jnp.inf))
            bottom.append((scores[HALF:, HALF:] * factor).astype(BF16))
            grad_scores[HALF:, HALF:] += mixed_low * factor
        lows = jnp.concatenate([p[HALF:] for p in parts], axis=0)
        grad_heads = carried + jnp.concatenate(
            [
                mul(jnp.concatenate(top, axis=1), jnp.concatenate(parts, axis=0)),
                mul(jnp.concatenate(bottom, axis=1), lows),
            ],
            axis=0,
        )
        gain_skip = sk_ref[:, cols]
        spanned = growth * across
        within = mixed - gain_skip * heads_in - spanned
        pick = (head == 2 * j + lane // HEADDIM).astype(F32)
        pick_low = pick.astype(BF16)
        acc_u[...] += by_head(grad_low.astype(F32) * within + grad_scan * spanned, pick_low)
        acc_v[...] += by_head(heads_float * grad_heads, pick_low)
        acc_l[...] += jnp.dot(last_sum, pick[:TILE], precision=FULL, preferred_element_type=F32)
        grad_conv = grad_heads + gain_skip * grad_scan
        gpre[:SPAN, cols] = grad_conv * (part_x * (1.0 + arg * (1.0 - part_x)))
        return carry

    lax.fori_loop(0, PAIRS, pair, 0)

    rows = lax.broadcasted_iota(jnp.int32, (SPAN, SPAN), 0)
    columns = lax.broadcasted_iota(jnp.int32, (SPAN, SPAN), 1)
    upper = (columns >= rows).astype(F32)
    at_end = lax.broadcasted_iota(jnp.int32, (SPAN, TILE), 0) == SPAN - 1
    to_step = acc_v[...]
    ends = jnp.sum(acc_l[...], axis=0, keepdims=True)
    grad_cumul = acc_u[...] - to_step + jnp.where(at_end, ends, 0.0)
    grad_log = jnp.dot(upper, grad_cumul, precision=FULL, preferred_element_type=F32)
    rate = jnp.exp(dl_ref[...])
    safe = jnp.where(step > 0.0, step, 1.0)
    grad_step = jnp.where(step > 0.0, to_step / safe, 0.0)
    grad_raw = (grad_step - rate * grad_log) * sigmoid(shifted)
    ghd_ref[:EDGE, :] += fold(grad_raw)
    ghd_ref[EDGE:, :] -= fold(rate * step * grad_log)
    raw_low = grad_raw.astype(BF16)
    gp_ref[:, DI + XBC :] = raw_low[:, :HEADS]

    scores_low = grad_scores[...].astype(BF16)
    scores_t = grad_scores[...].T.astype(BF16)
    for slot, grad in (
        (0, acc_k[...] + mul(scores_low, query)),
        (1, acc_q[...] + mul(scores_t, key)),
    ):
        arg = args[:, slot * TILE : (slot + 1) * TILE]
        part = sigmoid(arg)
        gpre[:SPAN, DI + slot * TILE : DI + (slot + 1) * TILE] = grad * (part * (1.0 + arg * (1.0 - part)))

    def through_conv(j, carry):
        cols = tile_at(j)
        here = gpre[:SPAN, cols]
        gcb_ref[:, cols] += fold(here)
        total = jnp.zeros_like(here)
        for tap in range(CONV):
            start = EDGE - CONV + 1 + tap
            taps_ref[tap, :, cols] += fold(here * cin_ref[0, start : start + SPAN, cols])
            ahead = CONV - 1 - tap
            total = total + cw_ref[tap : tap + 1, cols] * gpre[ahead : ahead + SPAN, cols]
        gp_ref[:, tile_at(j, DI)] = total.astype(BF16)
        return carry

    lax.fori_loop(0, PAIRS + 2, through_conv, 0)
    gpre[SPAN:, :] = gpre[:EDGE, :]

    for n in range(0, width, 256):
        grad = mul_nt(gp_ref[:, : DI + XBC], w_ref[n : n + 256, : DI + XBC])
        gg[:, n : n + 256] = grad + mul_nt(raw_low, ws[n : n + 256, :])
    for r in range(0, SPAN, 64):
        tok = tok_ref[r : r + 64, :].astype(F32)
        nrm = lax.rsqrt(jnp.mean(tok * tok, axis=-1, keepdims=True) + epsilon)
        grad = gg[r : r + 64, :width]
        gnw_ref[...] += fold(grad * tok * nrm)
        value = grad * nw_ref[...]
        centre = jnp.mean(value * tok, axis=-1, keepdims=True) * (nrm * nrm)
        grad_tok = nrm * (value - tok * centre)
        ig_ref[r : r + 64, :] = (cot_ref[r : r + 64, :].astype(F32) + grad_tok).astype(BF16)


def whole(shape):
    return pl.BlockSpec(shape, lambda i: (0,) * len(shape), pipeline_mode=pl.Buffered(1))


def rows_of(width, last=None):
    if last is None:
        return pl.BlockSpec((SPAN, width), lambda i: (i, 0))
    return pl.BlockSpec((SPAN, width), lambda i: (last - i, 0))


def params_specs(width):
    proj = DI + XBC + HEADS
    return [
        whole((width, proj)), whole((DI, width)), whole((1, width)), whole((CONV, XBC)), whole((1, XBC)),
        whole((1, TILE)), whole((1, TILE)), whole((1, DI)), whole((1, DI)),
    ]


LIMIT = 60 * 2**20


def run_forward(valid, tok, params):
    length, width = tok.shape
    count = length // SPAN
    shapes = [
        ((length, width), BF16), ((count, SPAN + EDGE, XBC), F32), ((length, DI), F32), ((length, DI), F32),
        ((count, STATE, DI), F32), ((length, TILE), F32), ((length, width), BF16), ((length, DI), BF16),
    ]
    out_specs = [
        rows_of(width), pl.BlockSpec((1, SPAN + EDGE, XBC), lambda i: (i, 0, 0)), rows_of(DI), rows_of(DI),
        pl.BlockSpec((1, STATE, DI), lambda i: (i, 0, 0)), rows_of(TILE), rows_of(width), rows_of(DI),
    ]
    return pl.pallas_call(
        forward_kernel,
        grid=(count,),
        out_shape=[jax.ShapeDtypeStruct(s, d) for s, d in shapes],
        in_specs=[pl.BlockSpec(memory_space=pltpu.SMEM), rows_of(width), *params_specs(width)],
        out_specs=out_specs,
        scratch_shapes=[
            pltpu.VMEM((width, TILE), BF16), pltpu.VMEM((HEADS, SPAN, TILE), F32), pltpu.VMEM((PAIRS, SPAN, TILE), F32),
            pltpu.VMEM((TILE, SPAN), F32), pltpu.VMEM((STATE, DI), F32), pltpu.VMEM((SPAN, SPAN), F32), pltpu.VMEM((SPAN, XBC), F32),
        ],
        compiler_params=pltpu.CompilerParams(dimension_semantics=("arbitrary",), vmem_limit_bytes=LIMIT),
        cost_estimate=pl.CostEstimate(flops=20 * 10**9, bytes_accessed=60 * 10**6, transcendentals=10**7),
    )(valid, tok, *params)


def run_backward(valid, cot, tok, params, kept):
    length, width = tok.shape
    count = length // SPAN
    proj = DI + XBC + HEADS
    last = count - 1
    shapes = [
        ((length, width), BF16), ((length, proj), BF16), ((length, width), BF16), ((CONV, EDGE, XBC), F32), ((EDGE, XBC), F32), ((EDGE, DI), F32),
        ((EDGE, DI), F32), ((EDGE, width), F32), ((2 * EDGE, TILE), F32),
    ]
    out_specs = [rows_of(width, last), rows_of(proj, last), rows_of(width, last), *(whole(s) for s, _ in shapes[3:])]
    kept_specs = [
        pl.BlockSpec((1, SPAN + EDGE, XBC), lambda i: (last - i, 0, 0)), rows_of(DI, last), rows_of(DI, last),
        pl.BlockSpec((1, STATE, DI), lambda i: (last - i, 0, 0)), rows_of(TILE, last),
    ]
    square, wide = pltpu.VMEM((SPAN, SPAN), F32), pltpu.VMEM((SPAN, DI), F32)
    narrow = pltpu.VMEM((SPAN, TILE), F32)
    return pl.pallas_call(
        backward_kernel,
        grid=(count,),
        out_shape=[jax.ShapeDtypeStruct(s, d) for s, d in shapes],
        in_specs=[pl.BlockSpec(memory_space=pltpu.SMEM), rows_of(width, last), rows_of(width, last), *params_specs(width), *kept_specs],
        out_specs=out_specs,
        scratch_shapes=[
            pltpu.VMEM((width, TILE), BF16), pltpu.VMEM((HEADS, SPAN, TILE), F32), pltpu.VMEM((PAIRS, SPAN, TILE), F32),
            pltpu.VMEM((TILE, SPAN), F32), pltpu.VMEM((STATE, DI), F32), square, square, wide, wide,
            pltpu.VMEM((SPAN + EDGE, XBC), F32), pltpu.VMEM((SPAN, 2 * TILE), F32),
            narrow, narrow, narrow, narrow, pltpu.VMEM((EDGE, TILE), F32),
        ],
        compiler_params=pltpu.CompilerParams(dimension_semantics=("arbitrary",), vmem_limit_bytes=LIMIT),
        cost_estimate=pl.CostEstimate(flops=40 * 10**9, bytes_accessed=60 * 10**6, transcendentals=2 * 10**7),
    )(valid, cot, tok, *params, *kept)


def prepare(norm_full, in_full, conv_full, shift_full, gate_full, out_full, step_bias, decay_log, skip_gain):
    pad = ((0, 0), (0, TILE - HEADS))
    return (
        in_full,
        out_full,
        norm_full.astype(F32)[None],
        conv_full.astype(F32).T,
        shift_full.astype(F32)[None],
        jnp.pad(step_bias[None], pad),
        jnp.pad(decay_log[None], pad),
        jnp.repeat(skip_gain, HEADDIM)[None],
        gate_full.astype(F32)[None],
    )


MESH = pl.DeviceIdType.MESH
PLANE = 4
REP = 2
CUTS = (1, 1, 1, 6, 11, 16)


def gather_kernel(
    n, tok_ref, in_ref, ow_ref, small_ref, seq_ref, inf_ref, owf_ref, smf_ref,
    own, tok_s, tok_r, small_s, small_r, line_s, line_r, plane_s, plane_r, sib_s, sib_r,
):
    planes = n // PLANE
    me = lax.axis_index("shard")
    core = lax.axis_index("rep")
    z, y, x = me // PLANE, (me // 2) % 2, me % 2
    across = me + 1 - 2 * x
    along = me + 2 - 4 * y
    piece = tok_ref.shape[1]
    arrays = ((in_ref, inf_ref), (ow_ref, owf_ref))

    barrier = pltpu.get_barrier_semaphore()
    for d in range(1, n):
        pl.semaphore_signal(barrier, inc=1, device_id={"shard": lax.rem(me + d, n)}, device_id_type=MESH)
    pl.semaphore_signal(barrier, inc=1, device_id={"rep": 1 - core}, device_id_type=MESH)
    pl.semaphore_wait(barrier, n)

    def region(a, k, part=None):
        src, dst = arrays[a]
        rows = src.shape[0] // REP
        start = pl.multiple_of(k * src.shape[0] + core * rows, 8)
        if part is None:
            return dst.at[pl.ds(start, rows)]
        half = src.shape[1] // 2 // TILE * TILE
        cols = pl.ds(0, half) if part == 0 else pl.ds(half, src.shape[1] - half)
        return dst.at[pl.ds(start, rows), cols]

    def send(view, to, s, r):
        return pltpu.make_async_remote_copy(
            src_ref=view, dst_ref=view, send_sem=s, recv_sem=r, device_id=to, device_id_type=MESH
        )

    def line(a, origin, to):
        return send(region(a, origin), {"shard": to}, line_s.at[a, origin // PLANE, (to > me).astype(jnp.int32)], line_r.at[a, origin // PLANE])

    def hop(a, zz, kind):
        here = zz * PLANE + 2 * y + x
        side = zz * PLANE + 2 * y + 1 - x
        ahead = zz * PLANE + 2 * (1 - y) + x
        origin, part, to = (
            (here, 0, across), (here, 1, along), (here, 0, along), (here, 1, across), (side, 0, along), (ahead, 1, across),
        )[kind]
        return send(region(a, origin, part), {"shard": to}, plane_s.at[a, zz, kind], plane_r.at[a, zz, kind])

    def sibling(a, zz, kind):
        origin = zz * PLANE + (2 * y + x, 2 * y + 1 - x, 2 * (1 - y) + x, 2 * (1 - y) + 1 - x)[kind]
        return send(region(a, origin), {"rep": 1 - core}, sib_s.at[a, zz, kind], sib_r.at[a, zz, kind])

    local = []
    for a, (src, _) in enumerate(arrays):
        rows = src.shape[0] // REP
        start = pl.multiple_of(core * rows, 8)
        copy = pltpu.make_async_copy(src.at[pl.ds(start, rows)], region(a, me), own.at[a])
        copy.start()
        local.append(copy)
    copy = pltpu.make_async_copy(tok_ref.at[me], seq_ref.at[pl.ds(pl.multiple_of(me * piece, 8), piece)], own.at[2])
    copy.start()
    local.append(copy)
    few = small_ref.shape[0]
    mine = smf_ref.at[pl.ds(pl.multiple_of(me * few, 8), few)]
    copy = pltpu.make_async_copy(small_ref, mine, own.at[3])
    copy.start()
    local.append(copy)
    for copy in local:
        copy.wait()

    def launch(zz):
        for a in range(2):
            for kind in range(4):
                hop(a, zz, kind).start()
            sibling(a, zz, 0).start()

    for a in range(2):
        @pl.when(z + 1 < planes)
        def _():
            line(a, me, me + PLANE).start()

        @pl.when(z > 0)
        def _():
            line(a, me, me - PLANE).start()
    launch(z)
    exchange = []

    def tokens(first, last):
        for d in range(first, last):
            to = lax.rem(me + d, n)
            copy = pltpu.make_async_remote_copy(
                src_ref=tok_ref.at[to], dst_ref=seq_ref.at[pl.ds(pl.multiple_of(me * piece, 8), piece)],
                send_sem=tok_s.at[d], recv_sem=tok_r.at[d], device_id={"shard": to}, device_id_type=MESH,
            )
            copy.start()
            exchange.append(copy)

    for d in range(1, n):
        copy = send(mine, {"shard": lax.rem(me + d, n)}, small_s.at[d], small_r.at[d])
        copy.start()
        exchange.append(copy)
    tokens(CUTS[0], CUTS[1])

    def relay(zz):
        for a in range(2):
            hop(a, zz, 0).wait_recv()
            hop(a, zz, 4).start()
            hop(a, zz, 1).wait_recv()
            hop(a, zz, 5).start()

    def collect(zz):
        for a in range(2):
            hop(a, zz, 3).wait_recv()
            sibling(a, zz, 1).start()
            hop(a, zz, 2).wait_recv()
            sibling(a, zz, 2).start()
            hop(a, zz, 4).wait_recv()
            hop(a, zz, 5).wait_recv()
            sibling(a, zz, 3).start()

    def each(d, step):
        @pl.when(z - d >= 0)
        def _():
            step(z - d, me - d * PLANE, me + PLANE, z + 1 < planes)

        @pl.when(z + d < planes)
        def _():
            step(z + d, me + d * PLANE, me - PLANE, z > 0)

    def arrived(zz, origin, to, more):
        for a in range(2):
            line(a, origin, to).wait_recv()

            @pl.when(more)
            def _():
                line(a, origin, to).start()
        launch(zz)

    for d in range(1, planes):
        each(d, arrived)
        if d == 1:
            relay(z)
        else:
            each(d - 1, lambda zz, *_: relay(zz))
        tokens(CUTS[d], CUTS[d + 1])
    collect(z)
    each(planes - 1, lambda zz, *_: relay(zz))
    tokens(CUTS[4], CUTS[5])
    for d in range(1, planes):
        each(d, lambda zz, *_: collect(zz))

    for copy in exchange:
        copy.wait()
    for zz in range(planes):
        for a in range(2):
            for kind in range(4):
                sibling(a, zz, kind).wait()
            for kind in range(6):
                hop(a, zz, kind).wait_send()
    for a in range(2):
        def sent(zz, origin, to, more):
            @pl.when(more)
            def _():
                line(a, origin, to).wait_send()

        for d in range(1, planes):
            each(d, sent)

        @pl.when(z + 1 < planes)
        def _():
            line(a, me, me + PLANE).wait_send()

        @pl.when(z > 0)
        def _():
            line(a, me, me - PLANE).wait_send()


def run_gather(tokens, in_weight, out_weight, small):
    n, piece, width = tokens.shape
    planes = n // PLANE
    hbm = pl.BlockSpec(memory_space=pl.ANY)
    dma = pltpu.SemaphoreType.DMA
    shapes = [
        ((n * piece, width), tokens.dtype), ((n * in_weight.shape[0], in_weight.shape[1]), in_weight.dtype),
        ((n * out_weight.shape[0], out_weight.shape[1]), out_weight.dtype), ((n * small.shape[0], TILE), small.dtype),
    ]
    return pl.pallas_call(
        functools.partial(gather_kernel, n),
        out_shape=[jax.ShapeDtypeStruct(s, d) for s, d in shapes],
        in_specs=[hbm] * 4,
        out_specs=[hbm] * 4,
        scratch_shapes=[
            dma((4,)), dma((n,)), dma((n,)), dma((n,)), dma((n,)), dma((2, planes, 2)), dma((2, planes)),
            dma((2, planes, 6)), dma((2, planes, 6)), dma((2, planes, 4)), dma((2, planes, 4)),
        ],
        compiler_params=pltpu.CompilerParams(collective_id=0, has_side_effects=True),
    )(tokens, in_weight, out_weight, small)


PARTS = (
    (1, 0, 384, 0), (1, 384, 384, 1), (0, 0, 768, 0), (0, 768, 768, 1), (0, 1536, 896, 0), (0, 2432, 920, 1),
)
SPREAD = (0, 4, 8, 12, 15)


def scatter_kernel(n, *refs):
    (
        ig_ref, nl_ref, gp_ref, gl_ref, gb_ref, small_ref,
        slot_ref, gin_ref, gout_ref, sum_ref,
    ) = refs[:10]
    refs = refs[10:]
    count = len(PARTS)
    bufs = [refs[i * 7 : (i + 1) * 7] for i in range(count)]
    (
        nl_t, gl_t, few, few_sib, own, ig_s, ig_r, few_s, few_r, pair_s, pair_r, s0s, s0r, s1s, s1r, s2s, s2r, s3s, s3r, s4s, s4r,
    ) = refs[count * 7 :]
    planes = n // PLANE
    me = lax.axis_index("shard")
    core = lax.axis_index("rep")
    z, y, x = me // PLANE, (me // 2) % 2, me % 2
    across = {"shard": me + 1 - 2 * x}
    along = {"shard": me + 2 - 4 * y}
    twin = {"rep": 1 - core}
    piece = slot_ref.shape[1]

    barrier = pltpu.get_barrier_semaphore()
    for d in range(1, n):
        pl.semaphore_signal(barrier, inc=1, device_id={"shard": lax.rem(me + d, n)}, device_id_type=MESH)
    pl.semaphore_signal(barrier, inc=1, device_id=twin, device_id_type=MESH)

    def remote(src, dst, s, r, to):
        return pltpu.make_async_remote_copy(
            src_ref=src, dst_ref=dst, send_sem=s, recv_sem=r, device_id=to, device_id_type=MESH
        )

    def ig_copy(d):
        to = lax.rem(me + d, n)
        src = ig_ref.at[pl.ds(pl.multiple_of(to * piece, 8), piece)]
        return remote(src, slot_ref.at[me], ig_s.at[d], ig_r.at[d], {"shard": to})

    def few_copy(d):
        to = lax.rem(me + d, n)
        return remote(small_ref.at[to], few.at[me], few_s.at[d], few_r.at[d], {"shard": to})

    first = core == 0

    def product(p):
        a, start, size, _ = PARTS[p]
        acc, s0 = bufs[p][0], bufs[p][1]
        left, right = (nl_t, gp_ref) if a == 0 else (gl_t, gb_ref)
        rows = acc.shape[3]
        for c in range(0, size, 256):
            wide = min(256, size - c)
            total = mul(left[...], right[:, start + c : start + c + wide])
            total = total.reshape(planes, 2, 2, 2, rows, wide)
            acc[:, :, :, :, c : c + wide] = jnp.where(first, total[:, :, :, 0], total[:, :, :, 1])
            s0[:, :, :, :, c : c + wide] = jnp.where(first, total[:, :, :, 1], total[:, :, :, 0]).astype(BF16)

    def c0(p):
        return remote(bufs[p][1], bufs[p][2], s0s.at[p], s0r.at[p], twin)

    def c1(p):
        sb, r1 = bufs[p][3], bufs[p][4]
        if PARTS[p][3] == 0:
            return remote(sb.at[:, 1 - y], r1, s1s.at[p], s1r.at[p], along)
        return remote(sb.at[:, :, 1 - x], r1, s1s.at[p], s1r.at[p], across)

    def c2(p):
        sb, r2 = bufs[p][3], bufs[p][5]
        if PARTS[p][3] == 0:
            return remote(sb.at[:, y, 1 - x], r2, s2s.at[p], s2r.at[p], across)
        return remote(sb.at[:, 1 - y, x], r2, s2s.at[p], s2r.at[p], along)

    def c3(p, dest, up):
        sb, r3 = bufs[p][3], bufs[p][6]
        to = {"shard": me + PLANE if up else me - PLANE}
        return remote(sb.at[dest, y, x], r3.at[int(up), dest], s3s.at[p, dest], s3r.at[p, int(up), dest], to)

    def into_half(p):
        acc, _, r0, sb = bufs[p][:4]
        c0(p).wait_recv()

        def step(i, carry):
            zz, yy, xx = i // PLANE, (i // 2) % 2, i % 2
            value = acc[zz, yy, xx] + r0[zz, yy, xx].astype(F32)
            acc[zz, yy, xx] = value
            sb[zz, yy, xx] = value.astype(BF16)
            return carry

        lax.fori_loop(0, n, step, 0)

    def after_first(p):
        acc, _, _, sb, r1 = bufs[p][:5]
        c1(p).wait_recv()
        c1(p).wait_send()

        def step(i, carry):
            zz, kk = i // 2, i % 2
            at = (zz, y, kk) if PARTS[p][3] == 0 else (zz, kk, x)
            value = acc[at] + r1[zz, kk].astype(F32)
            acc[at] = value
            sb[at] = value.astype(BF16)
            return carry

        lax.fori_loop(0, 2 * planes, step, 0)

    def after_second(p):
        acc, _, _, sb, _, r2 = bufs[p][:6]
        c2(p).wait_recv()
        c2(p).wait_send()
        for zz in range(planes):
            value = acc[zz, y, x] + r2[zz].astype(F32)
            acc[zz, y, x] = value
            sb[zz, y, x] = value.astype(BF16)

    def line(p):
        acc, sb, r3 = bufs[p][0], bufs[p][3], bufs[p][6]
        for i in range(planes - 1):
            for up in (True, False):
                dest = planes - 1 - i if up else i
                beyond = dest > z if up else dest < z
                more = z > 0 if up else z + 1 < planes

                @pl.when(beyond)
                def _():
                    @pl.when(more)
                    def _():
                        c3(p, dest, up).wait_recv()
                        value = acc[dest, y, x] + r3[int(up), dest].astype(F32)
                        sb[dest, y, x] = value.astype(BF16)

                    c3(p, dest, up).start()

    def results(p):
        a, start, size, _ = PARTS[p]
        acc = bufs[p][0]
        out = gin_ref if a == 0 else gout_ref
        rows = acc.shape[3]
        view = out.at[pl.ds(pl.multiple_of(core * rows, 8), rows), pl.ds(start, size)]
        return (
            remote(acc.at[z, y, x], view, s4s.at[p], s4r.at[p], twin),
            pltpu.make_async_copy(acc.at[z, y, x], view, own.at[p]),
        )

    def arrivals(p, up):
        r3 = bufs[p][6]
        return remote(bufs[p][3].at[z, y, x], r3.at[int(up), z], s3s.at[p, z], s3r.at[p, int(up), z], along)

    def finish(p):
        acc, r3 = bufs[p][0], bufs[p][6]
        for up in (True, False):
            @pl.when(z > 0 if up else z + 1 < planes)
            def _():
                arrivals(p, up).wait_recv()
                acc[z, y, x] += r3[int(up), z].astype(F32)

        for copy in results(p):
            copy.start()

    def igs(i):
        for d in range(1 + SPREAD[i], 1 + SPREAD[i + 1]):
            ig_copy(d).start()

    units = [(0, 1), (2, 3), (4, 5)]
    gl_t[...] = gl_ref[...].T
    for p in units[0]:
        product(p)
    pl.semaphore_wait(barrier, n)
    for p in units[0]:
        c0(p).start()
    for d in range(1, n):
        few_copy(d).start()
    igs(0)
    own_slot = pltpu.make_async_copy(
        ig_ref.at[pl.ds(pl.multiple_of(me * piece, 8), piece)], slot_ref.at[me], own.at[count]
    )
    own_slot.start()
    nl_t[...] = nl_ref[...].T

    def stage(fn, start, u):
        for p in units[u]:
            fn(p)
            if start is not None:
                start(p).start()

    for p in units[1]:
        product(p)
        c0(p).start()
    stage(into_half, c1, 0)
    for p in units[2]:
        product(p)
        c0(p).start()
    stage(into_half, c1, 1)
    igs(1)
    stage(after_first, c2, 0)
    stage(into_half, c1, 2)
    igs(2)
    stage(after_second, None, 0)
    stage(line, None, 0)
    stage(after_first, c2, 1)
    igs(3)
    stage(after_second, None, 1)
    stage(line, None, 1)
    stage(finish, None, 0)
    stage(after_first, c2, 2)
    stage(finish, None, 1)
    few[me] = small_ref[me]
    for d in range(1, n):
        few_copy(d).wait()
    total = few[0]
    for k in range(1, n):
        total = total + few[k]
    few_sib[0] = total
    pair = remote(few_sib.at[0], few_sib.at[1], pair_s, pair_r, twin)
    pair.start()
    stage(after_second, None, 2)
    stage(line, None, 2)
    stage(finish, None, 2)
    pair.wait()
    sum_ref[...] = few_sib[0] + few_sib[1]
    own_slot.wait()
    for d in range(1, n):
        ig_copy(d).wait()
    for p in range(count):
        c0(p).wait_send()
        for i in range(planes - 1):
            for up in (True, False):
                dest = planes - 1 - i if up else i

                @pl.when(dest > z if up else dest < z)
                def _():
                    c3(p, dest, up).wait_send()

        far, near = results(p)
        near.wait()
        far.wait()


def run_scatter(n, ig, normed, gp, gate_low, grad_branch, small):
    length, width = ig.shape
    piece = length // n
    planes = n // PLANE
    proj = gp.shape[1]
    inner = gate_low.shape[1]
    vmem = pl.BlockSpec(memory_space=pltpu.VMEM)
    hbm = pl.BlockSpec(memory_space=pl.ANY)
    dma = pltpu.SemaphoreType.DMA
    scratch = []
    for a, _, size, _ in PARTS:
        rows = (width if a == 0 else inner) // n // REP
        full = (planes, 2, 2, rows, size)
        scratch += [
            pltpu.VMEM(full, F32), pltpu.VMEM(full, BF16), pltpu.VMEM(full, BF16), pltpu.VMEM(full, BF16),
            pltpu.VMEM((planes, 2, rows, size), BF16), pltpu.VMEM((planes, rows, size), BF16), pltpu.VMEM((2, planes, rows, size), BF16),
        ]
    count = len(PARTS)
    few = small.shape[1:]
    scratch += [
        pltpu.VMEM((width, length), BF16), pltpu.VMEM((inner, length), BF16), pltpu.VMEM((n, *few), F32), pltpu.VMEM((2, *few), F32),
        dma((count + 1,)), dma((n,)), dma((n,)), dma((n,)), dma((n,)), dma(()), dma(()),
        *(dma((count,)) for _ in range(6)), dma((count, planes)), dma((count, 2, planes)), dma((count,)), dma((count,)),
    ]
    shapes = [
        ((n, piece, width), BF16), ((width // n, proj), F32), ((inner // n, width), F32), (few, F32),
    ]
    return pl.pallas_call(
        functools.partial(scatter_kernel, n),
        out_shape=[jax.ShapeDtypeStruct(s, d) for s, d in shapes],
        in_specs=[hbm, vmem, vmem, vmem, vmem, vmem],
        out_specs=[hbm, hbm, hbm, vmem],
        scratch_shapes=scratch,
        compiler_params=pltpu.CompilerParams(collective_id=1, has_side_effects=True, vmem_limit_bytes=LIMIT),
    )(ig, normed, gp, gate_low, grad_branch, small)


FEW = EDGE * TILE


def on_device(
    tokens, cotangent, lengths, order, norm_weight, in_weight, conv_weight, conv_bias,
    step_bias, decay_log, skip_gain, gate_norm_weight, out_weight,
):
    peers = lax.axis_size("shard")
    rank = lax.axis_index("shard")
    piece, width = tokens.shape[1:]

    def gather(x):
        return lax.all_gather(x, "shard", axis=0, tiled=True)

    def to_sequences(x):
        parts = x.reshape(peers, 1, piece, width)
        return lax.all_to_all(parts, "shard", split_axis=0, concat_axis=2, tiled=True).reshape(peers * piece, width)

    def to_slots(x):
        parts = x.reshape(peers, piece, width)
        return lax.all_to_all(parts, "shard", split_axis=0, concat_axis=0, tiled=True)

    slots = jnp.arange(peers, dtype=jnp.int32)
    sequence = jnp.sum(jnp.where(slots == rank, order[0], 0))
    valid = jnp.sum(jnp.where(slots == sequence, lengths[0], 0))[None]
    direct = peers == PLANE * PLANE and lax.axis_size("rep") == REP and piece % 16 == 0
    sizes = [v.size for v in (norm_weight, conv_weight, conv_bias, gate_norm_weight)]
    if direct:
        few = jnp.concatenate([v.astype(F32).reshape(-1) for v in (norm_weight, conv_weight, conv_bias, gate_norm_weight)])
        few = jnp.pad(few, (0, FEW - few.size)).reshape(EDGE, TILE)
        tok, in_full, out_full, few = run_gather(tokens, in_weight, out_weight, few)
        few = few.reshape(peers, FEW)
        ends = [sum(sizes[: i + 1]) for i in range(4)]
        norm_full, conv_full, shift_full, gate_full = (
            few[:, e - s : e].reshape(-1) for s, e in zip(sizes, ends)
        )
        conv_full = conv_full.reshape(XBC, CONV)
    else:
        tok = to_sequences(tokens)
        norm_full, in_full, conv_full = gather(norm_weight), gather(in_weight), gather(conv_weight)
        shift_full, gate_full, out_full = gather(conv_bias), gather(gate_norm_weight), gather(out_weight)
    cot = to_sequences(cotangent)
    params = prepare(norm_full, in_full, conv_full, shift_full, gate_full, out_full, step_bias, decay_log, skip_gain)
    out, cin, gr, mx, st, sr, normed, gate_low = run_forward(valid, tok, params)
    output = to_slots(out)
    ig, gp, gb, taps, gcb, ggn, gsk, gnw, ghd = run_backward(valid, cot, tok, params, (cin, gr, mx, st, sr))
    few = [jnp.sum(gnw, axis=0), jnp.sum(taps, axis=1).T, jnp.sum(gcb, axis=0), jnp.sum(ggn, axis=0)]
    heads = jnp.stack([
        jnp.sum(ghd[:EDGE], axis=0)[:HEADS], jnp.sum(ghd[EDGE:], axis=0)[:HEADS],
        jnp.sum(gsk.reshape(EDGE, HEADS, HEADDIM), axis=(0, 2)),
    ])
    if direct:
        rows = [v.reshape(peers, -1) for v in few] + [jnp.broadcast_to(heads.reshape(1, -1), (peers, heads.size))]
        few = jnp.concatenate(rows, axis=1)
        few = jnp.pad(few, ((0, 0), (0, FEW - few.shape[1]))).reshape(peers, EDGE, TILE)
        input_grad, grad_in, grad_out, few = run_scatter(peers, ig, normed, gp, gate_low, gb, few)
        few = few.reshape(-1)
        few, heads = [few[e - s : e] for s, e in zip(sizes, ends)], few[ends[3] : ends[3] + heads.size].reshape(heads.shape)
        few[1] = few[1].reshape(-1, CONV)
    else:
        input_grad = to_slots(ig)

        def scatter(v):
            return lax.psum(lax.psum_scatter(v, "shard", scatter_dimension=0, tiled=True), "rep")

        few = [scatter(v) for v in few]
        grad_in, grad_out = scatter(mul_tn(normed, gp)), scatter(mul_tn(gate_low, gb))
        heads = lax.psum(heads, ("rep", "shard"))
    return (
        output, input_grad, few[0], grad_in, few[1], few[2], heads[0], heads[1], heads[2], few[3], grad_out,
    )


def solution(mesh):
    placed = (
        P("rep", "shard", None), P("rep", "shard", None), P("rep", None), P("rep", None), P("shard"),
        P("shard", None), P("shard", None), P("shard"), P(), P(), P(), P("shard"), P("shard", None),
    )
    outs = (
        P("rep", "shard", None), P("rep", "shard", None), P("shard"), P("shard", None), P("shard", None),
        P("shard"), P(), P(), P(), P("shard"), P("shard", None),
    )
    return jax.shard_map(on_device, mesh=mesh, in_specs=placed, out_specs=outs, check_vma=False)
```

```python
import functools

import jax
import jax.numpy as jnp
from jax import lax
from jax.experimental import pallas as pl
from jax.experimental.pallas import tpu as pltpu
from jax.sharding import PartitionSpec as P

HEADS = 24
HEADDIM = 64
STATE = 128
CONV = 4
SPAN = 256
DI = 1536
XBC = 1792
TILE = 128
PAIRS = DI // TILE
HALF = SPAN // 2
EDGE = 8
epsilon = 1e-05
F32 = jnp.float32
BF16 = jnp.bfloat16
FULL = lax.Precision.HIGHEST


def mul(a, b):
    return jnp.dot(a, b, preferred_element_type=F32)


def mul_nt(a, b):
    return lax.dot_general(a, b, (((1,), (1,)), ((), ())), preferred_element_type=F32)


def mul_tn(a, b):
    return lax.dot_general(a, b, (((0,), (0,)), ((), ())), preferred_element_type=F32)


def sigmoid(v):
    return 0.5 * jnp.tanh(0.5 * v) + 0.5


def softplus(v):
    return jnp.maximum(v, 0.0) + jnp.log1p(jnp.exp(-jnp.abs(v)))


def fold(v):
    return jnp.sum(v.reshape(v.shape[0] // EDGE, EDGE, v.shape[1]), axis=0)


def tile_at(j, base=0):
    return pl.ds(pl.multiple_of(base + j * TILE, TILE), TILE)


def lane_low(shape):
    return lax.broadcasted_iota(jnp.int32, shape, 1) < HEADDIM


def spread(column, h):
    return jnp.broadcast_to(column[:, h : h + 1], (column.shape[0], TILE))


def conv_argument(cin_ref, cw_ref, cb_ref, cols):
    total = cb_ref[:, cols]
    for tap in range(CONV):
        start = EDGE - CONV + 1 + tap
        total = total + cw_ref[tap : tap + 1, cols] * cin_ref[0, start : start + SPAN, cols]
    return total


def head_times(step_raw, step_bias, decay_log):
    shifted = step_raw + step_bias
    step = softplus(shifted)
    log_decay = -jnp.exp(decay_log) * step
    rows = lax.broadcasted_iota(jnp.int32, (SPAN, SPAN), 0)
    columns = lax.broadcasted_iota(jnp.int32, (SPAN, SPAN), 1)
    lower = (rows >= columns).astype(F32)
    cumul = jnp.dot(lower, log_decay, precision=FULL, preferred_element_type=F32)
    return shifted, step, cumul, cumul - jnp.log(step)


def causal_mask(flip):
    rows = lax.broadcasted_iota(jnp.int32, (HALF, HALF), 0)
    columns = lax.broadcasted_iota(jnp.int32, (HALF, HALF), 1)
    return columns >= rows if flip else rows >= columns


def forward_start(w_ref, ws, state, cin_ref):
    ws[...] = jnp.zeros_like(ws)
    ws[:, :HEADS] = w_ref[:, DI + XBC : DI + XBC + HEADS]
    state[...] = jnp.zeros_like(state)
    cin_ref[0, :EDGE, :] = jnp.zeros((EDGE, XBC), F32)


def forward_step(
    block, len_ref, tok_ref, w_ref, ow_ref, nw_ref, cw_ref, cb_ref, sb_ref, dl_ref, sk_ref, gn_ref,
    out_ref, cin_ref, gr_ref, mx_ref, st_ref, sr_ref, nl_ref, gl_ref,
    ws, col_t, pair_s, row_s, state, scores, gated, hook=None,
):
    offset = block * SPAN

    @pl.when(block > 0)
    def _():
        cin_ref[0, :EDGE, :] = gated[:EDGE, :]

    for r in range(0, SPAN, 64):
        tok = tok_ref[r : r + 64, :].astype(F32)
        nrm = lax.rsqrt(jnp.mean(tok * tok, axis=-1, keepdims=True) + epsilon)
        nl_ref[r : r + 64, :] = (tok * nrm * nw_ref[...]).astype(BF16)
    low = nl_ref[...]
    sr_ref[...] = mul(low, ws[...])
    for n in range(0, XBC, 256):
        cin_ref[0, EDGE:, n : n + 256] = mul(low, w_ref[:, DI + n : DI + n + 256])
    for n in range(0, DI, 256):
        gr_ref[:, n : n + 256] = mul(low, w_ref[:, n : n + 256])

    _, _, cumul, shift = head_times(sr_ref[...], sb_ref[...], dl_ref[...])
    row_s[...] = shift.T
    low_lanes = lane_low((SPAN, TILE))
    for h in range(HEADS):
        col_t[h] = spread(cumul, h)
    for j in range(PAIRS):
        pair_s[j] = jnp.where(low_lanes, spread(shift, 2 * j), spread(shift, 2 * j + 1))

    def act(jt):
        arg = conv_argument(cin_ref, cw_ref, cb_ref, tile_at(jt))
        return arg * sigmoid(arg)

    key = act(PAIRS).astype(BF16)
    query = act(PAIRS + 1).astype(BF16)
    key_t = key.astype(F32).T.astype(BF16)
    scores[...] = mul_nt(query, key)
    st_ref[0] = state[...]
    mask = causal_mask(False)

    def pair(j, total):
        cols = tile_at(j)
        if hook is not None:
            hook(j)
        heads_in = act(j)
        heads_low = heads_in.astype(BF16)
        cum0, cum1 = col_t[2 * j], col_t[2 * j + 1]
        cum = jnp.where(low_lanes, cum0, cum1)
        last = cum[SPAN - 1 : SPAN, :]
        old = state[:, cols]
        across = mul(query, old.astype(BF16))
        weighted = (heads_low.astype(F32) * jnp.exp(last - pair_s[j])).astype(BF16)
        state[:, cols] = jnp.exp(last) * old + mul(key_t, weighted)
        zero = jnp.zeros_like(heads_low)
        parts = (jnp.where(low_lanes, heads_low, zero), jnp.where(low_lanes, zero, heads_low))
        top, bottom = [], []
        for h in range(2):
            col = (cum0, cum1)[h]
            row = row_s[pl.ds(2 * j + h, 1), :]
            first = jnp.where(mask, col[:HALF] - row[:, :HALF], -jnp.inf)
            top.append((scores[:HALF, :HALF] * jnp.exp(first)).astype(BF16))
            full = col[HALF:] - row[:, :HALF]
            bottom.append((scores[HALF:, :HALF] * jnp.exp(full)).astype(BF16))
            second = jnp.where(mask, col[HALF:] - row[:, HALF:], -jnp.inf)
            bottom.append((scores[HALF:, HALF:] * jnp.exp(second)).astype(BF16))
        tops = jnp.concatenate([p[:HALF] for p in parts], axis=0)
        within = jnp.concatenate(
            [
                mul(jnp.concatenate(top, axis=1), tops),
                mul(jnp.concatenate(bottom, axis=1), jnp.concatenate(parts, axis=0)),
            ],
            axis=0,
        )
        mixed = within + jnp.exp(cum) * across + sk_ref[:, cols] * heads_in
        mx_ref[:, cols] = mixed
        gate = gr_ref[:, cols]
        value = mixed * (gate * sigmoid(gate))
        gated[:, cols] = value
        return total + value * value

    total = lax.fori_loop(0, PAIRS, pair, jnp.zeros((SPAN, TILE), F32))
    rms = lax.rsqrt(jnp.sum(total, axis=-1, keepdims=True) * (1.0 / DI) + epsilon)

    def finish(j, carry):
        cols = tile_at(j)
        gl_ref[:, cols] = (gated[:, cols] * rms * gn_ref[:, cols]).astype(BF16)
        return carry

    lax.fori_loop(0, PAIRS, finish, 0)
    positions = offset + lax.broadcasted_iota(jnp.int32, (SPAN, 256), 0)
    valid = positions < len_ref[0]
    for n in range(0, tok_ref.shape[1], 256):
        branch = mul(gl_ref[...], ow_ref[:, n : n + 256])
        tok = tok_ref[:, n : n + 256].astype(F32)
        out_ref[:, n : n + 256] = (tok + jnp.where(valid, branch, 0.0)).astype(BF16)
    gated[:EDGE, :] = cin_ref[0, SPAN:, :]


def forward_kernel(
    len_ref, tok_ref, w_ref, ow_ref, nw_ref, cw_ref, cb_ref, sb_ref, dl_ref, sk_ref, gn_ref,
    out_ref, cin_ref, gr_ref, mx_ref, st_ref, sr_ref, nl_ref, gl_ref,
    ws, col_t, pair_s, row_s, state, scores, gated,
):
    block = pl.program_id(0)

    @pl.when(block == 0)
    def _():
        forward_start(w_ref, ws, state, cin_ref)

    forward_step(
        block, len_ref, tok_ref, w_ref, ow_ref, nw_ref, cw_ref, cb_ref, sb_ref, dl_ref, sk_ref, gn_ref,
        out_ref, cin_ref, gr_ref, mx_ref, st_ref, sr_ref, nl_ref, gl_ref,
        ws, col_t, pair_s, row_s, state, scores, gated,
    )


def backward_kernel(
    len_ref, cot_ref, tok_ref, w_ref, ow_ref, nw_ref, cw_ref, cb_ref, sb_ref, dl_ref, sk_ref, gn_ref,
    cin_ref, gr_ref, mx_ref, st_ref, sr_ref,
    ig_ref, gp_ref, gb_ref, taps_ref, gcb_ref, ggn_ref, gsk_ref, gnw_ref, ghd_ref,
    ws, col_s, pair_t, row_t, later, scores, grad_scores, gg, sig, gpre, args, acc_q, acc_k, acc_u, acc_v, acc_l,
):
    step_id = pl.program_id(0)
    count = pl.num_programs(0)
    offset = (count - 1 - step_id) * SPAN

    @pl.when(step_id == 0)
    def _():
        ws[...] = jnp.zeros_like(ws)
        ws[:, :HEADS] = w_ref[:, DI + XBC : DI + XBC + HEADS]
        later[...] = jnp.zeros_like(later)
        gpre[SPAN:, :] = jnp.zeros((EDGE, XBC), F32)
        for ref in (taps_ref, gcb_ref, ggn_ref, gsk_ref, gnw_ref, ghd_ref):
            ref[...] = jnp.zeros_like(ref)

    width = cot_ref.shape[1]
    positions = offset + lax.broadcasted_iota(jnp.int32, (SPAN, width), 0)
    grad_branch = jnp.where(positions < len_ref[0], cot_ref[...].astype(F32), 0.0).astype(BF16)
    gb_ref[...] = grad_branch
    for n in range(0, DI, 256):
        gg[:, n : n + 256] = mul_nt(grad_branch, ow_ref[n : n + 256, :])

    shifted, step, cumul, shift = head_times(sr_ref[...], sb_ref[...], dl_ref[...])
    row_t[...] = cumul.T
    low_lanes = lane_low((SPAN, TILE))
    for h in range(HEADS):
        col_s[h] = spread(shift, h)
    for j in range(PAIRS):
        pair_t[j] = jnp.where(low_lanes, spread(cumul, 2 * j), spread(cumul, 2 * j + 1))

    def sums(j, carry):
        squares, crossed = carry
        cols = tile_at(j)
        gate = gr_ref[:, cols]
        part = sigmoid(gate)
        sig[:, cols] = part
        value = mx_ref[:, cols] * (gate * part)
        return squares + value * value, crossed + (gg[:, cols] * gn_ref[:, cols]) * value

    nothing = jnp.zeros((SPAN, TILE), F32)
    squares, crossed = lax.fori_loop(0, PAIRS, sums, (nothing, nothing))
    rms = lax.rsqrt(jnp.sum(squares, axis=-1, keepdims=True) * (1.0 / DI) + epsilon)
    coef = rms * rms * (jnp.sum(crossed, axis=-1, keepdims=True) * (1.0 / DI))
    rms = jnp.broadcast_to(rms, (SPAN, TILE))
    coef = jnp.broadcast_to(coef, (SPAN, TILE))

    def act(jt, slot):
        arg = conv_argument(cin_ref, cw_ref, cb_ref, tile_at(jt))
        args[:, slot * TILE : (slot + 1) * TILE] = arg
        return (arg * sigmoid(arg)).astype(BF16)

    key = act(PAIRS, 0)
    query = act(PAIRS + 1, 1)
    query_t = query.astype(F32).T.astype(BF16)
    scores[...] = mul_nt(key, query)
    grad_scores[...] = jnp.zeros_like(grad_scores)
    for ref in (acc_q, acc_k, acc_u, acc_v, acc_l):
        ref[...] = jnp.zeros_like(ref)
    mask = causal_mask(True)
    lane = lax.broadcasted_iota(jnp.int32, (2 * TILE, TILE), 0) % TILE
    head = lax.broadcasted_iota(jnp.int32, (2 * TILE, TILE), 1)

    def by_head(value, pick):
        high = value.astype(BF16)
        rest = (value - high.astype(F32)).astype(BF16)
        return mul(jnp.concatenate([high, rest], axis=1), pick)

    def pair(j, carry):
        cols = tile_at(j)
        arg = conv_argument(cin_ref, cw_ref, cb_ref, cols)
        part_x = sigmoid(arg)
        heads_in = arg * part_x
        heads_low = heads_in.astype(BF16)
        heads_float = heads_low.astype(F32)
        gate, mixed, part, gain, back = (
            gr_ref[:, cols], mx_ref[:, cols], sig[:, cols], gn_ref[:, cols], gg[:, cols]
        )
        silu = gate * part
        value = mixed * silu
        ggn_ref[:, cols] += fold(back * value * rms)
        grad_gated = rms * (back * gain - value * coef)
        grad_scan = grad_gated * silu
        gp_ref[:, cols] = (grad_gated * mixed * (part * (1.0 + gate * (1.0 - part)))).astype(BF16)
        gsk_ref[:, cols] += fold(grad_scan * heads_in)
        cum = pair_t[j]
        growth = jnp.exp(cum)
        last = cum[SPAN - 1 : SPAN, :]
        grad_low = grad_scan.astype(BF16)
        scaled = growth * grad_scan
        grad_across = scaled.astype(BF16)
        col0, col1 = col_s[2 * j], col_s[2 * j + 1]
        carry_weight = jnp.exp(last - jnp.where(low_lanes, col0, col1))
        weighted = (heads_float * carry_weight).astype(BF16)
        after = later[:, cols]
        after_low = after.astype(BF16)
        before = st_ref[0, :, cols]
        before_low = before.astype(BF16)
        across = mul(query, before_low)
        acc_k[...] += mul_nt(weighted, after_low)
        acc_q[...] += mul_nt(grad_across, before_low)
        grow_last = jnp.exp(last)
        carried = mul(key, after_low) * carry_weight
        last_sum = fold(carried * heads_float) + fold(after * before) * grow_last
        later[:, cols] = mul(query_t, grad_across) + grow_last * after
        zero = jnp.zeros_like(grad_low)
        parts = (jnp.where(low_lanes, grad_low, zero), jnp.where(low_lanes, zero, grad_low))
        top, bottom = [], []
        for h in range(2):
            col = (col0, col1)[h]
            row = row_t[pl.ds(2 * j + h, 1), :]
            mixed_top = mul_nt(heads_low[:HALF], parts[h])
            mixed_low = mul_nt(heads_low[HALF:], parts[h][HALF:])
            factor = jnp.exp(jnp.where(mask, row[:, :HALF] - col[:HALF], -jnp.inf))
            top.append((scores[:HALF, :HALF] * factor).astype(BF16))
            grad_scores[:HALF, :HALF] += mixed_top[:, :HALF] * factor
            factor = jnp.exp(row[:, HALF:] - col[:HALF])
            top.append((scores[:HALF, HALF:] * factor).astype(BF16))
            grad_scores[:HALF, HALF:] += mixed_top[:, HALF:] * factor
            factor = jnp.exp(jnp.where(mask, row[:, HALF:] - col[HALF:], -jnp.inf))
            bottom.append((scores[HALF:, HALF:] * factor).astype(BF16))
            grad_scores[HALF:, HALF:] += mixed_low * factor
        lows = jnp.concatenate([p[HALF:] for p in parts], axis=0)
        grad_heads = carried + jnp.concatenate(
            [
                mul(jnp.concatenate(top, axis=1), jnp.concatenate(parts, axis=0)),
                mul(jnp.concatenate(bottom, axis=1), lows),
            ],
            axis=0,
        )
        gain_skip = sk_ref[:, cols]
        spanned = growth * across
        within = mixed - gain_skip * heads_in - spanned
        pick = (head == 2 * j + lane // HEADDIM).astype(F32)
        pick_low = pick.astype(BF16)
        acc_u[...] += by_head(grad_low.astype(F32) * within + grad_scan * spanned, pick_low)
        acc_v[...] += by_head(heads_float * grad_heads, pick_low)
        acc_l[...] += jnp.dot(last_sum, pick[:TILE], precision=FULL, preferred_element_type=F32)
        grad_conv = grad_heads + gain_skip * grad_scan
        gpre[:SPAN, cols] = grad_conv * (part_x * (1.0 + arg * (1.0 - part_x)))
        return carry

    lax.fori_loop(0, PAIRS, pair, 0)

    rows = lax.broadcasted_iota(jnp.int32, (SPAN, SPAN), 0)
    columns = lax.broadcasted_iota(jnp.int32, (SPAN, SPAN), 1)
    upper = (columns >= rows).astype(F32)
    at_end = lax.broadcasted_iota(jnp.int32, (SPAN, TILE), 0) == SPAN - 1
    to_step = acc_v[...]
    ends = jnp.sum(acc_l[...], axis=0, keepdims=True)
    grad_cumul = acc_u[...] - to_step + jnp.where(at_end, ends, 0.0)
    grad_log = jnp.dot(upper, grad_cumul, precision=FULL, preferred_element_type=F32)
    rate = jnp.exp(dl_ref[...])
    safe = jnp.where(step > 0.0, step, 1.0)
    grad_step = jnp.where(step > 0.0, to_step / safe, 0.0)
    grad_raw = (grad_step - rate * grad_log) * sigmoid(shifted)
    ghd_ref[:EDGE, :] += fold(grad_raw)
    ghd_ref[EDGE:, :] -= fold(rate * step * grad_log)
    raw_low = grad_raw.astype(BF16)
    gp_ref[:, DI + XBC :] = raw_low[:, :HEADS]

    scores_low = grad_scores[...].astype(BF16)
    scores_t = grad_scores[...].T.astype(BF16)
    for slot, grad in (
        (0, acc_k[...] + mul(scores_low, query)),
        (1, acc_q[...] + mul(scores_t, key)),
    ):
        arg = args[:, slot * TILE : (slot + 1) * TILE]
        part = sigmoid(arg)
        gpre[:SPAN, DI + slot * TILE : DI + (slot + 1) * TILE] = grad * (part * (1.0 + arg * (1.0 - part)))

    def through_conv(j, carry):
        cols = tile_at(j)
        here = gpre[:SPAN, cols]
        gcb_ref[:, cols] += fold(here)
        total = jnp.zeros_like(here)
        for tap in range(CONV):
            start = EDGE - CONV + 1 + tap
            taps_ref[tap, :, cols] += fold(here * cin_ref[0, start : start + SPAN, cols])
            ahead = CONV - 1 - tap
            total = total + cw_ref[tap : tap + 1, cols] * gpre[ahead : ahead + SPAN, cols]
        gp_ref[:, tile_at(j, DI)] = total.astype(BF16)
        return carry

    lax.fori_loop(0, PAIRS + 2, through_conv, 0)
    gpre[SPAN:, :] = gpre[:EDGE, :]

    for n in range(0, width, 256):
        grad = mul_nt(gp_ref[:, : DI + XBC], w_ref[n : n + 256, : DI + XBC])
        gg[:, n : n + 256] = grad + mul_nt(raw_low, ws[n : n + 256, :])
    for r in range(0, SPAN, 64):
        tok = tok_ref[r : r + 64, :].astype(F32)
        nrm = lax.rsqrt(jnp.mean(tok * tok, axis=-1, keepdims=True) + epsilon)
        grad = gg[r : r + 64, :width]
        gnw_ref[...] += fold(grad * tok * nrm)
        value = grad * nw_ref[...]
        centre = jnp.mean(value * tok, axis=-1, keepdims=True) * (nrm * nrm)
        grad_tok = nrm * (value - tok * centre)
        ig_ref[r : r + 64, :] = (cot_ref[r : r + 64, :].astype(F32) + grad_tok).astype(BF16)


def whole(shape):
    return pl.BlockSpec(shape, lambda i: (0,) * len(shape), pipeline_mode=pl.Buffered(1))


def rows_of(width, last=None):
    if last is None:
        return pl.BlockSpec((SPAN, width), lambda i: (i, 0))
    return pl.BlockSpec((SPAN, width), lambda i: (last - i, 0))


def params_specs(width, proj):
    return [
        whole((width, proj)), whole((DI, width)), whole((1, width)), whole((CONV, XBC)), whole((1, XBC)),
        whole((1, TILE)), whole((1, TILE)), whole((1, DI)), whole((1, DI)),
    ]


LIMIT = 60 * 2**20


def forward_results(length, width):
    count = length // SPAN
    shapes = [
        ((length, width), BF16), ((count, SPAN + EDGE, XBC), F32), ((length, DI), F32), ((length, DI), F32),
        ((count, STATE, DI), F32), ((length, TILE), F32), ((length, width), BF16), ((length, DI), BF16),
    ]
    out_specs = [
        rows_of(width), pl.BlockSpec((1, SPAN + EDGE, XBC), lambda i: (i, 0, 0)), rows_of(DI), rows_of(DI),
        pl.BlockSpec((1, STATE, DI), lambda i: (i, 0, 0)), rows_of(TILE), rows_of(width), rows_of(DI),
    ]
    scratch = [
        pltpu.VMEM((width, TILE), BF16), pltpu.VMEM((HEADS, SPAN, TILE), F32), pltpu.VMEM((PAIRS, SPAN, TILE), F32),
        pltpu.VMEM((TILE, SPAN), F32), pltpu.VMEM((STATE, DI), F32), pltpu.VMEM((SPAN, SPAN), F32), pltpu.VMEM((SPAN, XBC), F32),
    ]
    return [jax.ShapeDtypeStruct(s, d) for s, d in shapes], out_specs, scratch


def run_forward(valid, tok, params):
    length, width = tok.shape
    shapes, out_specs, scratch = forward_results(length, width)
    return pl.pallas_call(
        forward_kernel,
        grid=(length // SPAN,),
        out_shape=shapes,
        in_specs=[pl.BlockSpec(memory_space=pltpu.SMEM), rows_of(width), *params_specs(width, params[0].shape[1])],
        out_specs=out_specs,
        scratch_shapes=scratch,
        compiler_params=pltpu.CompilerParams(dimension_semantics=("arbitrary",), vmem_limit_bytes=LIMIT),
        cost_estimate=pl.CostEstimate(flops=20 * 10**9, bytes_accessed=60 * 10**6, transcendentals=10**7),
    )(valid, tok, *params)


def run_backward(valid, cot, tok, params, kept):
    length, width = tok.shape
    count = length // SPAN
    proj = DI + XBC + HEADS
    last = count - 1
    shapes = [
        ((length, width), BF16), ((length, proj), BF16), ((length, width), BF16), ((CONV, EDGE, XBC), F32), ((EDGE, XBC), F32), ((EDGE, DI), F32),
        ((EDGE, DI), F32), ((EDGE, width), F32), ((2 * EDGE, TILE), F32),
    ]
    out_specs = [rows_of(width, last), rows_of(proj, last), rows_of(width, last), *(whole(s) for s, _ in shapes[3:])]
    kept_specs = [
        pl.BlockSpec((1, SPAN + EDGE, XBC), lambda i: (last - i, 0, 0)), rows_of(DI, last), rows_of(DI, last),
        pl.BlockSpec((1, STATE, DI), lambda i: (last - i, 0, 0)), rows_of(TILE, last),
    ]
    square, wide = pltpu.VMEM((SPAN, SPAN), F32), pltpu.VMEM((SPAN, DI), F32)
    narrow = pltpu.VMEM((SPAN, TILE), F32)
    return pl.pallas_call(
        backward_kernel,
        grid=(count,),
        out_shape=[jax.ShapeDtypeStruct(s, d) for s, d in shapes],
        in_specs=[pl.BlockSpec(memory_space=pltpu.SMEM), rows_of(width, last), rows_of(width, last), *params_specs(width, params[0].shape[1]), *kept_specs],
        out_specs=out_specs,
        scratch_shapes=[
            pltpu.VMEM((width, TILE), BF16), pltpu.VMEM((HEADS, SPAN, TILE), F32), pltpu.VMEM((PAIRS, SPAN, TILE), F32),
            pltpu.VMEM((TILE, SPAN), F32), pltpu.VMEM((STATE, DI), F32), square, square, wide, wide,
            pltpu.VMEM((SPAN + EDGE, XBC), F32), pltpu.VMEM((SPAN, 2 * TILE), F32),
            narrow, narrow, narrow, narrow, pltpu.VMEM((EDGE, TILE), F32),
        ],
        compiler_params=pltpu.CompilerParams(dimension_semantics=("arbitrary",), vmem_limit_bytes=LIMIT),
        cost_estimate=pl.CostEstimate(flops=40 * 10**9, bytes_accessed=60 * 10**6, transcendentals=2 * 10**7),
    )(valid, cot, tok, *params, *kept)


def prepare(norm_full, in_full, conv_full, shift_full, gate_full, out_full, step_bias, decay_log, skip_gain):
    pad = ((0, 0), (0, TILE - HEADS))
    return (
        in_full,
        out_full,
        norm_full.astype(F32)[None],
        conv_full.astype(F32).T,
        shift_full.astype(F32)[None],
        jnp.pad(step_bias[None], pad),
        jnp.pad(decay_log[None], pad),
        jnp.repeat(skip_gain, HEADDIM)[None],
        gate_full.astype(F32)[None],
    )


MESH = pl.DeviceIdType.MESH
PLANE = 4
REP = 2
COT_AT = 1


def lay_out(few, n, nw_ref, cw_ref, cb_ref, gn_ref):
    for ref, row in ((nw_ref, 0), (cw_ref, 1), (cb_ref, 1 + CONV), (gn_ref, 2 + CONV)):
        size = ref.shape[1] // n
        for k in range(n):
            ref[:, k * size : (k + 1) * size] = few[k, row : row + ref.shape[0], :size]


def gather_forward_kernel(n, *refs):
    len_ref, tok_ref, cot_ref, in_ref, ow_ref, small_ref, head_ref = refs[:7]
    blocks = refs[7:15]
    seq_ref, cots_ref, inf_ref, owf_ref, nw_ref, cw_ref, cb_ref, sk_ref, gn_ref = refs[15:24]
    own_scratch = refs[24:31]
    (
        tok_v, w_v, ow_v, few, tok_stage, cot_stage, own,
        tok_s, tok_r, tok_fs, tok_fr, tok_l, cot_s, cot_r, cot_fs, cot_fr, cot_l, small_s, small_r, line_s, line_r, plane_s, plane_r, sib_s, sib_r, keep_s,
    ) = refs[31:]
    planes = n // PLANE
    block = pl.program_id(0)
    me = lax.axis_index("shard")
    core = lax.axis_index("rep")
    z, y, x = me // PLANE, (me // 2) % 2, me % 2
    across = me + 1 - 2 * x
    along = me + 2 - 4 * y
    piece = tok_ref.shape[1]
    arrays = ((in_ref, w_v), (ow_ref, ow_v))

    def region(a, k, part=None):
        src, dst = arrays[a]
        half = src.shape[1] // REP
        first = pl.cdiv(half // TILE, 2) * TILE
        rows = pl.ds(pl.multiple_of(k * src.shape[0], src.shape[0]), src.shape[0])
        start, size = ((0, first), (first, half - first), (0, half))[2 if part is None else part]
        return dst.at[rows, pl.ds(pl.multiple_of(core * half + start, TILE), size)]

    def send(view, to, s, r):
        return pltpu.make_async_remote_copy(
            src_ref=view, dst_ref=view, send_sem=s, recv_sem=r, device_id=to, device_id_type=MESH
        )

    def line(a, origin, to):
        return send(region(a, origin), {"shard": to}, line_s.at[a, origin // PLANE, (to > me).astype(jnp.int32)], line_r.at[a, origin // PLANE])

    def hop(a, zz, kind):
        here = zz * PLANE + 2 * y + x
        side = zz * PLANE + 2 * y + 1 - x
        ahead = zz * PLANE + 2 * (1 - y) + x
        origin, part, to = (
            (here, 0, across), (here, 1, along), (here, 0, along), (here, 1, across), (side, 0, along), (ahead, 1, across),
        )[kind]
        return send(region(a, origin, part), {"shard": to}, plane_s.at[a, zz, kind], plane_r.at[a, zz, kind])

    def sibling(a, zz, kind):
        origin = zz * PLANE + (2 * y + x, 2 * y + 1 - x, 2 * (1 - y) + x, 2 * (1 - y) + 1 - x)[kind]
        return send(region(a, origin), {"rep": 1 - core}, sib_s.at[a, zz, kind], sib_r.at[a, zz, kind])

    def rows(k):
        return pl.ds(pl.multiple_of(k * piece, piece), piece)

    quad = me % PLANE
    moves = (
        (tok_ref, tok_stage, tok_v, tok_s, tok_r, tok_fs, tok_fr, tok_l),
        (cot_ref, cot_stage, cots_ref, cot_s, cot_r, cot_fs, cot_fr, cot_l),
    )

    def stage_copy(m, to, source):
        src, stage, _, ss, sr = moves[m][:5]
        return pltpu.make_async_remote_copy(
            src_ref=src.at[pl.ds(pl.multiple_of(to * PLANE, PLANE), PLANE)], dst_ref=stage.at[source],
            send_sem=ss.at[to], recv_sem=sr.at[source],
            device_id={"shard": to * PLANE + quad}, device_id_type=MESH,
        )

    def own_stage(m):
        src, stage = moves[m][:2]
        return pltpu.make_async_copy(src.at[pl.ds(pl.multiple_of(z * PLANE, PLANE), PLANE)], stage.at[z], moves[m][7].at[planes])

    def pass_copy(m, zz, j, source):
        _, stage, dst, _, _, ss, sr, _ = moves[m]
        return pltpu.make_async_remote_copy(
            src_ref=stage.at[zz, j], dst_ref=dst.at[rows(zz * PLANE + source)],
            send_sem=ss.at[zz, j], recv_sem=sr.at[zz, source],
            device_id={"shard": z * PLANE + j}, device_id_type=MESH,
        )

    def keep_copy(m, zz):
        _, stage, dst = moves[m][:3]
        return pltpu.make_async_copy(stage.at[zz, quad], dst.at[rows(zz * PLANE + quad)], moves[m][7].at[zz])

    def start_stage(m):
        for p in range(planes):
            @pl.when(p != z)
            def _():
                stage_copy(m, p, z).start()

    def pass_on(m, zz):
        @pl.when(zz != z)
        def _():
            stage_copy(m, zz, zz).wait_recv()

        for j in range(PLANE):
            @pl.when(j != quad)
            def _():
                pass_copy(m, zz, j, quad).start()

        keep_copy(m, zz).start()

    def landed(m, zz):
        for j in range(PLANE):
            @pl.when(j != quad)
            def _():
                pass_copy(m, zz, j, j).wait_recv()

        keep_copy(m, zz).wait()

    def gone(m):
        for zz in range(planes):
            @pl.when(zz != z)
            def _():
                stage_copy(m, zz, z).wait_send()

            for j in range(PLANE):
                @pl.when(j != quad)
                def _():
                    pass_copy(m, zz, j, quad).wait_send()

    def small_copy(to, source):
        return pltpu.make_async_remote_copy(
            src_ref=small_ref, dst_ref=few.at[source], send_sem=small_s.at[to], recv_sem=small_r.at[source],
            device_id={"shard": to}, device_id_type=MESH,
        )

    def local_copies():
        both = [
            pltpu.make_async_copy(src, dst.at[pl.ds(pl.multiple_of(me * src.shape[0], 8), src.shape[0])], own.at[a])
            for a, (src, dst) in enumerate(arrays)
        ]
        return both + [
            pltpu.make_async_copy(small_ref, few.at[me], own.at[2]),
            own_stage(0),
            own_stage(1),
        ]

    def saves():
        return [
            pltpu.make_async_copy(w_v, inf_ref, keep_s.at[0]),
            pltpu.make_async_copy(ow_v, owf_ref, keep_s.at[1]),
        ]

    def launch(a, zz):
        for kind in range(4):
            hop(a, zz, kind).start()

    def relay(a, zz):
        hop(a, zz, 0).wait_recv()
        hop(a, zz, 4).start()
        hop(a, zz, 1).wait_recv()
        hop(a, zz, 5).start()

    def collect(a, zz):
        hop(a, zz, 3).wait_recv()
        sibling(a, zz, 1).start()
        hop(a, zz, 2).wait_recv()
        sibling(a, zz, 2).start()
        hop(a, zz, 4).wait_recv()
        hop(a, zz, 5).wait_recv()
        sibling(a, zz, 3).start()

    def each(d, step):
        @pl.when(z - d >= 0)
        def _():
            step(z - d, me - d * PLANE, me + PLANE, z + 1 < planes)

        @pl.when(z + d < planes)
        def _():
            step(z + d, me + d * PLANE, me - PLANE, z > 0)

    def start_line(a):
        @pl.when(z + 1 < planes)
        def _():
            line(a, me, me + PLANE).start()

        @pl.when(z > 0)
        def _():
            line(a, me, me - PLANE).start()

    def arrived(a):
        def step(zz, origin, to, more):
            line(a, origin, to).wait_recv()

            @pl.when(more)
            def _():
                line(a, origin, to).start()

            sibling(a, zz, 0).start()
            launch(a, zz)

        return step

    def send_pieces(copy, first, last):
        for d in range(first, last):
            copy(lax.rem(me + d, n), me).start()

    @pl.when(block == 0)
    def _():
        barrier = pltpu.get_barrier_semaphore()
        for d in range(1, n):
            pl.semaphore_signal(barrier, inc=1, device_id={"shard": lax.rem(me + d, n)}, device_id_type=MESH)
        pl.semaphore_signal(barrier, inc=1, device_id={"rep": 1 - core}, device_id_type=MESH)
        local = local_copies()
        for copy in local:
            copy.start()
        for copy in local[:2]:
            copy.wait()
        pl.semaphore_wait(barrier, n)
        for a in range(2):
            start_line(a)
        for a in range(2):
            launch(a, z)

        @pl.when(z == 0)
        def _():
            start_stage(0)

        send_pieces(small_copy, 1, n)
        for d in range(1, planes):
            for a in range(2):
                each(d, arrived(a))
                if d == 1:
                    relay(a, z)
                else:
                    each(d - 1, lambda zz, *_: relay(a, zz))

        @pl.when(z > 0)
        def _():
            start_stage(0)

        for a in range(2):
            collect(a, z)
            each(planes - 1, lambda zz, *_: relay(a, zz))
        for a in range(2):
            for d in range(1, planes):
                each(d, lambda zz, *_: collect(a, zz))
        for copy in local[2:]:
            copy.wait()
        for k in range(n):
            @pl.when(me != k)
            def _():
                small_copy(k, k).wait_recv()
        lay_out(few, n, nw_ref, cw_ref, cb_ref, gn_ref)
        for h in range(HEADS):
            sk_ref[:, h * HEADDIM : (h + 1) * HEADDIM] = jnp.broadcast_to(head_ref[2:3, h : h + 1], (1, HEADDIM))
        for a in range(2):
            for d in range(planes):
                for kind in range(4):
                    if kind > 0:
                        sibling(a, d, kind).wait_recv()
                    else:
                        @pl.when(z != d)
                        def _():
                            sibling(a, d, kind).wait_recv()
        for copy in saves():
            copy.start()
        pass_on(0, 0)
        forward_start(w_v, own_scratch[0], own_scratch[4], blocks[1])

    @pl.when(block + 1 < planes)
    def _():
        pass_on(0, block + 1)

    landed(0, block)

    @pl.when(block == COT_AT)
    def _():
        start_stage(1)

    forward_step(
        block, len_ref, tok_v.at[pl.ds(pl.multiple_of(block * SPAN, SPAN), SPAN)], w_v, ow_v,
        nw_ref, cw_ref, cb_ref, head_ref.at[0:1], head_ref.at[1:2], sk_ref, gn_ref, *blocks, *own_scratch,
    )

    @pl.when(block == pl.num_programs(0) - 1)
    def _():
        keep = pltpu.make_async_copy(tok_v, seq_ref, keep_s.at[2])
        keep.start()
        for copy in saves():
            copy.wait()
        for zz in range(planes):
            pass_on(1, zz)
        for m in range(2):
            gone(m)
        for zz in range(planes):
            landed(1, zz)
        for k in range(n):
            @pl.when(me != k)
            def _():
                small_copy(k, k).wait_send()
        for a in range(2):
            def sent(zz, origin, to, more):
                @pl.when(more)
                def _():
                    line(a, origin, to).wait_send()

            for d in range(1, planes):
                each(d, sent)

            @pl.when(z + 1 < planes)
            def _():
                line(a, me, me + PLANE).wait_send()

            @pl.when(z > 0)
            def _():
                line(a, me, me - PLANE).wait_send()

            for zz in range(planes):
                for kind in range(6):
                    hop(a, zz, kind).wait_send()
                for kind in range(4):
                    if kind > 0:
                        sibling(a, zz, kind).wait_send()
                    else:
                        @pl.when(z != zz)
                        def _():
                            sibling(a, zz, kind).wait_send()
        keep.wait()


def run_gather_forward(valid, tokens, cotangent, in_weight, out_weight, small, heads):
    n, piece, width = tokens.shape
    length = n * piece
    planes = n // PLANE
    proj = in_weight.shape[1]
    inner = n * out_weight.shape[0]
    hbm = pl.BlockSpec(memory_space=pl.ANY)
    vmem = pl.BlockSpec(memory_space=pltpu.VMEM)
    dma = pltpu.SemaphoreType.DMA
    shapes, out_specs, scratch = forward_results(length, width)
    rows = [(1, width), (CONV, XBC), (1, XBC), (1, DI), (1, DI)]
    more = [((length, width), BF16)] * 2 + [((width, proj), BF16), ((inner, width), BF16)] + [(r, F32) for r in rows]
    results = pl.pallas_call(
        functools.partial(gather_forward_kernel, n),
        grid=(length // SPAN,),
        out_shape=shapes + [jax.ShapeDtypeStruct(s, d) for s, d in more],
        in_specs=[pl.BlockSpec(memory_space=pltpu.SMEM), hbm, hbm, hbm, hbm, vmem, vmem],
        out_specs=out_specs + [hbm] * 4 + [whole(r) for r in rows],
        scratch_shapes=scratch + [
            pltpu.VMEM((length, width), BF16), pltpu.VMEM((width, proj), BF16), pltpu.VMEM((inner, width), BF16),
            pltpu.VMEM((n, EDGE, TILE), F32), *(pltpu.VMEM((planes, PLANE, piece, width), BF16) for _ in range(2)), dma((3,)),
            *(dma(d) for _ in range(2) for d in ((planes,), (planes,), (planes, PLANE), (planes, PLANE), (planes + 1,))), dma((n,)), dma((n,)), dma((2, planes, 2)), dma((2, planes)),
            dma((2, planes, 6)), dma((2, planes, 6)), dma((2, planes, 4)), dma((2, planes, 4)), dma((3,)),
        ],
        compiler_params=pltpu.CompilerParams(
            dimension_semantics=("arbitrary",), collective_id=0, has_side_effects=True, vmem_limit_bytes=LIMIT
        ),
    )(valid, tokens, cotangent, in_weight, out_weight, small, heads)
    return results[:8], results[8:]


PARTS = (
    (1, 0, 384, 0), (1, 384, 384, 1), (0, 0, 768, 0), (0, 768, 768, 1), (0, 1536, 896, 0), (0, 2432, 920, 1),
)
SPREAD = (0, 4, 8, 12, 15)


def scatter_kernel(n, *refs):
    (
        ig_ref, nl_ref, gp_ref, gl_ref, gb_ref, small_ref,
        slot_ref, gin_ref, gout_ref, sum_ref,
    ) = refs[:10]
    refs = refs[10:]
    count = len(PARTS)
    bufs = [refs[i * 7 : (i + 1) * 7] for i in range(count)]
    (
        nl_t, gl_t, few, few_sib, own, ig_s, ig_r, few_s, few_r, pair_s, pair_r, s0s, s0r, s1s, s1r, s2s, s2r, s3s, s3r, s4s, s4r,
    ) = refs[count * 7 :]
    planes = n // PLANE
    me = lax.axis_index("shard")
    core = lax.axis_index("rep")
    z, y, x = me // PLANE, (me // 2) % 2, me % 2
    across = {"shard": me + 1 - 2 * x}
    along = {"shard": me + 2 - 4 * y}
    twin = {"rep": 1 - core}
    piece = slot_ref.shape[1]

    barrier = pltpu.get_barrier_semaphore()
    for d in range(1, n):
        pl.semaphore_signal(barrier, inc=1, device_id={"shard": lax.rem(me + d, n)}, device_id_type=MESH)
    pl.semaphore_signal(barrier, inc=1, device_id=twin, device_id_type=MESH)

    def remote(src, dst, s, r, to):
        return pltpu.make_async_remote_copy(
            src_ref=src, dst_ref=dst, send_sem=s, recv_sem=r, device_id=to, device_id_type=MESH
        )

    def ig_copy(d):
        to = lax.rem(me + d, n)
        src = ig_ref.at[pl.ds(pl.multiple_of(to * piece, 8), piece)]
        return remote(src, slot_ref.at[me], ig_s.at[d], ig_r.at[d], {"shard": to})

    def few_copy(d):
        to = lax.rem(me + d, n)
        return remote(small_ref.at[to], few.at[me], few_s.at[d], few_r.at[d], {"shard": to})

    first = core == 0

    def product(p):
        a, start, size, _ = PARTS[p]
        acc, s0 = bufs[p][0], bufs[p][1]
        left, right = (nl_t, gp_ref) if a == 0 else (gl_t, gb_ref)
        rows = acc.shape[3]
        for c in range(0, size, 256):
            wide = min(256, size - c)
            total = mul(left[...], right[:, start + c : start + c + wide])
            total = total.reshape(planes, 2, 2, 2, rows, wide)
            acc[:, :, :, :, c : c + wide] = jnp.where(first, total[:, :, :, 0], total[:, :, :, 1])
            s0[:, :, :, :, c : c + wide] = jnp.where(first, total[:, :, :, 1], total[:, :, :, 0]).astype(BF16)

    def c0(p):
        return remote(bufs[p][1], bufs[p][2], s0s.at[p], s0r.at[p], twin)

    def c1(p):
        sb, r1 = bufs[p][3], bufs[p][4]
        if PARTS[p][3] == 0:
            return remote(sb.at[:, 1 - y], r1, s1s.at[p], s1r.at[p], along)
        return remote(sb.at[:, :, 1 - x], r1, s1s.at[p], s1r.at[p], across)

    def c2(p):
        sb, r2 = bufs[p][3], bufs[p][5]
        if PARTS[p][3] == 0:
            return remote(sb.at[:, y, 1 - x], r2, s2s.at[p], s2r.at[p], across)
        return remote(sb.at[:, 1 - y, x], r2, s2s.at[p], s2r.at[p], along)

    def c3(p, dest, source):
        sb, r3 = bufs[p][3], bufs[p][6]
        to = {"shard": dest * PLANE + 2 * y + x}
        return remote(sb.at[dest, y, x], r3.at[source], s3s.at[p, dest], s3r.at[p, source], to)

    def into_half(p):
        acc, _, r0, sb = bufs[p][:4]
        c0(p).wait_recv()

        def step(i, carry):
            zz, yy, xx = i // PLANE, (i // 2) % 2, i % 2
            value = acc[zz, yy, xx] + r0[zz, yy, xx].astype(F32)
            acc[zz, yy, xx] = value
            sb[zz, yy, xx] = value.astype(BF16)
            return carry

        lax.fori_loop(0, n, step, 0)

    def after_first(p):
        acc, _, _, sb, r1 = bufs[p][:5]
        c1(p).wait_recv()
        c1(p).wait_send()

        def step(i, carry):
            zz, kk = i // 2, i % 2
            at = (zz, y, kk) if PARTS[p][3] == 0 else (zz, kk, x)
            value = acc[at] + r1[zz, kk].astype(F32)
            acc[at] = value
            sb[at] = value.astype(BF16)
            return carry

        lax.fori_loop(0, 2 * planes, step, 0)

    def after_second(p):
        acc, _, _, sb, _, r2 = bufs[p][:6]
        c2(p).wait_recv()
        c2(p).wait_send()
        for zz in range(planes):
            value = acc[zz, y, x] + r2[zz].astype(F32)
            acc[zz, y, x] = value
            sb[zz, y, x] = value.astype(BF16)

    def to_planes(p):
        for dest in range(planes):
            @pl.when(dest != z)
            def _():
                c3(p, dest, z).start()

    def results(p):
        a, start, size, _ = PARTS[p]
        acc = bufs[p][0]
        out = gin_ref if a == 0 else gout_ref
        rows = acc.shape[3]
        view = out.at[pl.ds(pl.multiple_of(core * rows, 8), rows), pl.ds(start, size)]
        return (
            remote(acc.at[z, y, x], view, s4s.at[p], s4r.at[p], twin),
            pltpu.make_async_copy(acc.at[z, y, x], view, own.at[p]),
        )

    def finish(p):
        acc, r3 = bufs[p][0], bufs[p][6]
        for source in range(planes):
            @pl.when(source != z)
            def _():
                c3(p, source, source).wait_recv()
                acc[z, y, x] += r3[source].astype(F32)

        for copy in results(p):
            copy.start()

    def igs(i):
        for d in range(1 + SPREAD[i], 1 + SPREAD[i + 1]):
            ig_copy(d).start()

    units = [(0, 1), (2, 3), (4, 5)]
    gl_t[...] = gl_ref[...].T
    for p in units[0]:
        product(p)
    pl.semaphore_wait(barrier, n)
    for p in units[0]:
        c0(p).start()
    for d in range(1, n):
        few_copy(d).start()
    igs(0)
    own_slot = pltpu.make_async_copy(
        ig_ref.at[pl.ds(pl.multiple_of(me * piece, 8), piece)], slot_ref.at[me], own.at[count]
    )
    own_slot.start()
    nl_t[...] = nl_ref[...].T

    def stage(fn, start, u):
        for p in units[u]:
            fn(p)
            if start is not None:
                start(p).start()

    for p in units[1]:
        product(p)
        c0(p).start()
    stage(into_half, c1, 0)
    for p in units[2]:
        product(p)
        c0(p).start()
    stage(into_half, c1, 1)
    igs(1)
    stage(after_first, c2, 0)
    stage(into_half, c1, 2)
    igs(2)
    stage(after_second, None, 0)
    stage(to_planes, None, 0)
    stage(after_first, c2, 1)
    igs(3)
    stage(after_second, None, 1)
    stage(to_planes, None, 1)
    stage(finish, None, 0)
    stage(after_first, c2, 2)
    stage(finish, None, 1)
    few[me] = small_ref[me]
    for d in range(1, n):
        few_copy(d).wait()
    total = few[0]
    for k in range(1, n):
        total = total + few[k]
    few_sib[0] = total
    pair = remote(few_sib.at[0], few_sib.at[1], pair_s, pair_r, twin)
    pair.start()
    stage(after_second, None, 2)
    stage(to_planes, None, 2)
    stage(finish, None, 2)
    pair.wait()
    sum_ref[...] = few_sib[0] + few_sib[1]
    own_slot.wait()
    for d in range(1, n):
        ig_copy(d).wait()
    for p in range(count):
        c0(p).wait_send()
        for dest in range(planes):
            @pl.when(dest != z)
            def _():
                c3(p, dest, z).wait_send()

        far, near = results(p)
        near.wait()
        far.wait()


def run_scatter(n, ig, normed, gp, gate_low, grad_branch, small):
    length, width = ig.shape
    piece = length // n
    planes = n // PLANE
    proj = gp.shape[1]
    inner = gate_low.shape[1]
    vmem = pl.BlockSpec(memory_space=pltpu.VMEM)
    hbm = pl.BlockSpec(memory_space=pl.ANY)
    dma = pltpu.SemaphoreType.DMA
    scratch = []
    for a, _, size, _ in PARTS:
        rows = (width if a == 0 else inner) // n // REP
        full = (planes, 2, 2, rows, size)
        scratch += [
            pltpu.VMEM(full, F32), pltpu.VMEM(full, BF16), pltpu.VMEM(full, BF16), pltpu.VMEM(full, BF16),
            pltpu.VMEM((planes, 2, rows, size), BF16), pltpu.VMEM((planes, rows, size), BF16), pltpu.VMEM((planes, rows, size), BF16),
        ]
    count = len(PARTS)
    few = small.shape[1:]
    scratch += [
        pltpu.VMEM((width, length), BF16), pltpu.VMEM((inner, length), BF16), pltpu.VMEM((n, *few), F32), pltpu.VMEM((2, *few), F32),
        dma((count + 1,)), dma((n,)), dma((n,)), dma((n,)), dma((n,)), dma(()), dma(()),
        *(dma((count,)) for _ in range(6)), dma((count, planes)), dma((count, planes)), dma((count,)), dma((count,)),
    ]
    shapes = [
        ((n, piece, width), BF16), ((width // n, proj), F32), ((inner // n, width), F32), (few, F32),
    ]
    return pl.pallas_call(
        functools.partial(scatter_kernel, n),
        out_shape=[jax.ShapeDtypeStruct(s, d) for s, d in shapes],
        in_specs=[hbm, vmem, vmem, vmem, vmem, vmem],
        out_specs=[hbm, hbm, hbm, vmem],
        scratch_shapes=scratch,
        compiler_params=pltpu.CompilerParams(collective_id=1, has_side_effects=True, vmem_limit_bytes=LIMIT),
    )(ig, normed, gp, gate_low, grad_branch, small)


def on_device(
    tokens, cotangent, lengths, order, norm_weight, in_weight, conv_weight, conv_bias,
    step_bias, decay_log, skip_gain, gate_norm_weight, out_weight,
):
    peers = lax.axis_size("shard")
    rank = lax.axis_index("shard")
    piece, width = tokens.shape[1:]

    def gather(x):
        return lax.all_gather(x, "shard", axis=0, tiled=True)

    def to_sequences(x):
        parts = x.reshape(peers, 1, piece, width)
        return lax.all_to_all(parts, "shard", split_axis=0, concat_axis=2, tiled=True).reshape(peers * piece, width)

    def to_slots(x):
        parts = x.reshape(peers, piece, width)
        return lax.all_to_all(parts, "shard", split_axis=0, concat_axis=0, tiled=True)

    slots = jnp.arange(peers, dtype=jnp.int32)
    sequence = jnp.sum(jnp.where(slots == rank, order[0], 0))
    valid = jnp.sum(jnp.where(slots == sequence, lengths[0], 0))[None]
    direct = peers == PLANE * PLANE and lax.axis_size("rep") == REP and piece % 16 == 0
    if direct:
        def row(v):
            return jnp.pad(v.astype(F32).reshape(-1, v.shape[-1]), ((0, 0), (0, TILE - v.shape[-1])))

        blank = jnp.zeros((EDGE - CONV - 3, TILE), F32)
        small = jnp.concatenate([row(norm_weight), row(conv_weight.T), row(conv_bias), row(gate_norm_weight), blank])
        heads = jnp.concatenate([row(step_bias), row(decay_log), row(skip_gain), jnp.zeros((EDGE - 3, TILE), F32)])
        wide = jnp.pad(in_weight, ((0, 0), (0, -in_weight.shape[1] % (2 * REP * TILE))))
        forward, gathered = run_gather_forward(valid, tokens, cotangent, wide, out_weight, small, heads)
        out, cin, gr, mx, st, sr, normed, gate_low = forward
        tok, cot, in_full, out_full, norm_row, taps_rows, shift_row, skip_row, gate_row = gathered
        params = (in_full, out_full, norm_row, taps_rows, shift_row, heads[0:1], heads[1:2], skip_row, gate_row)
    else:
        tok, cot = to_sequences(tokens), to_sequences(cotangent)
        params = prepare(
            gather(norm_weight), gather(in_weight), gather(conv_weight), gather(conv_bias),
            gather(gate_norm_weight), gather(out_weight), step_bias, decay_log, skip_gain,
        )
        out, cin, gr, mx, st, sr, normed, gate_low = run_forward(valid, tok, params)
    output = to_slots(out)
    ig, gp, gb, taps, gcb, ggn, gsk, gnw, ghd = run_backward(valid, cot, tok, params, (cin, gr, mx, st, sr))
    few = [jnp.sum(gnw, axis=0), jnp.sum(taps, axis=1), jnp.sum(gcb, axis=0), jnp.sum(ggn, axis=0)]
    heads = jnp.stack([
        jnp.sum(ghd[:EDGE], axis=0)[:HEADS], jnp.sum(ghd[EDGE:], axis=0)[:HEADS],
        jnp.sum(gsk.reshape(EDGE, HEADS, HEADDIM), axis=(0, 2)),
    ])
    if direct:
        parts = [jnp.moveaxis(v.reshape(-1, peers, v.shape[-1] // peers), 1, 0) for v in few]
        parts.append(jnp.broadcast_to(heads.reshape(1, 1, -1), (peers, 1, heads.size)))
        few = jnp.concatenate([jnp.pad(v, ((0, 0), (0, 0), (0, TILE - v.shape[2]))) for v in parts], axis=1)
        input_grad, grad_in, grad_out, few = run_scatter(peers, ig, normed, gp, gate_low, gb, few)
        heads = few[EDGE - 1, : heads.size].reshape(heads.shape)
        few = [
            few[0, : norm_weight.size], few[1 : 1 + CONV, : conv_bias.size].T,
            few[1 + CONV, : conv_bias.size], few[2 + CONV, : gate_norm_weight.size],
        ]
    else:
        input_grad = to_slots(ig)

        def scatter(v):
            return lax.psum(lax.psum_scatter(v, "shard", scatter_dimension=0, tiled=True), "rep")

        few[1] = few[1].T
        few = [scatter(v) for v in few]
        grad_in, grad_out = scatter(mul_tn(normed, gp)), scatter(mul_tn(gate_low, gb))
        heads = lax.psum(heads, ("rep", "shard"))
    return (
        output, input_grad, few[0], grad_in, few[1], few[2], heads[0], heads[1], heads[2], few[3], grad_out,
    )


def solution(mesh):
    placed = (
        P("rep", "shard", None), P("rep", "shard", None), P("rep", None), P("rep", None), P("shard"),
        P("shard", None), P("shard", None), P("shard"), P(), P(), P(), P("shard"), P("shard", None),
    )
    outs = (
        P("rep", "shard", None), P("rep", "shard", None), P("shard"), P("shard", None), P("shard", None),
        P("shard"), P(), P(), P(), P("shard"), P("shard", None),
    )
    return jax.shard_map(on_device, mesh=mesh, in_specs=placed, out_specs=outs, check_vma=False)
```

```python
import functools

import jax
import jax.numpy as jnp
from jax import lax
from jax.experimental import pallas as pl
from jax.experimental.pallas import tpu as pltpu
from jax.sharding import PartitionSpec as P

HEADS = 24
HEADDIM = 64
STATE = 128
CONV = 4
SPAN = 256
DI = 1536
XBC = 1792
TILE = 128
PAIRS = DI // TILE
HALF = SPAN // 2
EDGE = 8
epsilon = 1e-05
F32 = jnp.float32
BF16 = jnp.bfloat16
FULL = lax.Precision.HIGHEST


def mul(a, b):
    return jnp.dot(a, b, preferred_element_type=F32)


def mul_nt(a, b):
    return lax.dot_general(a, b, (((1,), (1,)), ((), ())), preferred_element_type=F32)


def mul_tn(a, b):
    return lax.dot_general(a, b, (((0,), (0,)), ((), ())), preferred_element_type=F32)


def sigmoid(v):
    return 0.5 * jnp.tanh(0.5 * v) + 0.5


def softplus(v):
    return jnp.maximum(v, 0.0) + jnp.log1p(jnp.exp(-jnp.abs(v)))


def fold(v):
    return jnp.sum(v.reshape(v.shape[0] // EDGE, EDGE, v.shape[1]), axis=0)


def tile_at(j, base=0):
    return pl.ds(pl.multiple_of(base + j * TILE, TILE), TILE)


def lane_low(shape):
    return lax.broadcasted_iota(jnp.int32, shape, 1) < HEADDIM


def spread(column, h):
    return jnp.broadcast_to(column[:, h : h + 1], (column.shape[0], TILE))


def conv_argument(cin_ref, cw_ref, cb_ref, cols):
    total = cb_ref[:, cols]
    for tap in range(CONV):
        start = EDGE - CONV + 1 + tap
        total = total + cw_ref[tap : tap + 1, cols] * cin_ref[0, start : start + SPAN, cols]
    return total


def head_times(step_raw, step_bias, decay_log):
    shifted = step_raw + step_bias
    step = softplus(shifted)
    log_decay = -jnp.exp(decay_log) * step
    rows = lax.broadcasted_iota(jnp.int32, (SPAN, SPAN), 0)
    columns = lax.broadcasted_iota(jnp.int32, (SPAN, SPAN), 1)
    lower = (rows >= columns).astype(F32)
    cumul = jnp.dot(lower, log_decay, precision=FULL, preferred_element_type=F32)
    return shifted, step, cumul, cumul - jnp.log(step)


def own_length(len_ref, ord_ref):
    return len_ref[0, ord_ref[0, lax.axis_index("shard")]]


def causal_mask(flip):
    rows = lax.broadcasted_iota(jnp.int32, (HALF, HALF), 0)
    columns = lax.broadcasted_iota(jnp.int32, (HALF, HALF), 1)
    return columns >= rows if flip else rows >= columns


def forward_start(w_ref, ws, state, cin_ref):
    ws[...] = jnp.zeros_like(ws)
    ws[:, :HEADS] = w_ref[:, DI + XBC : DI + XBC + HEADS]
    state[...] = jnp.zeros_like(state)
    cin_ref[0, :EDGE, :] = jnp.zeros((EDGE, XBC), F32)


def forward_step(
    block, length, tok_ref, w_ref, ow_ref, nw_ref, cw_ref, cb_ref, sb_ref, dl_ref, sk_ref, gn_ref,
    out_ref, cin_ref, gr_ref, mx_ref, st_ref, sr_ref, nl_ref, gl_ref, ar_ref,
    ws, col_t, pair_s, row_s, state, scores, gated, hook=None,
):
    offset = block * SPAN

    @pl.when(block > 0)
    def _():
        cin_ref[0, :EDGE, :] = gated[:EDGE, :]

    for r in range(0, SPAN, 64):
        tok = tok_ref[r : r + 64, :].astype(F32)
        nrm = lax.rsqrt(jnp.mean(tok * tok, axis=-1, keepdims=True) + epsilon)
        nl_ref[r : r + 64, :] = (tok * nrm * nw_ref[...]).astype(BF16)
    low = nl_ref[...]
    sr_ref[...] = mul(low, ws[...])
    for n in range(0, XBC, 256):
        cin_ref[0, EDGE:, n : n + 256] = mul(low, w_ref[:, DI + n : DI + n + 256])
    for n in range(0, DI, 256):
        gr_ref[:, n : n + 256] = mul(low, w_ref[:, n : n + 256])

    _, _, cumul, shift = head_times(sr_ref[...], sb_ref[...], dl_ref[...])
    row_s[...] = shift.T
    low_lanes = lane_low((SPAN, TILE))
    for h in range(HEADS):
        col_t[h] = spread(cumul, h)
    for j in range(PAIRS):
        pair_s[j] = jnp.where(low_lanes, spread(shift, 2 * j), spread(shift, 2 * j + 1))

    def act(jt):
        cols = tile_at(jt)
        arg = conv_argument(cin_ref, cw_ref, cb_ref, cols)
        ar_ref[:, cols] = arg
        return arg * sigmoid(arg)

    key = act(PAIRS).astype(BF16)
    query = act(PAIRS + 1).astype(BF16)
    key_t = key.astype(F32).T.astype(BF16)
    scores[...] = mul_nt(query, key)
    st_ref[0] = state[...]
    mask = causal_mask(False)

    def pair(j, total):
        cols = tile_at(j)
        if hook is not None:
            hook(j)
        heads_in = act(j)
        heads_low = heads_in.astype(BF16)
        cum0, cum1 = col_t[2 * j], col_t[2 * j + 1]
        cum = jnp.where(low_lanes, cum0, cum1)
        last = cum[SPAN - 1 : SPAN, :]
        old = state[:, cols]
        across = mul(query, old.astype(BF16))
        weighted = (heads_low.astype(F32) * jnp.exp(last - pair_s[j])).astype(BF16)
        state[:, cols] = jnp.exp(last) * old + mul(key_t, weighted)
        zero = jnp.zeros_like(heads_low)
        parts = (jnp.where(low_lanes, heads_low, zero), jnp.where(low_lanes, zero, heads_low))
        top, bottom = [], []
        for h in range(2):
            col = (cum0, cum1)[h]
            row = row_s[pl.ds(2 * j + h, 1), :]
            first = jnp.where(mask, col[:HALF] - row[:, :HALF], -jnp.inf)
            top.append((scores[:HALF, :HALF] * jnp.exp(first)).astype(BF16))
            full = col[HALF:] - row[:, :HALF]
            bottom.append((scores[HALF:, :HALF] * jnp.exp(full)).astype(BF16))
            second = jnp.where(mask, col[HALF:] - row[:, HALF:], -jnp.inf)
            bottom.append((scores[HALF:, HALF:] * jnp.exp(second)).astype(BF16))
        tops = jnp.concatenate([p[:HALF] for p in parts], axis=0)
        within = jnp.concatenate(
            [
                mul(jnp.concatenate(top, axis=1), tops),
                mul(jnp.concatenate(bottom, axis=1), jnp.concatenate(parts, axis=0)),
            ],
            axis=0,
        )
        mixed = within + jnp.exp(cum) * across + sk_ref[:, cols] * heads_in
        mx_ref[:, cols] = mixed
        gate = gr_ref[:, cols]
        value = mixed * (gate * sigmoid(gate))
        gated[:, cols] = value
        return total + value * value

    total = lax.fori_loop(0, PAIRS, pair, jnp.zeros((SPAN, TILE), F32), unroll=3)
    rms = lax.rsqrt(jnp.sum(total, axis=-1, keepdims=True) * (1.0 / DI) + epsilon)

    def finish(j, carry):
        cols = tile_at(j)
        gl_ref[:, cols] = (gated[:, cols] * rms * gn_ref[:, cols]).astype(BF16)
        return carry

    lax.fori_loop(0, PAIRS, finish, 0)
    positions = offset + lax.broadcasted_iota(jnp.int32, (SPAN, 256), 0)
    valid = positions < length
    for n in range(0, tok_ref.shape[1], 256):
        branch = mul(gl_ref[...], ow_ref[:, n : n + 256])
        tok = tok_ref[:, n : n + 256].astype(F32)
        out_ref[:, n : n + 256] = (tok + jnp.where(valid, branch, 0.0)).astype(BF16)
    gated[:EDGE, :] = cin_ref[0, SPAN:, :]


def forward_kernel(
    len_ref, ord_ref, tok_ref, w_ref, ow_ref, nw_ref, cw_ref, cb_ref, sb_ref, dl_ref, sk_ref, gn_ref,
    out_ref, cin_ref, gr_ref, mx_ref, st_ref, sr_ref, nl_ref, gl_ref, ar_ref,
    ws, col_t, pair_s, row_s, state, scores, gated,
):
    block = pl.program_id(0)

    @pl.when(block == 0)
    def _():
        forward_start(w_ref, ws, state, cin_ref)

    forward_step(
        block, own_length(len_ref, ord_ref), tok_ref, w_ref, ow_ref, nw_ref, cw_ref, cb_ref, sb_ref, dl_ref, sk_ref, gn_ref,
        out_ref, cin_ref, gr_ref, mx_ref, st_ref, sr_ref, nl_ref, gl_ref, ar_ref,
        ws, col_t, pair_s, row_s, state, scores, gated,
    )


def backward_kernel(
    peers, len_ref, ord_ref, cot_ref, tok_ref, w_ref, ow_ref, nw_ref, cw_ref, cb_ref, sb_ref, dl_ref, sk_ref, gn_ref,
    cin_ref, gr_ref, mx_ref, st_ref, sr_ref, ar_ref,
    ig_ref, gp_ref, gb_ref, few_ref,
    taps_ref, gcb_ref, ggn_ref, gsk_ref, gnw_ref, ghd_ref,
    ws, col_s, pair_t, row_t, later, scores, grad_scores, gg, sig, gpre, acc_q, acc_k, acc_u, acc_v, acc_l,
):
    step_id = pl.program_id(0)
    count = pl.num_programs(0)
    offset = (count - 1 - step_id) * SPAN

    @pl.when(step_id == 0)
    def _():
        ws[...] = jnp.zeros_like(ws)
        ws[:, :HEADS] = w_ref[:, DI + XBC : DI + XBC + HEADS]
        later[...] = jnp.zeros_like(later)
        gpre[SPAN:, :] = jnp.zeros((EDGE, XBC), F32)
        for ref in (taps_ref, gcb_ref, ggn_ref, gsk_ref, gnw_ref, ghd_ref):
            ref[...] = jnp.zeros_like(ref)

    width = cot_ref.shape[1]
    positions = offset + lax.broadcasted_iota(jnp.int32, (SPAN, width), 0)
    grad_branch = jnp.where(positions < own_length(len_ref, ord_ref), cot_ref[...].astype(F32), 0.0).astype(BF16)
    gb_ref[...] = grad_branch
    for n in range(0, DI, 256):
        gg[:, n : n + 256] = mul_nt(grad_branch, ow_ref[n : n + 256, :])

    shifted, step, cumul, shift = head_times(sr_ref[...], sb_ref[...], dl_ref[...])
    row_t[...] = cumul.T
    low_lanes = lane_low((SPAN, TILE))
    for h in range(HEADS):
        col_s[h] = spread(shift, h)
    for j in range(PAIRS):
        pair_t[j] = jnp.where(low_lanes, spread(cumul, 2 * j), spread(cumul, 2 * j + 1))

    def sums(j, carry):
        squares, crossed = carry
        cols = tile_at(j)
        gate = gr_ref[:, cols]
        part = sigmoid(gate)
        sig[:, cols] = part
        value = mx_ref[:, cols] * (gate * part)
        return squares + value * value, crossed + (gg[:, cols] * gn_ref[:, cols]) * value

    nothing = jnp.zeros((SPAN, TILE), F32)
    squares, crossed = lax.fori_loop(0, PAIRS, sums, (nothing, nothing))
    rms = lax.rsqrt(jnp.sum(squares, axis=-1, keepdims=True) * (1.0 / DI) + epsilon)
    coef = rms * rms * (jnp.sum(crossed, axis=-1, keepdims=True) * (1.0 / DI))
    rms = jnp.broadcast_to(rms, (SPAN, TILE))
    coef = jnp.broadcast_to(coef, (SPAN, TILE))

    def act(jt):
        arg = ar_ref[:, jt * TILE : (jt + 1) * TILE]
        return (arg * sigmoid(arg)).astype(BF16)

    key = act(PAIRS)
    query = act(PAIRS + 1)
    query_t = query.astype(F32).T.astype(BF16)
    scores[...] = mul_nt(key, query)
    grad_scores[...] = jnp.zeros_like(grad_scores)
    for ref in (acc_q, acc_k, acc_u, acc_v, acc_l):
        ref[...] = jnp.zeros_like(ref)
    mask = causal_mask(True)
    lane = lax.broadcasted_iota(jnp.int32, (2 * TILE, TILE), 0) % TILE
    head = lax.broadcasted_iota(jnp.int32, (2 * TILE, TILE), 1)

    def by_head(value, pick):
        high = value.astype(BF16)
        rest = (value - high.astype(F32)).astype(BF16)
        return mul(jnp.concatenate([high, rest], axis=1), pick)

    def pair(j, carry):
        cols = tile_at(j)
        arg = ar_ref[:, cols]
        part_x = sigmoid(arg)
        heads_in = arg * part_x
        heads_low = heads_in.astype(BF16)
        heads_float = heads_low.astype(F32)
        gate, mixed, part, gain, back = (
            gr_ref[:, cols], mx_ref[:, cols], sig[:, cols], gn_ref[:, cols], gg[:, cols]
        )
        silu = gate * part
        value = mixed * silu
        ggn_ref[:, cols] += fold(back * value * rms)
        grad_gated = rms * (back * gain - value * coef)
        grad_scan = grad_gated * silu
        gp_ref[:, cols] = (grad_gated * mixed * (part * (1.0 + gate * (1.0 - part)))).astype(BF16)
        gsk_ref[:, cols] += fold(grad_scan * heads_in)
        cum = pair_t[j]
        growth = jnp.exp(cum)
        last = cum[SPAN - 1 : SPAN, :]
        grad_low = grad_scan.astype(BF16)
        scaled = growth * grad_scan
        grad_across = scaled.astype(BF16)
        col0, col1 = col_s[2 * j], col_s[2 * j + 1]
        carry_weight = jnp.exp(last - jnp.where(low_lanes, col0, col1))
        weighted = (heads_float * carry_weight).astype(BF16)
        after = later[:, cols]
        after_low = after.astype(BF16)
        before = st_ref[0, :, cols]
        before_low = before.astype(BF16)
        across = mul(query, before_low)
        acc_k[...] += mul_nt(weighted, after_low)
        acc_q[...] += mul_nt(grad_across, before_low)
        grow_last = jnp.exp(last)
        carried = mul(key, after_low) * carry_weight
        last_sum = fold(carried * heads_float) + fold(after * before) * grow_last
        later[:, cols] = mul(query_t, grad_across) + grow_last * after
        zero = jnp.zeros_like(grad_low)
        parts = (jnp.where(low_lanes, grad_low, zero), jnp.where(low_lanes, zero, grad_low))
        top, bottom = [], []
        for h in range(2):
            col = (col0, col1)[h]
            row = row_t[pl.ds(2 * j + h, 1), :]
            mixed_top = mul_nt(heads_low[:HALF], parts[h])
            mixed_low = mul_nt(heads_low[HALF:], parts[h][HALF:])
            factor = jnp.exp(jnp.where(mask, row[:, :HALF] - col[:HALF], -jnp.inf))
            top.append((scores[:HALF, :HALF] * factor).astype(BF16))
            grad_scores[:HALF, :HALF] += mixed_top[:, :HALF] * factor
            factor = jnp.exp(row[:, HALF:] - col[:HALF])
            top.append((scores[:HALF, HALF:] * factor).astype(BF16))
            grad_scores[:HALF, HALF:] += mixed_top[:, HALF:] * factor
            factor = jnp.exp(jnp.where(mask, row[:, HALF:] - col[HALF:], -jnp.inf))
            bottom.append((scores[HALF:, HALF:] * factor).astype(BF16))
            grad_scores[HALF:, HALF:] += mixed_low * factor
        lows = jnp.concatenate([p[HALF:] for p in parts], axis=0)
        grad_heads = carried + jnp.concatenate(
            [
                mul(jnp.concatenate(top, axis=1), jnp.concatenate(parts, axis=0)),
                mul(jnp.concatenate(bottom, axis=1), lows),
            ],
            axis=0,
        )
        gain_skip = sk_ref[:, cols]
        spanned = growth * across
        within = mixed - gain_skip * heads_in - spanned
        pick = (head == 2 * j + lane // HEADDIM).astype(F32)
        pick_low = pick.astype(BF16)
        acc_u[...] += by_head(grad_low.astype(F32) * within + grad_scan * spanned, pick_low)
        acc_v[...] += by_head(heads_float * grad_heads, pick_low)
        acc_l[...] += jnp.dot(last_sum, pick[:TILE], precision=FULL, preferred_element_type=F32)
        grad_conv = grad_heads + gain_skip * grad_scan
        gpre[:SPAN, cols] = grad_conv * (part_x * (1.0 + arg * (1.0 - part_x)))
        return carry

    lax.fori_loop(0, PAIRS, pair, 0, unroll=3)

    rows = lax.broadcasted_iota(jnp.int32, (SPAN, SPAN), 0)
    columns = lax.broadcasted_iota(jnp.int32, (SPAN, SPAN), 1)
    upper = (columns >= rows).astype(F32)
    at_end = lax.broadcasted_iota(jnp.int32, (SPAN, TILE), 0) == SPAN - 1
    to_step = acc_v[...]
    ends = jnp.sum(acc_l[...], axis=0, keepdims=True)
    grad_cumul = acc_u[...] - to_step + jnp.where(at_end, ends, 0.0)
    grad_log = jnp.dot(upper, grad_cumul, precision=FULL, preferred_element_type=F32)
    rate = jnp.exp(dl_ref[...])
    safe = jnp.where(step > 0.0, step, 1.0)
    grad_step = jnp.where(step > 0.0, to_step / safe, 0.0)
    grad_raw = (grad_step - rate * grad_log) * sigmoid(shifted)
    ghd_ref[:EDGE, :] += fold(grad_raw)
    ghd_ref[EDGE:, :] -= fold(rate * step * grad_log)
    raw_low = grad_raw.astype(BF16)
    gp_ref[:, DI + XBC :] = raw_low[:, :HEADS]

    scores_low = grad_scores[...].astype(BF16)
    scores_t = grad_scores[...].T.astype(BF16)
    for slot, grad in (
        (0, acc_k[...] + mul(scores_low, query)),
        (1, acc_q[...] + mul(scores_t, key)),
    ):
        arg = ar_ref[:, DI + slot * TILE : DI + (slot + 1) * TILE]
        part = sigmoid(arg)
        gpre[:SPAN, DI + slot * TILE : DI + (slot + 1) * TILE] = grad * (part * (1.0 + arg * (1.0 - part)))

    def through_conv(j, carry):
        cols = tile_at(j)
        here = gpre[:SPAN, cols]
        gcb_ref[:, cols] += fold(here)
        total = jnp.zeros_like(here)
        given = cin_ref[0, EDGE:, cols]
        for tap in range(CONV):
            ahead = CONV - 1 - tap
            later_grad = gpre[ahead : ahead + SPAN, cols]
            taps_ref[tap, :, cols] += fold(given * later_grad)
            total = total + cw_ref[tap : tap + 1, cols] * later_grad
        gp_ref[:, tile_at(j, DI)] = total.astype(BF16)
        return carry

    lax.fori_loop(0, PAIRS + 2, through_conv, 0)
    gpre[SPAN:, :] = gpre[:EDGE, :]

    for n in range(0, width, 256):
        grad = mul_nt(gp_ref[:, : DI + XBC], w_ref[n : n + 256, : DI + XBC])
        gg[:, n : n + 256] = grad + mul_nt(raw_low, ws[n : n + 256, :])
    for r in range(0, SPAN, 64):
        tok = tok_ref[r : r + 64, :].astype(F32)
        nrm = lax.rsqrt(jnp.mean(tok * tok, axis=-1, keepdims=True) + epsilon)
        grad = gg[r : r + 64, :width]
        gnw_ref[...] += fold(grad * tok * nrm)
        value = grad * nw_ref[...]
        centre = jnp.mean(value * tok, axis=-1, keepdims=True) * (nrm * nrm)
        grad_tok = nrm * (value - tok * centre)
        ig_ref[r : r + 64, :] = (cot_ref[r : r + 64, :].astype(F32) + grad_tok).astype(BF16)

    @pl.when(step_id == count - 1)
    def _():
        rows = lax.broadcasted_iota(jnp.int32, (DI, TILE), 0) // HEADDIM
        pick = (lax.broadcasted_iota(jnp.int32, (DI, TILE), 1) == rows + 2 * HEADS).astype(F32)
        skips = jnp.dot(gsk_ref[...], pick, precision=FULL, preferred_element_type=F32)
        heads = ghd_ref[:EDGE, :] + pltpu.roll(ghd_ref[EDGE:, :], HEADS, 1) + skips
        heads = jnp.sum(heads, axis=0, keepdims=True)
        few_ref[...] = jnp.zeros_like(few_ref)
        grads = [jnp.sum(gnw_ref[...], axis=0, keepdims=True)]
        grads += [jnp.sum(taps_ref[tap], axis=0, keepdims=True) for tap in range(CONV)]
        grads += [jnp.sum(ref[...], axis=0, keepdims=True) for ref in (gcb_ref, ggn_ref)]
        for r, grad in enumerate(grads):
            size = grad.shape[1] // peers
            for k in range(peers):
                few_ref[k, r : r + 1, :size] = grad[:, k * size : (k + 1) * size]
        for k in range(peers):
            few_ref[k, EDGE - 1 : EDGE, :] = heads


def split_kernel(sum_ref, *outs):
    rows = [0, 1, 1 + CONV, 2 + CONV] + [EDGE - 1] * 3
    for i, (ref, r) in enumerate(zip(outs, rows)):
        start = max(i - 4, 0) * HEADS
        ref[...] = sum_ref[r : r + ref.shape[0], start : start + ref.shape[1]]


def run_split(total, norm, taps, gate):
    shapes = [(1, norm), (CONV, taps), (1, taps), (1, gate)] + [(1, HEADS)] * 3
    outs = pl.pallas_call(split_kernel, out_shape=[jax.ShapeDtypeStruct(s, F32) for s in shapes])(total)
    return [outs[0][0], outs[1].T, outs[2][0], outs[3][0]], [o[0] for o in outs[4:]]


def whole(shape):
    return pl.BlockSpec(shape, lambda i: (0,) * len(shape), pipeline_mode=pl.Buffered(1))


def rows_of(width, last=None):
    if last is None:
        return pl.BlockSpec((SPAN, width), lambda i: (i, 0))
    return pl.BlockSpec((SPAN, width), lambda i: (last - i, 0))


def params_specs(width, proj):
    return [
        whole((width, proj)), whole((DI, width)), whole((1, width)), whole((CONV, XBC)), whole((1, XBC)),
        whole((1, TILE)), whole((1, TILE)), whole((1, DI)), whole((1, DI)),
    ]


LIMIT = 60 * 2**20
SCALARS = pl.BlockSpec(memory_space=pltpu.SMEM)


def forward_results(length, width):
    count = length // SPAN
    shapes = [
        ((length, width), BF16), ((count, SPAN + EDGE, XBC), F32), ((length, DI), F32), ((length, DI), F32),
        ((count, STATE, DI), F32), ((length, TILE), F32), ((length, width), BF16), ((length, DI), BF16), ((length, XBC), F32),
    ]
    out_specs = [
        rows_of(width), pl.BlockSpec((1, SPAN + EDGE, XBC), lambda i: (i, 0, 0)), rows_of(DI), rows_of(DI),
        pl.BlockSpec((1, STATE, DI), lambda i: (i, 0, 0)), rows_of(TILE), rows_of(width), rows_of(DI), rows_of(XBC),
    ]
    scratch = [
        pltpu.VMEM((width, TILE), BF16), pltpu.VMEM((HEADS, SPAN, TILE), F32), pltpu.VMEM((PAIRS, SPAN, TILE), F32),
        pltpu.VMEM((TILE, SPAN), F32), pltpu.VMEM((STATE, DI), F32), pltpu.VMEM((SPAN, SPAN), F32), pltpu.VMEM((SPAN, XBC), F32),
    ]
    return [jax.ShapeDtypeStruct(s, d) for s, d in shapes], out_specs, scratch


def run_forward(lengths, order, tok, params):
    length, width = tok.shape
    shapes, out_specs, scratch = forward_results(length, width)
    return pl.pallas_call(
        forward_kernel,
        grid=(length // SPAN,),
        out_shape=shapes,
        in_specs=[SCALARS, SCALARS, rows_of(width), *params_specs(width, params[0].shape[1])],
        out_specs=out_specs,
        scratch_shapes=scratch,
        compiler_params=pltpu.CompilerParams(dimension_semantics=("arbitrary",), vmem_limit_bytes=LIMIT),
        cost_estimate=pl.CostEstimate(flops=20 * 10**9, bytes_accessed=60 * 10**6, transcendentals=10**7),
    )(lengths, order, tok, *params)


def run_backward(peers, lengths, order, cot, tok, params, kept):
    length, width = tok.shape
    count = length // SPAN
    proj = DI + XBC + HEADS
    last = count - 1
    shapes = [((length, width), BF16), ((length, proj), BF16), ((length, width), BF16), ((peers, EDGE, TILE), F32)]
    out_specs = [rows_of(width, last), rows_of(proj, last), rows_of(width, last), whole(shapes[3][0])]
    kept_specs = [
        pl.BlockSpec((1, SPAN + EDGE, XBC), lambda i: (last - i, 0, 0)), rows_of(DI, last), rows_of(DI, last),
        pl.BlockSpec((1, STATE, DI), lambda i: (last - i, 0, 0)), rows_of(TILE, last), rows_of(XBC, last),
    ]
    square, wide = pltpu.VMEM((SPAN, SPAN), F32), pltpu.VMEM((SPAN, DI), F32)
    narrow = pltpu.VMEM((SPAN, TILE), F32)
    return pl.pallas_call(
        functools.partial(backward_kernel, peers),
        grid=(count,),
        out_shape=[jax.ShapeDtypeStruct(s, d) for s, d in shapes],
        in_specs=[SCALARS, SCALARS, rows_of(width, last), rows_of(width, last), *params_specs(width, params[0].shape[1]), *kept_specs],
        out_specs=out_specs,
        scratch_shapes=[
            *(pltpu.VMEM(s, F32) for s in ((CONV, EDGE, XBC), (EDGE, XBC), (EDGE, DI), (EDGE, DI), (EDGE, width), (2 * EDGE, TILE))),
            pltpu.VMEM((width, TILE), BF16), pltpu.VMEM((HEADS, SPAN, TILE), F32), pltpu.VMEM((PAIRS, SPAN, TILE), F32),
            pltpu.VMEM((TILE, SPAN), F32), pltpu.VMEM((STATE, DI), F32), square, square, wide, wide,
            pltpu.VMEM((SPAN + EDGE, XBC), F32),
            narrow, narrow, narrow, narrow, pltpu.VMEM((EDGE, TILE), F32),
        ],
        compiler_params=pltpu.CompilerParams(dimension_semantics=("arbitrary",), vmem_limit_bytes=LIMIT),
        cost_estimate=pl.CostEstimate(flops=40 * 10**9, bytes_accessed=60 * 10**6, transcendentals=2 * 10**7),
    )(lengths, order, cot, tok, *params, *kept)


def prepare(norm_full, in_full, conv_full, shift_full, gate_full, out_full, step_bias, decay_log, skip_gain):
    pad = ((0, 0), (0, TILE - HEADS))
    return (
        in_full,
        out_full,
        norm_full.astype(F32)[None],
        conv_full.astype(F32).T,
        shift_full.astype(F32)[None],
        jnp.pad(step_bias[None], pad),
        jnp.pad(decay_log[None], pad),
        jnp.repeat(skip_gain, HEADDIM)[None],
        gate_full.astype(F32)[None],
    )


MESH = pl.DeviceIdType.MESH
PLANE = 4
REP = 2
COT_AT = 1


def lay_out(few, n, nw_ref, cw_ref, cb_ref, gn_ref):
    for ref, row in ((nw_ref, 0), (cw_ref, 1), (cb_ref, 1 + CONV), (gn_ref, 2 + CONV)):
        size = ref.shape[1] // n
        for k in range(n):
            ref[:, k * size : (k + 1) * size] = few[k, row : row + ref.shape[0], :size]


def gather_forward_kernel(n, *refs):
    len_ref, ord_ref, tok_ref, cot_ref, in_ref, ow_ref = refs[:6]
    pieces, (sb_in, dl_in, sk_in) = refs[6:10], refs[10:13]
    blocks = refs[13:22]
    seq_ref, cots_ref, inf_ref, owf_ref, nw_ref, cw_ref, cb_ref, sb_ref, dl_ref, sk_ref, gn_ref = refs[22:33]
    own_scratch = refs[33:40]
    (
        tok_v, w_v, ow_v, small_ref, few, tok_stage, cot_stage, own,
        tok_s, tok_r, tok_fs, tok_fr, tok_l, cot_s, cot_r, cot_fs, cot_fr, cot_l, small_s, small_r, line_s, line_r, plane_s, plane_r, sib_s, sib_r, keep_s,
    ) = refs[40:]
    planes = n // PLANE
    block = pl.program_id(0)
    me = lax.axis_index("shard")
    core = lax.axis_index("rep")
    z, y, x = me // PLANE, (me // 2) % 2, me % 2
    across = me + 1 - 2 * x
    along = me + 2 - 4 * y
    piece = tok_ref.shape[1]
    arrays = ((in_ref, w_v), (ow_ref, ow_v))

    def region(a, k, part=None):
        src, dst = arrays[a]
        half = dst.shape[1] // REP
        first = pl.cdiv(half // TILE, 2) * TILE
        rows = pl.ds(pl.multiple_of(k * src.shape[0], src.shape[0]), src.shape[0])
        start, size = ((0, first), (first, half - first), (0, half))[2 if part is None else part]
        return dst.at[rows, pl.ds(pl.multiple_of(core * half + start, TILE), size)]

    def send(view, to, s, r):
        return pltpu.make_async_remote_copy(
            src_ref=view, dst_ref=view, send_sem=s, recv_sem=r, device_id=to, device_id_type=MESH
        )

    def line(a, origin, to):
        return send(region(a, origin), {"shard": to}, line_s.at[a, origin // PLANE, (to > me).astype(jnp.int32)], line_r.at[a, origin // PLANE])

    def hop(a, zz, kind):
        here = zz * PLANE + 2 * y + x
        side = zz * PLANE + 2 * y + 1 - x
        ahead = zz * PLANE + 2 * (1 - y) + x
        origin, part, to = (
            (here, 0, across), (here, 1, along), (here, 0, along), (here, 1, across), (side, 0, along), (ahead, 1, across),
        )[kind]
        return send(region(a, origin, part), {"shard": to}, plane_s.at[a, zz, kind], plane_r.at[a, zz, kind])

    def sibling(a, zz, kind):
        origin = zz * PLANE + (2 * y + x, 2 * y + 1 - x, 2 * (1 - y) + x, 2 * (1 - y) + 1 - x)[kind]
        return send(region(a, origin), {"rep": 1 - core}, sib_s.at[a, zz, kind], sib_r.at[a, zz, kind])

    def rows(k):
        return pl.ds(pl.multiple_of(k * piece, piece), piece)

    quad = me % PLANE
    moves = (
        (tok_ref, tok_stage, tok_v, tok_s, tok_r, tok_fs, tok_fr, tok_l),
        (cot_ref, cot_stage, cots_ref, cot_s, cot_r, cot_fs, cot_fr, cot_l),
    )

    def stage_copy(m, to, source):
        src, stage, _, ss, sr = moves[m][:5]
        return pltpu.make_async_remote_copy(
            src_ref=src.at[pl.ds(pl.multiple_of(to * PLANE, PLANE), PLANE)], dst_ref=stage.at[source],
            send_sem=ss.at[to], recv_sem=sr.at[source],
            device_id={"shard": to * PLANE + quad}, device_id_type=MESH,
        )

    def own_stage(m):
        src, stage = moves[m][:2]
        return pltpu.make_async_copy(src.at[pl.ds(pl.multiple_of(z * PLANE, PLANE), PLANE)], stage.at[z], moves[m][7].at[planes])

    def pass_copy(m, zz, j, source):
        _, stage, dst, _, _, ss, sr, _ = moves[m]
        return pltpu.make_async_remote_copy(
            src_ref=stage.at[zz, j], dst_ref=dst.at[rows(zz * PLANE + source)],
            send_sem=ss.at[zz, j], recv_sem=sr.at[zz, source],
            device_id={"shard": z * PLANE + j}, device_id_type=MESH,
        )

    def keep_copy(m, zz):
        _, stage, dst = moves[m][:3]
        return pltpu.make_async_copy(stage.at[zz, quad], dst.at[rows(zz * PLANE + quad)], moves[m][7].at[zz])

    def start_stage(m):
        for p in range(planes):
            @pl.when(p != z)
            def _():
                stage_copy(m, p, z).start()

    def pass_on(m, zz):
        @pl.when(zz != z)
        def _():
            stage_copy(m, zz, zz).wait_recv()

        for j in range(PLANE):
            @pl.when(j != quad)
            def _():
                pass_copy(m, zz, j, quad).start()

        keep_copy(m, zz).start()

    def landed(m, zz):
        for j in range(PLANE):
            @pl.when(j != quad)
            def _():
                pass_copy(m, zz, j, j).wait_recv()

        keep_copy(m, zz).wait()

    def gone(m):
        for zz in range(planes):
            @pl.when(zz != z)
            def _():
                stage_copy(m, zz, z).wait_send()

            for j in range(PLANE):
                @pl.when(j != quad)
                def _():
                    pass_copy(m, zz, j, quad).wait_send()

    def small_copy(to, source):
        return pltpu.make_async_remote_copy(
            src_ref=small_ref, dst_ref=few.at[source], send_sem=small_s.at[to], recv_sem=small_r.at[source],
            device_id={"shard": to}, device_id_type=MESH,
        )

    def local_copies():
        src, dst = arrays[1]
        return [
            pltpu.make_async_copy(src, dst.at[pl.ds(pl.multiple_of(me * src.shape[0], 8), src.shape[0])], own.at[1]),
            pltpu.make_async_copy(small_ref, few.at[me], own.at[2]),
            own_stage(0),
            own_stage(1),
        ]

    def saves():
        return [
            pltpu.make_async_copy(w_v, inf_ref, keep_s.at[0]),
            pltpu.make_async_copy(ow_v, owf_ref, keep_s.at[1]),
        ]

    def launch(a, zz):
        for kind in range(4):
            hop(a, zz, kind).start()

    def relay(a, zz):
        hop(a, zz, 0).wait_recv()
        hop(a, zz, 4).start()
        hop(a, zz, 1).wait_recv()
        hop(a, zz, 5).start()

    def collect(a, zz):
        hop(a, zz, 3).wait_recv()
        sibling(a, zz, 1).start()
        hop(a, zz, 2).wait_recv()
        sibling(a, zz, 2).start()
        hop(a, zz, 4).wait_recv()
        hop(a, zz, 5).wait_recv()
        sibling(a, zz, 3).start()

    def each(d, step):
        @pl.when(z - d >= 0)
        def _():
            step(z - d, me - d * PLANE, me + PLANE, z + 1 < planes)

        @pl.when(z + d < planes)
        def _():
            step(z + d, me + d * PLANE, me - PLANE, z > 0)

    def start_line(a):
        @pl.when(z + 1 < planes)
        def _():
            line(a, me, me + PLANE).start()

        @pl.when(z > 0)
        def _():
            line(a, me, me - PLANE).start()

    def arrived(a):
        def step(zz, origin, to, more):
            line(a, origin, to).wait_recv()

            @pl.when(more)
            def _():
                line(a, origin, to).start()

            sibling(a, zz, 0).start()
            launch(a, zz)

        return step

    def send_pieces(copy, first, last):
        for d in range(first, last):
            copy(lax.rem(me + d, n), me).start()

    @pl.when(block == 0)
    def _():
        barrier = pltpu.get_barrier_semaphore()
        for d in range(1, n):
            pl.semaphore_signal(barrier, inc=1, device_id={"shard": lax.rem(me + d, n)}, device_id_type=MESH)
        pl.semaphore_signal(barrier, inc=1, device_id={"rep": 1 - core}, device_id_type=MESH)
        small_ref[...] = jnp.zeros_like(small_ref)
        for row, ref in zip((0, 1, 1 + CONV, 2 + CONV), pieces):
            small_ref[row : row + ref.shape[0], : ref.shape[1]] = ref[...].astype(F32)
        for ref, given in ((sb_ref, sb_in), (dl_ref, dl_in)):
            ref[...] = jnp.zeros_like(ref)
            ref[:, :HEADS] = given[...]
        for h in range(HEADS):
            sk_ref[:, h * HEADDIM : (h + 1) * HEADDIM] = jnp.broadcast_to(sk_in[:, h : h + 1], (1, HEADDIM))
        local = local_copies()
        for copy in local:
            copy.start()
        width = in_ref.shape[1]
        mine = pl.ds(pl.multiple_of(me * in_ref.shape[0], in_ref.shape[0]), in_ref.shape[0])
        w_v[mine, width // TILE * TILE :] = jnp.zeros((in_ref.shape[0], w_v.shape[1] - width // TILE * TILE), BF16)
        w_v[mine, :width] = in_ref[...]
        for copy in local[:1]:
            copy.wait()
        pl.semaphore_wait(barrier, n)
        for a in range(2):
            start_line(a)
        for a in range(2):
            launch(a, z)

        @pl.when(z == 0)
        def _():
            start_stage(0)

        send_pieces(small_copy, 1, n)
        for d in range(1, planes):
            for a in range(2):
                each(d, arrived(a))
                if d == 1:
                    relay(a, z)
                else:
                    each(d - 1, lambda zz, *_: relay(a, zz))

        @pl.when(z > 0)
        def _():
            start_stage(0)

        for a in range(2):
            collect(a, z)
            each(planes - 1, lambda zz, *_: relay(a, zz))
        for a in range(2):
            for d in range(1, planes):
                each(d, lambda zz, *_: collect(a, zz))
        for copy in local[1:]:
            copy.wait()
        for k in range(n):
            @pl.when(me != k)
            def _():
                small_copy(k, k).wait_recv()
        lay_out(few, n, nw_ref, cw_ref, cb_ref, gn_ref)
        for a in range(2):
            for d in range(planes):
                for kind in range(4):
                    if kind > 0:
                        sibling(a, d, kind).wait_recv()
                    else:
                        @pl.when(z != d)
                        def _():
                            sibling(a, d, kind).wait_recv()
        for copy in saves():
            copy.start()
        pass_on(0, 0)
        forward_start(w_v, own_scratch[0], own_scratch[4], blocks[1])

    @pl.when(block + 1 < planes)
    def _():
        pass_on(0, block + 1)

    landed(0, block)

    @pl.when(block == COT_AT)
    def _():
        start_stage(1)

    forward_step(
        block, own_length(len_ref, ord_ref), tok_v.at[pl.ds(pl.multiple_of(block * SPAN, SPAN), SPAN)], w_v, ow_v,
        nw_ref, cw_ref, cb_ref, sb_ref, dl_ref, sk_ref, gn_ref, *blocks, *own_scratch,
    )

    @pl.when(block == pl.num_programs(0) - 1)
    def _():
        keep = pltpu.make_async_copy(tok_v, seq_ref, keep_s.at[2])
        keep.start()
        for copy in saves():
            copy.wait()
        for zz in range(planes):
            pass_on(1, zz)
        for m in range(2):
            gone(m)
        for zz in range(planes):
            landed(1, zz)
        for k in range(n):
            @pl.when(me != k)
            def _():
                small_copy(k, k).wait_send()
        for a in range(2):
            def sent(zz, origin, to, more):
                @pl.when(more)
                def _():
                    line(a, origin, to).wait_send()

            for d in range(1, planes):
                each(d, sent)

            @pl.when(z + 1 < planes)
            def _():
                line(a, me, me + PLANE).wait_send()

            @pl.when(z > 0)
            def _():
                line(a, me, me - PLANE).wait_send()

            for zz in range(planes):
                for kind in range(6):
                    hop(a, zz, kind).wait_send()
                for kind in range(4):
                    if kind > 0:
                        sibling(a, zz, kind).wait_send()
                    else:
                        @pl.when(z != zz)
                        def _():
                            sibling(a, zz, kind).wait_send()
        keep.wait()


def run_gather_forward(lengths, order, tokens, cotangent, in_weight, out_weight, pieces, heads):
    n, piece, width = tokens.shape
    length = n * piece
    planes = n // PLANE
    proj = pl.cdiv(in_weight.shape[1], 2 * REP * TILE) * 2 * REP * TILE
    inner = n * out_weight.shape[0]
    hbm = pl.BlockSpec(memory_space=pl.ANY)
    vmem = pl.BlockSpec(memory_space=pltpu.VMEM)
    dma = pltpu.SemaphoreType.DMA
    shapes, out_specs, scratch = forward_results(length, width)
    rows = [(1, width), (CONV, XBC), (1, XBC), (1, TILE), (1, TILE), (1, DI), (1, DI)]
    more = [((length, width), BF16)] * 2 + [((width, proj), BF16), ((inner, width), BF16)] + [(r, F32) for r in rows]
    results = pl.pallas_call(
        functools.partial(gather_forward_kernel, n),
        grid=(length // SPAN,),
        out_shape=shapes + [jax.ShapeDtypeStruct(s, d) for s, d in more],
        in_specs=[SCALARS, SCALARS, hbm, hbm, vmem, hbm] + [vmem] * 7,
        out_specs=out_specs + [hbm] * 4 + [whole(r) for r in rows],
        scratch_shapes=scratch + [
            pltpu.VMEM((length, width), BF16), pltpu.VMEM((width, proj), BF16), pltpu.VMEM((inner, width), BF16),
            pltpu.VMEM((EDGE, TILE), F32), pltpu.VMEM((n, EDGE, TILE), F32), *(pltpu.VMEM((planes, PLANE, piece, width), BF16) for _ in range(2)), dma((3,)),
            *(dma(d) for _ in range(2) for d in ((planes,), (planes,), (planes, PLANE), (planes, PLANE), (planes + 1,))), dma((n,)), dma((n,)), dma((2, planes, 2)), dma((2, planes)),
            dma((2, planes, 6)), dma((2, planes, 6)), dma((2, planes, 4)), dma((2, planes, 4)), dma((3,)),
        ],
        compiler_params=pltpu.CompilerParams(
            dimension_semantics=("arbitrary",), collective_id=0, has_side_effects=True, vmem_limit_bytes=LIMIT
        ),
    )(lengths, order, tokens, cotangent, in_weight, out_weight, *pieces, *heads)
    return results[:9], results[9:]


PARTS = (
    (1, 0, 384, 0), (1, 384, 384, 1), (0, 0, 768, 0), (0, 768, 768, 1), (0, 1536, 896, 0), (0, 2432, 920, 1),
)
SPREAD = (0, 4, 8, 12, 15)


def scatter_kernel(n, *refs):
    (
        ig_ref, nl_ref, gp_ref, gl_ref, gb_ref, small_ref,
        slot_ref, gin_ref, gout_ref, sum_ref,
    ) = refs[:10]
    refs = refs[10:]
    count = len(PARTS)
    bufs = [refs[i * 7 : (i + 1) * 7] for i in range(count)]
    (
        nl_t, gl_t, few, few_sib, own, ig_s, ig_r, few_s, few_r, pair_s, pair_r, s0s, s0r, s1s, s1r, s2s, s2r, s3s, s3r, s4s, s4r,
    ) = refs[count * 7 :]
    planes = n // PLANE
    me = lax.axis_index("shard")
    core = lax.axis_index("rep")
    z, y, x = me // PLANE, (me // 2) % 2, me % 2
    across = {"shard": me + 1 - 2 * x}
    along = {"shard": me + 2 - 4 * y}
    twin = {"rep": 1 - core}
    piece = slot_ref.shape[1]

    barrier = pltpu.get_barrier_semaphore()
    for d in range(1, n):
        pl.semaphore_signal(barrier, inc=1, device_id={"shard": lax.rem(me + d, n)}, device_id_type=MESH)
    pl.semaphore_signal(barrier, inc=1, device_id=twin, device_id_type=MESH)

    def remote(src, dst, s, r, to):
        return pltpu.make_async_remote_copy(
            src_ref=src, dst_ref=dst, send_sem=s, recv_sem=r, device_id=to, device_id_type=MESH
        )

    def ig_copy(d):
        to = lax.rem(me + d, n)
        src = ig_ref.at[pl.ds(pl.multiple_of(to * piece, 8), piece)]
        return remote(src, slot_ref.at[me], ig_s.at[d], ig_r.at[d], {"shard": to})

    def few_copy(d):
        to = lax.rem(me + d, n)
        return remote(small_ref.at[to], few.at[me], few_s.at[d], few_r.at[d], {"shard": to})

    first = core == 0

    def product(p):
        a, start, size, _ = PARTS[p]
        acc, s0 = bufs[p][0], bufs[p][1]
        left, right = (nl_t, gp_ref) if a == 0 else (gl_t, gb_ref)
        rows = acc.shape[3]
        for c in range(0, size, 256):
            wide = min(256, size - c)
            total = mul(left[...], right[:, start + c : start + c + wide])
            total = total.reshape(planes, 2, 2, 2, rows, wide)
            acc[:, :, :, :, c : c + wide] = jnp.where(first, total[:, :, :, 0], total[:, :, :, 1])
            s0[:, :, :, :, c : c + wide] = jnp.where(first, total[:, :, :, 1], total[:, :, :, 0]).astype(BF16)

    def c0(p):
        return remote(bufs[p][1], bufs[p][2], s0s.at[p], s0r.at[p], twin)

    def c1(p):
        sb, r1 = bufs[p][3], bufs[p][4]
        if PARTS[p][3] == 0:
            return remote(sb.at[:, 1 - y], r1, s1s.at[p], s1r.at[p], along)
        return remote(sb.at[:, :, 1 - x], r1, s1s.at[p], s1r.at[p], across)

    def c2(p):
        sb, r2 = bufs[p][3], bufs[p][5]
        if PARTS[p][3] == 0:
            return remote(sb.at[:, y, 1 - x], r2, s2s.at[p], s2r.at[p], across)
        return remote(sb.at[:, 1 - y, x], r2, s2s.at[p], s2r.at[p], along)

    def c3(p, dest, source):
        sb, r3 = bufs[p][3], bufs[p][6]
        to = {"shard": dest * PLANE + 2 * y + x}
        return remote(sb.at[dest, y, x], r3.at[source], s3s.at[p, dest], s3r.at[p, source], to)

    def into_half(p):
        acc, _, r0, sb = bufs[p][:4]
        c0(p).wait_recv()

        def step(i, carry):
            zz, yy, xx = i // PLANE, (i // 2) % 2, i % 2
            value = acc[zz, yy, xx] + r0[zz, yy, xx].astype(F32)
            acc[zz, yy, xx] = value
            sb[zz, yy, xx] = value.astype(BF16)
            return carry

        lax.fori_loop(0, n, step, 0)

    def after_first(p):
        acc, _, _, sb, r1 = bufs[p][:5]
        c1(p).wait_recv()
        c1(p).wait_send()

        def step(i, carry):
            zz, kk = i // 2, i % 2
            at = (zz, y, kk) if PARTS[p][3] == 0 else (zz, kk, x)
            value = acc[at] + r1[zz, kk].astype(F32)
            acc[at] = value
            sb[at] = value.astype(BF16)
            return carry

        lax.fori_loop(0, 2 * planes, step, 0)

    def after_second(p):
        acc, _, _, sb, _, r2 = bufs[p][:6]
        c2(p).wait_recv()
        c2(p).wait_send()
        for zz in range(planes):
            value = acc[zz, y, x] + r2[zz].astype(F32)
            acc[zz, y, x] = value
            sb[zz, y, x] = value.astype(BF16)

    def to_planes(p):
        for dest in range(planes):
            @pl.when(dest != z)
            def _():
                c3(p, dest, z).start()

    def results(p):
        a, start, size, _ = PARTS[p]
        acc = bufs[p][0]
        out = gin_ref if a == 0 else gout_ref
        rows = acc.shape[3]
        view = out.at[pl.ds(pl.multiple_of(core * rows, 8), rows), pl.ds(start, size)]
        return (
            remote(acc.at[z, y, x], view, s4s.at[p], s4r.at[p], twin),
            pltpu.make_async_copy(acc.at[z, y, x], view, own.at[p]),
        )

    def finish(p):
        acc, r3 = bufs[p][0], bufs[p][6]
        for source in range(planes):
            @pl.when(source != z)
            def _():
                c3(p, source, source).wait_recv()
                acc[z, y, x] += r3[source].astype(F32)

        for copy in results(p):
            copy.start()

    def igs(i):
        for d in range(1 + SPREAD[i], 1 + SPREAD[i + 1]):
            ig_copy(d).start()

    units = [(0, 1), (2, 3), (4, 5)]
    gl_t[...] = gl_ref[...].T
    for p in units[0]:
        product(p)
    pl.semaphore_wait(barrier, n)
    for p in units[0]:
        c0(p).start()
    for d in range(1, n):
        few_copy(d).start()
    igs(0)
    own_slot = pltpu.make_async_copy(
        ig_ref.at[pl.ds(pl.multiple_of(me * piece, 8), piece)], slot_ref.at[me], own.at[count]
    )
    own_slot.start()
    nl_t[...] = nl_ref[...].T

    def stage(fn, start, u):
        for p in units[u]:
            fn(p)
            if start is not None:
                start(p).start()

    for p in units[1]:
        product(p)
        c0(p).start()
    stage(into_half, c1, 0)
    for p in units[2]:
        product(p)
        c0(p).start()
    stage(into_half, c1, 1)
    igs(1)
    stage(after_first, c2, 0)
    stage(into_half, c1, 2)
    igs(2)
    stage(after_second, None, 0)
    stage(to_planes, None, 0)
    stage(after_first, c2, 1)
    igs(3)
    stage(after_second, None, 1)
    stage(to_planes, None, 1)
    stage(finish, None, 0)
    stage(after_first, c2, 2)
    stage(finish, None, 1)
    few[me] = small_ref[me]
    for d in range(1, n):
        few_copy(d).wait()
    total = few[0]
    for k in range(1, n):
        total = total + few[k]
    few_sib[0] = total
    pair = remote(few_sib.at[0], few_sib.at[1], pair_s, pair_r, twin)
    pair.start()
    stage(after_second, None, 2)
    stage(to_planes, None, 2)
    stage(finish, None, 2)
    pair.wait()
    sum_ref[...] = few_sib[0] + few_sib[1]
    own_slot.wait()
    for d in range(1, n):
        ig_copy(d).wait()
    for p in range(count):
        c0(p).wait_send()
        for dest in range(planes):
            @pl.when(dest != z)
            def _():
                c3(p, dest, z).wait_send()

        far, near = results(p)
        near.wait()
        far.wait()


def run_scatter(n, ig, normed, gp, gate_low, grad_branch, small):
    length, width = ig.shape
    piece = length // n
    planes = n // PLANE
    proj = gp.shape[1]
    inner = gate_low.shape[1]
    vmem = pl.BlockSpec(memory_space=pltpu.VMEM)
    hbm = pl.BlockSpec(memory_space=pl.ANY)
    dma = pltpu.SemaphoreType.DMA
    scratch = []
    for a, _, size, _ in PARTS:
        rows = (width if a == 0 else inner) // n // REP
        full = (planes, 2, 2, rows, size)
        scratch += [
            pltpu.VMEM(full, F32), pltpu.VMEM(full, BF16), pltpu.VMEM(full, BF16), pltpu.VMEM(full, BF16),
            pltpu.VMEM((planes, 2, rows, size), BF16), pltpu.VMEM((planes, rows, size), BF16), pltpu.VMEM((planes, rows, size), BF16),
        ]
    count = len(PARTS)
    few = small.shape[1:]
    scratch += [
        pltpu.VMEM((width, length), BF16), pltpu.VMEM((inner, length), BF16), pltpu.VMEM((n, *few), F32), pltpu.VMEM((2, *few), F32),
        dma((count + 1,)), dma((n,)), dma((n,)), dma((n,)), dma((n,)), dma(()), dma(()),
        *(dma((count,)) for _ in range(6)), dma((count, planes)), dma((count, planes)), dma((count,)), dma((count,)),
    ]
    shapes = [
        ((n, piece, width), BF16), ((width // n, proj), F32), ((inner // n, width), F32), (few, F32),
    ]
    return pl.pallas_call(
        functools.partial(scatter_kernel, n),
        out_shape=[jax.ShapeDtypeStruct(s, d) for s, d in shapes],
        in_specs=[hbm, vmem, vmem, vmem, vmem, vmem],
        out_specs=[hbm, hbm, hbm, vmem],
        scratch_shapes=scratch,
        compiler_params=pltpu.CompilerParams(collective_id=1, has_side_effects=True, vmem_limit_bytes=LIMIT),
    )(ig, normed, gp, gate_low, grad_branch, small)


def on_device(
    tokens, cotangent, lengths, order, norm_weight, in_weight, conv_weight, conv_bias,
    step_bias, decay_log, skip_gain, gate_norm_weight, out_weight,
):
    peers = lax.axis_size("shard")
    rank = lax.axis_index("shard")
    piece, width = tokens.shape[1:]

    def gather(x):
        return lax.all_gather(x, "shard", axis=0, tiled=True)

    def to_sequences(x):
        parts = x.reshape(peers, 1, piece, width)
        return lax.all_to_all(parts, "shard", split_axis=0, concat_axis=2, tiled=True).reshape(peers * piece, width)

    def to_slots(x):
        parts = x.reshape(peers, piece, width)
        return lax.all_to_all(parts, "shard", split_axis=0, concat_axis=0, tiled=True)

    direct = peers == PLANE * PLANE and lax.axis_size("rep") == REP and piece % 16 == 0
    if direct:
        pieces = (norm_weight[None], conv_weight.T, conv_bias[None], gate_norm_weight[None])
        heads = (step_bias[None], decay_log[None], skip_gain[None])
        forward, gathered = run_gather_forward(lengths, order, tokens, cotangent, in_weight, out_weight, pieces, heads)
        out, cin, gr, mx, st, sr, normed, gate_low, ar = forward
        tok, cot, params = gathered[0], gathered[1], gathered[2:]
    else:
        tok, cot = to_sequences(tokens), to_sequences(cotangent)
        params = prepare(
            gather(norm_weight), gather(in_weight), gather(conv_weight), gather(conv_bias),
            gather(gate_norm_weight), gather(out_weight), step_bias, decay_log, skip_gain,
        )
        out, cin, gr, mx, st, sr, normed, gate_low, ar = run_forward(lengths, order, tok, params)
    output = to_slots(out)
    ig, gp, gb, few = run_backward(peers, lengths, order, cot, tok, params, (cin, gr, mx, st, sr, ar))
    if direct:
        input_grad, grad_in, grad_out, few = run_scatter(peers, ig, normed, gp, gate_low, gb, few)
    else:
        input_grad = to_slots(ig)

        def scatter(v):
            return lax.psum(lax.psum_scatter(v, "shard", scatter_dimension=0, tiled=True), "rep")

        grad_in, grad_out = scatter(mul_tn(normed, gp)), scatter(mul_tn(gate_low, gb))
        parts = scatter(few[:, : EDGE - 1])
        few = jnp.concatenate([parts[0], lax.psum(few[0, EDGE - 1 :], ("rep", "shard"))])
    few, heads = run_split(few, norm_weight.size, conv_bias.size, gate_norm_weight.size)
    return (
        output, input_grad, few[0], grad_in, few[1], few[2], heads[0], heads[1], heads[2], few[3], grad_out,
    )


def solution(mesh):
    placed = (
        P("rep", "shard", None), P("rep", "shard", None), P("rep", None), P("rep", None), P("shard"),
        P("shard", None), P("shard", None), P("shard"), P(), P(), P(), P("shard"), P("shard", None),
    )
    outs = (
        P("rep", "shard", None), P("rep", "shard", None), P("shard"), P("shard", None), P("shard", None),
        P("shard"), P(), P(), P(), P("shard"), P("shard", None),
    )
    return jax.shard_map(on_device, mesh=mesh, in_specs=placed, out_specs=outs, check_vma=False)
```

```python
import functools

import jax
import jax.numpy as jnp
from jax import lax
from jax.experimental import pallas as pl
from jax.experimental.pallas import tpu as pltpu
from jax.sharding import PartitionSpec as P

HEADS = 24
HEADDIM = 64
STATE = 128
CONV = 4
SPAN = 256
DI = 1536
XBC = 1792
TILE = 128
PAIRS = DI // TILE
HALF = SPAN // 2
EDGE = 8
epsilon = 1e-05
F32 = jnp.float32
BF16 = jnp.bfloat16
FULL = lax.Precision.HIGHEST


def mul(a, b):
    return jnp.dot(a, b, preferred_element_type=F32)


def mul_nt(a, b):
    return lax.dot_general(a, b, (((1,), (1,)), ((), ())), preferred_element_type=F32)


def mul_tn(a, b):
    return lax.dot_general(a, b, (((0,), (0,)), ((), ())), preferred_element_type=F32)


def sigmoid(v):
    return 0.5 * jnp.tanh(0.5 * v) + 0.5


def softplus(v):
    return jnp.maximum(v, 0.0) + jnp.log1p(jnp.exp(-jnp.abs(v)))


def fold(v):
    return jnp.sum(v.reshape(v.shape[0] // EDGE, EDGE, v.shape[1]), axis=0)


def tile_at(j, base=0):
    return pl.ds(pl.multiple_of(base + j * TILE, TILE), TILE)


def lane_low(shape):
    return lax.broadcasted_iota(jnp.int32, shape, 1) < HEADDIM


def spread(column, h):
    return jnp.broadcast_to(column[:, h : h + 1], (column.shape[0], TILE))


def conv_argument(cin_ref, cw_ref, cb_ref, cols):
    total = cb_ref[:, cols]
    for tap in range(CONV):
        start = EDGE - CONV + 1 + tap
        total = total + cw_ref[tap : tap + 1, cols] * cin_ref[0, start : start + SPAN, cols]
    return total


def head_times(step_raw, step_bias, decay_log):
    shifted = step_raw + step_bias
    step = softplus(shifted)
    log_decay = -jnp.exp(decay_log) * step
    rows = lax.broadcasted_iota(jnp.int32, (SPAN, SPAN), 0)
    columns = lax.broadcasted_iota(jnp.int32, (SPAN, SPAN), 1)
    lower = (rows >= columns).astype(F32)
    cumul = jnp.dot(lower, log_decay, precision=FULL, preferred_element_type=F32)
    return shifted, step, cumul, cumul - jnp.log(step)


def own_length(len_ref, ord_ref):
    return len_ref[0, ord_ref[0, lax.axis_index("shard")]]


def causal_mask(flip):
    rows = lax.broadcasted_iota(jnp.int32, (HALF, HALF), 0)
    columns = lax.broadcasted_iota(jnp.int32, (HALF, HALF), 1)
    return columns >= rows if flip else rows >= columns


def forward_start(w_ref, ws, state, cin_ref):
    ws[...] = jnp.zeros_like(ws)
    ws[:, :HEADS] = w_ref[:, DI + XBC : DI + XBC + HEADS]
    state[...] = jnp.zeros_like(state)
    cin_ref[0, :EDGE, :] = jnp.zeros((EDGE, XBC), F32)


def forward_step(
    block, length, tok_ref, w_ref, ow_ref, nw_ref, cw_ref, cb_ref, sb_ref, dl_ref, sk_ref, gn_ref,
    out_ref, cin_ref, gr_ref, mx_ref, st_ref, sr_ref, nl_ref, gt_ref, ar_ref,
    ws, col_t, pair_s, row_s, state, scores, gated, gl_ref, hook=None,
):
    offset = block * SPAN

    @pl.when(block > 0)
    def _():
        cin_ref[0, :EDGE, :] = gated[:EDGE, :]

    for r in range(0, SPAN, 64):
        tok = tok_ref[r : r + 64, :].astype(F32)
        nrm = lax.rsqrt(jnp.mean(tok * tok, axis=-1, keepdims=True) + epsilon)
        nl_ref[r : r + 64, :] = (tok * nrm * nw_ref[...]).astype(BF16)
    low = nl_ref[...]
    sr_ref[...] = mul(low, ws[...])
    for n in range(0, XBC, 256):
        cin_ref[0, EDGE:, n : n + 256] = mul(low, w_ref[:, DI + n : DI + n + 256])
    for n in range(0, DI, 256):
        gr_ref[:, n : n + 256] = mul(low, w_ref[:, n : n + 256])

    _, _, cumul, shift = head_times(sr_ref[...], sb_ref[...], dl_ref[...])
    row_s[...] = shift.T
    low_lanes = lane_low((SPAN, TILE))
    for h in range(HEADS):
        col_t[h] = spread(cumul, h)
    for j in range(PAIRS):
        pair_s[j] = jnp.where(low_lanes, spread(shift, 2 * j), spread(shift, 2 * j + 1))

    def act(jt):
        cols = tile_at(jt)
        arg = conv_argument(cin_ref, cw_ref, cb_ref, cols)
        ar_ref[:, cols] = arg
        return arg * sigmoid(arg)

    key = act(PAIRS).astype(BF16)
    query = act(PAIRS + 1).astype(BF16)
    key_t = key.astype(F32).T.astype(BF16)
    scores[...] = mul_nt(query, key)
    st_ref[0] = state[...]
    mask = causal_mask(False)

    def pair(j, total):
        cols = tile_at(j)
        if hook is not None:
            hook(j)
        heads_in = act(j)
        heads_low = heads_in.astype(BF16)
        cum0, cum1 = col_t[2 * j], col_t[2 * j + 1]
        cum = jnp.where(low_lanes, cum0, cum1)
        last = cum[SPAN - 1 : SPAN, :]
        old = state[:, cols]
        across = mul(query, old.astype(BF16))
        weighted = (heads_low.astype(F32) * jnp.exp(last - pair_s[j])).astype(BF16)
        state[:, cols] = jnp.exp(last) * old + mul(key_t, weighted)
        zero = jnp.zeros_like(heads_low)
        parts = (jnp.where(low_lanes, heads_low, zero), jnp.where(low_lanes, zero, heads_low))
        top, bottom = [], []
        for h in range(2):
            col = (cum0, cum1)[h]
            row = row_s[pl.ds(2 * j + h, 1), :]
            first = jnp.where(mask, col[:HALF] - row[:, :HALF], -jnp.inf)
            top.append((scores[:HALF, :HALF] * jnp.exp(first)).astype(BF16))
            full = col[HALF:] - row[:, :HALF]
            bottom.append((scores[HALF:, :HALF] * jnp.exp(full)).astype(BF16))
            second = jnp.where(mask, col[HALF:] - row[:, HALF:], -jnp.inf)
            bottom.append((scores[HALF:, HALF:] * jnp.exp(second)).astype(BF16))
        tops = jnp.concatenate([p[:HALF] for p in parts], axis=0)
        within = jnp.concatenate(
            [
                mul(jnp.concatenate(top, axis=1), tops),
                mul(jnp.concatenate(bottom, axis=1), jnp.concatenate(parts, axis=0)),
            ],
            axis=0,
        )
        mixed = within + jnp.exp(cum) * across + sk_ref[:, cols] * heads_in
        mx_ref[:, cols] = mixed
        gate = gr_ref[:, cols]
        value = mixed * (gate * sigmoid(gate))
        gated[:, cols] = value
        return total + value * value

    total = lax.fori_loop(0, PAIRS, pair, jnp.zeros((SPAN, TILE), F32), unroll=3)
    rms = lax.rsqrt(jnp.sum(total, axis=-1, keepdims=True) * (1.0 / DI) + epsilon)

    def finish(j, carry):
        cols = tile_at(j)
        gl_ref[:, cols] = (gated[:, cols] * rms * gn_ref[:, cols]).astype(BF16)
        return carry

    lax.fori_loop(0, PAIRS, finish, 0)
    gt_ref[...] = gl_ref[...].T
    positions = offset + lax.broadcasted_iota(jnp.int32, (SPAN, 256), 0)
    valid = positions < length
    for n in range(0, tok_ref.shape[1], 256):
        branch = mul(gl_ref[...], ow_ref[:, n : n + 256])
        tok = tok_ref[:, n : n + 256].astype(F32)
        out_ref[:, n : n + 256] = (tok + jnp.where(valid, branch, 0.0)).astype(BF16)
    gated[:EDGE, :] = cin_ref[0, SPAN:, :]


def forward_kernel(
    len_ref, ord_ref, tok_ref, w_ref, ow_ref, nw_ref, cw_ref, cb_ref, sb_ref, dl_ref, sk_ref, gn_ref,
    out_ref, cin_ref, gr_ref, mx_ref, st_ref, sr_ref, nl_ref, gt_ref, ar_ref,
    ws, col_t, pair_s, row_s, state, scores, gated, gl_ref,
):
    block = pl.program_id(0)

    @pl.when(block == 0)
    def _():
        forward_start(w_ref, ws, state, cin_ref)

    forward_step(
        block, own_length(len_ref, ord_ref), tok_ref, w_ref, ow_ref, nw_ref, cw_ref, cb_ref, sb_ref, dl_ref, sk_ref, gn_ref,
        out_ref, cin_ref, gr_ref, mx_ref, st_ref, sr_ref, nl_ref, gt_ref, ar_ref,
        ws, col_t, pair_s, row_s, state, scores, gated, gl_ref,
    )


def backward_kernel(
    peers, len_ref, ord_ref, cot_ref, tok_ref, w_ref, ow_ref, nw_ref, cw_ref, cb_ref, sb_ref, dl_ref, sk_ref, gn_ref,
    cin_ref, gr_ref, mx_ref, st_ref, sr_ref, ar_ref,
    ig_ref, gp_ref, gb_ref, few_ref,
    taps_ref, gcb_ref, ggn_ref, gsk_ref, gnw_ref, ghd_ref,
    ws, col_s, pair_t, row_t, later, scores, grad_scores, gg, sig, gpre, acc_q, acc_k, acc_u, acc_v, acc_l,
):
    step_id = pl.program_id(0)
    count = pl.num_programs(0)
    offset = (count - 1 - step_id) * SPAN

    @pl.when(step_id == 0)
    def _():
        ws[...] = jnp.zeros_like(ws)
        ws[:, :HEADS] = w_ref[:, DI + XBC : DI + XBC + HEADS]
        later[...] = jnp.zeros_like(later)
        gpre[SPAN:, :] = jnp.zeros((EDGE, XBC), F32)
        for ref in (taps_ref, gcb_ref, ggn_ref, gsk_ref, gnw_ref, ghd_ref):
            ref[...] = jnp.zeros_like(ref)

    width = cot_ref.shape[1]
    positions = offset + lax.broadcasted_iota(jnp.int32, (SPAN, width), 0)
    grad_branch = jnp.where(positions < own_length(len_ref, ord_ref), cot_ref[...].astype(F32), 0.0).astype(BF16)
    gb_ref[...] = grad_branch
    for n in range(0, DI, 256):
        gg[:, n : n + 256] = mul_nt(grad_branch, ow_ref[n : n + 256, :])

    shifted, step, cumul, shift = head_times(sr_ref[...], sb_ref[...], dl_ref[...])
    row_t[...] = cumul.T
    low_lanes = lane_low((SPAN, TILE))
    for h in range(HEADS):
        col_s[h] = spread(shift, h)
    for j in range(PAIRS):
        pair_t[j] = jnp.where(low_lanes, spread(cumul, 2 * j), spread(cumul, 2 * j + 1))

    def sums(j, carry):
        squares, crossed = carry
        cols = tile_at(j)
        gate = gr_ref[:, cols]
        part = sigmoid(gate)
        sig[:, cols] = part
        value = mx_ref[:, cols] * (gate * part)
        return squares + value * value, crossed + (gg[:, cols] * gn_ref[:, cols]) * value

    nothing = jnp.zeros((SPAN, TILE), F32)
    squares, crossed = lax.fori_loop(0, PAIRS, sums, (nothing, nothing))
    rms = lax.rsqrt(jnp.sum(squares, axis=-1, keepdims=True) * (1.0 / DI) + epsilon)
    coef = rms * rms * (jnp.sum(crossed, axis=-1, keepdims=True) * (1.0 / DI))
    rms = jnp.broadcast_to(rms, (SPAN, TILE))
    coef = jnp.broadcast_to(coef, (SPAN, TILE))

    def act(jt):
        arg = ar_ref[:, jt * TILE : (jt + 1) * TILE]
        return (arg * sigmoid(arg)).astype(BF16)

    key = act(PAIRS)
    query = act(PAIRS + 1)
    query_t = query.astype(F32).T.astype(BF16)
    scores[...] = mul_nt(key, query)
    grad_scores[...] = jnp.zeros_like(grad_scores)
    for ref in (acc_q, acc_k, acc_u, acc_v, acc_l):
        ref[...] = jnp.zeros_like(ref)
    mask = causal_mask(True)
    lane = lax.broadcasted_iota(jnp.int32, (2 * TILE, TILE), 0) % TILE
    head = lax.broadcasted_iota(jnp.int32, (2 * TILE, TILE), 1)

    def by_head(value, pick):
        high = value.astype(BF16)
        rest = (value - high.astype(F32)).astype(BF16)
        return mul(jnp.concatenate([high, rest], axis=1), pick)

    def pair(j, carry):
        cols = tile_at(j)
        arg = ar_ref[:, cols]
        part_x = sigmoid(arg)
        heads_in = arg * part_x
        heads_low = heads_in.astype(BF16)
        heads_float = heads_low.astype(F32)
        gate, mixed, part, gain, back = (
            gr_ref[:, cols], mx_ref[:, cols], sig[:, cols], gn_ref[:, cols], gg[:, cols]
        )
        silu = gate * part
        value = mixed * silu
        ggn_ref[:, cols] += fold(back * value * rms)
        grad_gated = rms * (back * gain - value * coef)
        grad_scan = grad_gated * silu
        gp_ref[:, cols] = (grad_gated * mixed * (part * (1.0 + gate * (1.0 - part)))).astype(BF16)
        gsk_ref[:, cols] += fold(grad_scan * heads_in)
        cum = pair_t[j]
        growth = jnp.exp(cum)
        last = cum[SPAN - 1 : SPAN, :]
        grad_low = grad_scan.astype(BF16)
        scaled = growth * grad_scan
        grad_across = scaled.astype(BF16)
        col0, col1 = col_s[2 * j], col_s[2 * j + 1]
        carry_weight = jnp.exp(last - jnp.where(low_lanes, col0, col1))
        weighted = (heads_float * carry_weight).astype(BF16)
        after = later[:, cols]
        after_low = after.astype(BF16)
        before = st_ref[0, :, cols]
        before_low = before.astype(BF16)
        across = mul(query, before_low)
        acc_k[...] += mul_nt(weighted, after_low)
        acc_q[...] += mul_nt(grad_across, before_low)
        grow_last = jnp.exp(last)
        carried = mul(key, after_low) * carry_weight
        last_sum = fold(carried * heads_float) + fold(after * before) * grow_last
        later[:, cols] = mul(query_t, grad_across) + grow_last * after
        zero = jnp.zeros_like(grad_low)
        parts = (jnp.where(low_lanes, grad_low, zero), jnp.where(low_lanes, zero, grad_low))
        top, bottom = [], []
        for h in range(2):
            col = (col0, col1)[h]
            row = row_t[pl.ds(2 * j + h, 1), :]
            mixed_top = mul_nt(heads_low[:HALF], parts[h])
            mixed_low = mul_nt(heads_low[HALF:], parts[h][HALF:])
            factor = jnp.exp(jnp.where(mask, row[:, :HALF] - col[:HALF], -jnp.inf))
            top.append((scores[:HALF, :HALF] * factor).astype(BF16))
            grad_scores[:HALF, :HALF] += mixed_top[:, :HALF] * factor
            factor = jnp.exp(row[:, HALF:] - col[:HALF])
            top.append((scores[:HALF, HALF:] * factor).astype(BF16))
            grad_scores[:HALF, HALF:] += mixed_top[:, HALF:] * factor
            factor = jnp.exp(jnp.where(mask, row[:, HALF:] - col[HALF:], -jnp.inf))
            bottom.append((scores[HALF:, HALF:] * factor).astype(BF16))
            grad_scores[HALF:, HALF:] += mixed_low * factor
        lows = jnp.concatenate([p[HALF:] for p in parts], axis=0)
        grad_heads = carried + jnp.concatenate(
            [
                mul(jnp.concatenate(top, axis=1), jnp.concatenate(parts, axis=0)),
                mul(jnp.concatenate(bottom, axis=1), lows),
            ],
            axis=0,
        )
        gain_skip = sk_ref[:, cols]
        spanned = growth * across
        within = mixed - gain_skip * heads_in - spanned
        pick = (head == 2 * j + lane // HEADDIM).astype(F32)
        pick_low = pick.astype(BF16)
        acc_u[...] += by_head(grad_low.astype(F32) * within + grad_scan * spanned, pick_low)
        acc_v[...] += by_head(heads_float * grad_heads, pick_low)
        acc_l[...] += jnp.dot(last_sum, pick[:TILE], precision=FULL, preferred_element_type=F32)
        grad_conv = grad_heads + gain_skip * grad_scan
        gpre[:SPAN, cols] = grad_conv * (part_x * (1.0 + arg * (1.0 - part_x)))
        return carry

    lax.fori_loop(0, PAIRS, pair, 0, unroll=3)

    rows = lax.broadcasted_iota(jnp.int32, (SPAN, SPAN), 0)
    columns = lax.broadcasted_iota(jnp.int32, (SPAN, SPAN), 1)
    upper = (columns >= rows).astype(F32)
    at_end = lax.broadcasted_iota(jnp.int32, (SPAN, TILE), 0) == SPAN - 1
    to_step = acc_v[...]
    ends = jnp.sum(acc_l[...], axis=0, keepdims=True)
    grad_cumul = acc_u[...] - to_step + jnp.where(at_end, ends, 0.0)
    grad_log = jnp.dot(upper, grad_cumul, precision=FULL, preferred_element_type=F32)
    rate = jnp.exp(dl_ref[...])
    safe = jnp.where(step > 0.0, step, 1.0)
    grad_step = jnp.where(step > 0.0, to_step / safe, 0.0)
    grad_raw = (grad_step - rate * grad_log) * sigmoid(shifted)
    ghd_ref[:EDGE, :] += fold(grad_raw)
    ghd_ref[EDGE:, :] -= fold(rate * step * grad_log)
    raw_low = grad_raw.astype(BF16)
    gp_ref[:, DI + XBC :] = raw_low[:, :HEADS]

    scores_low = grad_scores[...].astype(BF16)
    scores_t = grad_scores[...].T.astype(BF16)
    for slot, grad in (
        (0, acc_k[...] + mul(scores_low, query)),
        (1, acc_q[...] + mul(scores_t, key)),
    ):
        arg = ar_ref[:, DI + slot * TILE : DI + (slot + 1) * TILE]
        part = sigmoid(arg)
        gpre[:SPAN, DI + slot * TILE : DI + (slot + 1) * TILE] = grad * (part * (1.0 + arg * (1.0 - part)))

    def through_conv(j, carry):
        cols = tile_at(j)
        here = gpre[:SPAN, cols]
        gcb_ref[:, cols] += fold(here)
        total = jnp.zeros_like(here)
        given = cin_ref[0, EDGE:, cols]
        for tap in range(CONV):
            ahead = CONV - 1 - tap
            later_grad = gpre[ahead : ahead + SPAN, cols]
            taps_ref[tap, :, cols] += fold(given * later_grad)
            total = total + cw_ref[tap : tap + 1, cols] * later_grad
        gp_ref[:, tile_at(j, DI)] = total.astype(BF16)
        return carry

    lax.fori_loop(0, PAIRS + 2, through_conv, 0)
    gpre[SPAN:, :] = gpre[:EDGE, :]

    for n in range(0, width, 256):
        grad = mul_nt(gp_ref[:, : DI + XBC], w_ref[n : n + 256, : DI + XBC])
        gg[:, n : n + 256] = grad + mul_nt(raw_low, ws[n : n + 256, :])
    for r in range(0, SPAN, 64):
        tok = tok_ref[r : r + 64, :].astype(F32)
        nrm = lax.rsqrt(jnp.mean(tok * tok, axis=-1, keepdims=True) + epsilon)
        grad = gg[r : r + 64, :width]
        gnw_ref[...] += fold(grad * tok * nrm)
        value = grad * nw_ref[...]
        centre = jnp.mean(value * tok, axis=-1, keepdims=True) * (nrm * nrm)
        grad_tok = nrm * (value - tok * centre)
        ig_ref[r : r + 64, :] = (cot_ref[r : r + 64, :].astype(F32) + grad_tok).astype(BF16)

    @pl.when(step_id == count - 1)
    def _():
        rows = lax.broadcasted_iota(jnp.int32, (DI, TILE), 0) // HEADDIM
        pick = (lax.broadcasted_iota(jnp.int32, (DI, TILE), 1) == rows + 2 * HEADS).astype(F32)
        skips = jnp.dot(gsk_ref[...], pick, precision=FULL, preferred_element_type=F32)
        heads = ghd_ref[:EDGE, :] + pltpu.roll(ghd_ref[EDGE:, :], HEADS, 1) + skips
        heads = jnp.sum(heads, axis=0, keepdims=True)
        few_ref[...] = jnp.zeros_like(few_ref)
        grads = [jnp.sum(gnw_ref[...], axis=0, keepdims=True)]
        grads += [jnp.sum(taps_ref[tap], axis=0, keepdims=True) for tap in range(CONV)]
        grads += [jnp.sum(ref[...], axis=0, keepdims=True) for ref in (gcb_ref, ggn_ref)]
        for r, grad in enumerate(grads):
            size = grad.shape[1] // peers
            for k in range(peers):
                few_ref[k, r : r + 1, :size] = grad[:, k * size : (k + 1) * size]
        for k in range(peers):
            few_ref[k, EDGE - 1 : EDGE, :] = heads


def split_kernel(sum_ref, *outs):
    rows = [0, 1, 1 + CONV, 2 + CONV] + [EDGE - 1] * 3
    for i, (ref, r) in enumerate(zip(outs, rows)):
        start = max(i - 4, 0) * HEADS
        ref[...] = sum_ref[r : r + ref.shape[0], start : start + ref.shape[1]]


def run_split(total, norm, taps, gate):
    shapes = [(1, norm), (CONV, taps), (1, taps), (1, gate)] + [(1, HEADS)] * 3
    outs = pl.pallas_call(split_kernel, out_shape=[jax.ShapeDtypeStruct(s, F32) for s in shapes])(total)
    return [outs[0][0], outs[1].T, outs[2][0], outs[3][0]], [o[0] for o in outs[4:]]


def whole(shape):
    return pl.BlockSpec(shape, lambda i: (0,) * len(shape), pipeline_mode=pl.Buffered(1))


def rows_of(width, last=None):
    if last is None:
        return pl.BlockSpec((SPAN, width), lambda i: (i, 0))
    return pl.BlockSpec((SPAN, width), lambda i: (last - i, 0))


def params_specs(width, proj):
    return [
        whole((width, proj)), whole((DI, width)), whole((1, width)), whole((CONV, XBC)), whole((1, XBC)),
        whole((1, TILE)), whole((1, TILE)), whole((1, DI)), whole((1, DI)),
    ]


LIMIT = 60 * 2**20
SCALARS = pl.BlockSpec(memory_space=pltpu.SMEM)


def forward_results(length, width):
    count = length // SPAN
    shapes = [
        ((length, width), BF16), ((count, SPAN + EDGE, XBC), F32), ((length, DI), F32), ((length, DI), F32),
        ((count, STATE, DI), F32), ((length, TILE), F32), ((length, width), BF16), ((DI, length), BF16), ((length, XBC), F32),
    ]
    out_specs = [
        rows_of(width), pl.BlockSpec((1, SPAN + EDGE, XBC), lambda i: (i, 0, 0)), rows_of(DI), rows_of(DI),
        pl.BlockSpec((1, STATE, DI), lambda i: (i, 0, 0)), rows_of(TILE), rows_of(width), pl.BlockSpec((DI, SPAN), lambda i: (0, i)), rows_of(XBC),
    ]
    scratch = [
        pltpu.VMEM((width, TILE), BF16), pltpu.VMEM((HEADS, SPAN, TILE), F32), pltpu.VMEM((PAIRS, SPAN, TILE), F32),
        pltpu.VMEM((TILE, SPAN), F32), pltpu.VMEM((STATE, DI), F32), pltpu.VMEM((SPAN, SPAN), F32), pltpu.VMEM((SPAN, XBC), F32), pltpu.VMEM((SPAN, DI), BF16),
    ]
    return [jax.ShapeDtypeStruct(s, d) for s, d in shapes], out_specs, scratch


def run_forward(lengths, order, tok, params):
    length, width = tok.shape
    shapes, out_specs, scratch = forward_results(length, width)
    return pl.pallas_call(
        forward_kernel,
        grid=(length // SPAN,),
        out_shape=shapes,
        in_specs=[SCALARS, SCALARS, rows_of(width), *params_specs(width, params[0].shape[1])],
        out_specs=out_specs,
        scratch_shapes=scratch,
        compiler_params=pltpu.CompilerParams(dimension_semantics=("arbitrary",), vmem_limit_bytes=LIMIT),
        cost_estimate=pl.CostEstimate(flops=20 * 10**9, bytes_accessed=60 * 10**6, transcendentals=10**7),
    )(lengths, order, tok, *params)


def backward_scratch(width):
    square, wide = pltpu.VMEM((SPAN, SPAN), F32), pltpu.VMEM((SPAN, DI), F32)
    narrow = pltpu.VMEM((SPAN, TILE), F32)
    return [
        *(pltpu.VMEM(s, F32) for s in ((CONV, EDGE, XBC), (EDGE, XBC), (EDGE, DI), (EDGE, DI), (EDGE, width), (2 * EDGE, TILE))),
        pltpu.VMEM((width, TILE), BF16), pltpu.VMEM((HEADS, SPAN, TILE), F32), pltpu.VMEM((PAIRS, SPAN, TILE), F32),
        pltpu.VMEM((TILE, SPAN), F32), pltpu.VMEM((STATE, DI), F32), square, square, wide, wide,
        pltpu.VMEM((SPAN + EDGE, XBC), F32),
        narrow, narrow, narrow, narrow, pltpu.VMEM((EDGE, TILE), F32),
    ]


def kept_blocks(last):
    return [
        pl.BlockSpec((1, SPAN + EDGE, XBC), lambda i: (last - i, 0, 0)), rows_of(DI, last), rows_of(DI, last),
        pl.BlockSpec((1, STATE, DI), lambda i: (last - i, 0, 0)), rows_of(TILE, last), rows_of(XBC, last),
    ]


def run_backward(peers, lengths, order, cot, tok, params, kept):
    length, width = tok.shape
    count = length // SPAN
    proj = DI + XBC + HEADS
    last = count - 1
    shapes = [((length, width), BF16), ((length, proj), BF16), ((length, width), BF16), ((peers, EDGE, TILE), F32)]
    out_specs = [rows_of(width, last), rows_of(proj, last), rows_of(width, last), whole(shapes[3][0])]
    kept_specs = kept_blocks(last)
    return pl.pallas_call(
        functools.partial(backward_kernel, peers),
        grid=(count,),
        out_shape=[jax.ShapeDtypeStruct(s, d) for s, d in shapes],
        in_specs=[SCALARS, SCALARS, rows_of(width, last), rows_of(width, last), *params_specs(width, params[0].shape[1]), *kept_specs],
        out_specs=out_specs,
        scratch_shapes=backward_scratch(width),
        compiler_params=pltpu.CompilerParams(dimension_semantics=("arbitrary",), vmem_limit_bytes=LIMIT),
        cost_estimate=pl.CostEstimate(flops=40 * 10**9, bytes_accessed=60 * 10**6, transcendentals=2 * 10**7),
    )(lengths, order, cot, tok, *params, *kept)


def prepare(norm_full, in_full, conv_full, shift_full, gate_full, out_full, step_bias, decay_log, skip_gain):
    pad = ((0, 0), (0, TILE - HEADS))
    return (
        in_full,
        out_full,
        norm_full.astype(F32)[None],
        conv_full.astype(F32).T,
        shift_full.astype(F32)[None],
        jnp.pad(step_bias[None], pad),
        jnp.pad(decay_log[None], pad),
        jnp.repeat(skip_gain, HEADDIM)[None],
        gate_full.astype(F32)[None],
    )


MESH = pl.DeviceIdType.MESH
PLANE = 4
REP = 2
COT_AT = 1


def lay_out(few, n, nw_ref, cw_ref, cb_ref, gn_ref):
    for ref, row in ((nw_ref, 0), (cw_ref, 1), (cb_ref, 1 + CONV), (gn_ref, 2 + CONV)):
        size = ref.shape[1] // n
        for k in range(n):
            ref[:, k * size : (k + 1) * size] = few[k, row : row + ref.shape[0], :size]


def gather_forward_kernel(n, *refs):
    len_ref, ord_ref, tok_ref, cot_ref, in_ref, ow_ref = refs[:6]
    pieces, (sb_in, dl_in, sk_in) = refs[6:10], refs[10:13]
    blocks = refs[13:22]
    seq_ref, cots_ref, inf_ref, owf_ref, nw_ref, cw_ref, cb_ref, sb_ref, dl_ref, sk_ref, gn_ref = refs[22:33]
    own_scratch = refs[33:41]
    (
        tok_v, w_v, ow_v, small_ref, few, tok_stage, own,
        tok_s, tok_r, tok_fs, tok_fr, tok_l, cot_s, cot_r, small_s, small_r, line_s, line_r, plane_s, plane_r, sib_s, sib_r, keep_s,
    ) = refs[41:]
    planes = n // PLANE
    block = pl.program_id(0)
    me = lax.axis_index("shard")
    core = lax.axis_index("rep")
    z, y, x = me // PLANE, (me // 2) % 2, me % 2
    across = me + 1 - 2 * x
    along = me + 2 - 4 * y
    piece = tok_ref.shape[1]
    arrays = ((in_ref, w_v), (ow_ref, ow_v))

    def region(a, k, part=None):
        src, dst = arrays[a]
        half = dst.shape[1] // REP
        first = pl.cdiv(half // TILE, 2) * TILE
        rows = pl.ds(pl.multiple_of(k * src.shape[0], src.shape[0]), src.shape[0])
        start, size = ((0, first), (first, half - first), (0, half))[2 if part is None else part]
        return dst.at[rows, pl.ds(pl.multiple_of(core * half + start, TILE), size)]

    def send(view, to, s, r):
        return pltpu.make_async_remote_copy(
            src_ref=view, dst_ref=view, send_sem=s, recv_sem=r, device_id=to, device_id_type=MESH
        )

    def line(a, origin, to):
        return send(region(a, origin), {"shard": to}, line_s.at[a, origin // PLANE, (to > me).astype(jnp.int32)], line_r.at[a, origin // PLANE])

    def hop(a, zz, kind):
        here = zz * PLANE + 2 * y + x
        side = zz * PLANE + 2 * y + 1 - x
        ahead = zz * PLANE + 2 * (1 - y) + x
        origin, part, to = (
            (here, 0, across), (here, 1, along), (here, 0, along), (here, 1, across), (side, 0, along), (ahead, 1, across),
        )[kind]
        return send(region(a, origin, part), {"shard": to}, plane_s.at[a, zz, kind], plane_r.at[a, zz, kind])

    def sibling(a, zz, kind):
        origin = zz * PLANE + (2 * y + x, 2 * y + 1 - x, 2 * (1 - y) + x, 2 * (1 - y) + 1 - x)[kind]
        return send(region(a, origin), {"rep": 1 - core}, sib_s.at[a, zz, kind], sib_r.at[a, zz, kind])

    def rows(k):
        return pl.ds(pl.multiple_of(k * piece, piece), piece)

    quad = me % PLANE
    moves = (
        (tok_ref, tok_stage, tok_v, tok_s, tok_r, tok_fs, tok_fr, tok_l),
    )

    def stage_copy(m, to, source):
        src, stage, _, ss, sr = moves[m][:5]
        return pltpu.make_async_remote_copy(
            src_ref=src.at[pl.ds(pl.multiple_of(to * PLANE, PLANE), PLANE)], dst_ref=stage.at[source],
            send_sem=ss.at[to], recv_sem=sr.at[source],
            device_id={"shard": to * PLANE + quad}, device_id_type=MESH,
        )

    def own_stage(m):
        src, stage = moves[m][:2]
        return pltpu.make_async_copy(src.at[pl.ds(pl.multiple_of(z * PLANE, PLANE), PLANE)], stage.at[z], moves[m][7].at[planes])

    def pass_copy(m, zz, j, source):
        _, stage, dst, _, _, ss, sr, _ = moves[m]
        return pltpu.make_async_remote_copy(
            src_ref=stage.at[zz, j], dst_ref=dst.at[rows(zz * PLANE + source)],
            send_sem=ss.at[zz, j], recv_sem=sr.at[zz, source],
            device_id={"shard": z * PLANE + j}, device_id_type=MESH,
        )

    def keep_copy(m, zz):
        _, stage, dst = moves[m][:3]
        return pltpu.make_async_copy(stage.at[zz, quad], dst.at[rows(zz * PLANE + quad)], moves[m][7].at[zz])

    def start_stage(m):
        for p in range(planes):
            @pl.when(p != z)
            def _():
                stage_copy(m, p, z).start()

    def pass_on(m, zz):
        @pl.when(zz != z)
        def _():
            stage_copy(m, zz, zz).wait_recv()

        for j in range(PLANE):
            @pl.when(j != quad)
            def _():
                pass_copy(m, zz, j, quad).start()

        keep_copy(m, zz).start()

    def landed(m, zz):
        for j in range(PLANE):
            @pl.when(j != quad)
            def _():
                pass_copy(m, zz, j, j).wait_recv()

        keep_copy(m, zz).wait()

    def gone(m):
        for zz in range(planes):
            @pl.when(zz != z)
            def _():
                stage_copy(m, zz, z).wait_send()

            for j in range(PLANE):
                @pl.when(j != quad)
                def _():
                    pass_copy(m, zz, j, quad).wait_send()

    def cot_copy(to, source):
        return pltpu.make_async_remote_copy(
            src_ref=cot_ref.at[to], dst_ref=cots_ref.at[rows(source)], send_sem=cot_s.at[to], recv_sem=cot_r.at[source],
            device_id={"shard": to}, device_id_type=MESH,
        )

    def small_copy(to, source):
        return pltpu.make_async_remote_copy(
            src_ref=small_ref, dst_ref=few.at[source], send_sem=small_s.at[to], recv_sem=small_r.at[source],
            device_id={"shard": to}, device_id_type=MESH,
        )

    def local_copies():
        src, dst = arrays[1]
        return [
            pltpu.make_async_copy(src, dst.at[pl.ds(pl.multiple_of(me * src.shape[0], 8), src.shape[0])], own.at[1]),
            pltpu.make_async_copy(small_ref, few.at[me], own.at[2]),
            own_stage(0),
            pltpu.make_async_copy(cot_ref.at[me], cots_ref.at[rows(me)], own.at[0]),
        ]

    def saves():
        return [
            pltpu.make_async_copy(w_v, inf_ref, keep_s.at[0]),
            pltpu.make_async_copy(ow_v, owf_ref, keep_s.at[1]),
        ]

    def launch(a, zz):
        for kind in range(4):
            hop(a, zz, kind).start()

    def relay(a, zz):
        hop(a, zz, 0).wait_recv()
        hop(a, zz, 4).start()
        hop(a, zz, 1).wait_recv()
        hop(a, zz, 5).start()

    def collect(a, zz):
        hop(a, zz, 3).wait_recv()
        sibling(a, zz, 1).start()
        hop(a, zz, 2).wait_recv()
        sibling(a, zz, 2).start()
        hop(a, zz, 4).wait_recv()
        hop(a, zz, 5).wait_recv()
        sibling(a, zz, 3).start()

    def each(d, step):
        @pl.when(z - d >= 0)
        def _():
            step(z - d, me - d * PLANE, me + PLANE, z + 1 < planes)

        @pl.when(z + d < planes)
        def _():
            step(z + d, me + d * PLANE, me - PLANE, z > 0)

    def start_line(a):
        @pl.when(z + 1 < planes)
        def _():
            line(a, me, me + PLANE).start()

        @pl.when(z > 0)
        def _():
            line(a, me, me - PLANE).start()

    def arrived(a):
        def step(zz, origin, to, more):
            line(a, origin, to).wait_recv()

            @pl.when(more)
            def _():
                line(a, origin, to).start()

            sibling(a, zz, 0).start()
            launch(a, zz)

        return step

    def send_pieces(copy, first, last):
        for d in range(first, last):
            copy(lax.rem(me + d, n), me).start()

    @pl.when(block == 0)
    def _():
        barrier = pltpu.get_barrier_semaphore()
        for d in range(1, n):
            pl.semaphore_signal(barrier, inc=1, device_id={"shard": lax.rem(me + d, n)}, device_id_type=MESH)
        pl.semaphore_signal(barrier, inc=1, device_id={"rep": 1 - core}, device_id_type=MESH)
        small_ref[...] = jnp.zeros_like(small_ref)
        for row, ref in zip((0, 1, 1 + CONV, 2 + CONV), pieces):
            small_ref[row : row + ref.shape[0], : ref.shape[1]] = ref[...].astype(F32)
        for ref, given in ((sb_ref, sb_in), (dl_ref, dl_in)):
            ref[...] = jnp.zeros_like(ref)
            ref[:, :HEADS] = given[...]
        for h in range(HEADS):
            sk_ref[:, h * HEADDIM : (h + 1) * HEADDIM] = jnp.broadcast_to(sk_in[:, h : h + 1], (1, HEADDIM))
        local = local_copies()
        for copy in local:
            copy.start()
        width = in_ref.shape[1]
        mine = pl.ds(pl.multiple_of(me * in_ref.shape[0], in_ref.shape[0]), in_ref.shape[0])
        w_v[mine, width // TILE * TILE :] = jnp.zeros((in_ref.shape[0], w_v.shape[1] - width // TILE * TILE), BF16)
        w_v[mine, :width] = in_ref[...]
        for copy in local[:1]:
            copy.wait()
        pl.semaphore_wait(barrier, n)
        for a in range(2):
            start_line(a)
        for a in range(2):
            launch(a, z)

        @pl.when(z == 0)
        def _():
            start_stage(0)

        send_pieces(small_copy, 1, n)
        for d in range(1, planes):
            for a in range(2):
                each(d, arrived(a))
                if d == 1:
                    relay(a, z)
                else:
                    each(d - 1, lambda zz, *_: relay(a, zz))

        @pl.when(z > 0)
        def _():
            start_stage(0)

        for a in range(2):
            collect(a, z)
            each(planes - 1, lambda zz, *_: relay(a, zz))
        for a in range(2):
            for d in range(1, planes):
                each(d, lambda zz, *_: collect(a, zz))
        for copy in local[1:]:
            copy.wait()
        for k in range(n):
            @pl.when(me != k)
            def _():
                small_copy(k, k).wait_recv()
        lay_out(few, n, nw_ref, cw_ref, cb_ref, gn_ref)
        for a in range(2):
            for d in range(planes):
                for kind in range(4):
                    if kind > 0:
                        sibling(a, d, kind).wait_recv()
                    else:
                        @pl.when(z != d)
                        def _():
                            sibling(a, d, kind).wait_recv()
        for copy in saves():
            copy.start()
        pass_on(0, 0)
        forward_start(w_v, own_scratch[0], own_scratch[4], blocks[1])

    @pl.when(block + 1 < planes)
    def _():
        pass_on(0, block + 1)

    landed(0, block)

    @pl.when(block == COT_AT)
    def _():
        send_pieces(cot_copy, 1, n)

    forward_step(
        block, own_length(len_ref, ord_ref), tok_v.at[pl.ds(pl.multiple_of(block * SPAN, SPAN), SPAN)], w_v, ow_v,
        nw_ref, cw_ref, cb_ref, sb_ref, dl_ref, sk_ref, gn_ref, *blocks, *own_scratch,
    )

    @pl.when(block == pl.num_programs(0) - 1)
    def _():
        keep = pltpu.make_async_copy(tok_v, seq_ref, keep_s.at[2])
        keep.start()
        for copy in saves():
            copy.wait()
        gone(0)
        for k in range(n):
            @pl.when(me != k)
            def _():
                small_copy(k, k).wait_send()
                cot_copy(k, k).wait()
        for a in range(2):
            def sent(zz, origin, to, more):
                @pl.when(more)
                def _():
                    line(a, origin, to).wait_send()

            for d in range(1, planes):
                each(d, sent)

            @pl.when(z + 1 < planes)
            def _():
                line(a, me, me + PLANE).wait_send()

            @pl.when(z > 0)
            def _():
                line(a, me, me - PLANE).wait_send()

            for zz in range(planes):
                for kind in range(6):
                    hop(a, zz, kind).wait_send()
                for kind in range(4):
                    if kind > 0:
                        sibling(a, zz, kind).wait_send()
                    else:
                        @pl.when(z != zz)
                        def _():
                            sibling(a, zz, kind).wait_send()
        keep.wait()


def run_gather_forward(lengths, order, tokens, cotangent, in_weight, out_weight, pieces, heads):
    n, piece, width = tokens.shape
    length = n * piece
    planes = n // PLANE
    proj = pl.cdiv(in_weight.shape[1], 2 * REP * TILE) * 2 * REP * TILE
    inner = n * out_weight.shape[0]
    hbm = pl.BlockSpec(memory_space=pl.ANY)
    vmem = pl.BlockSpec(memory_space=pltpu.VMEM)
    dma = pltpu.SemaphoreType.DMA
    shapes, out_specs, scratch = forward_results(length, width)
    rows = [(1, width), (CONV, XBC), (1, XBC), (1, TILE), (1, TILE), (1, DI), (1, DI)]
    more = [((length, width), BF16)] * 2 + [((width, proj), BF16), ((inner, width), BF16)] + [(r, F32) for r in rows]
    results = pl.pallas_call(
        functools.partial(gather_forward_kernel, n),
        grid=(length // SPAN,),
        out_shape=shapes + [jax.ShapeDtypeStruct(s, d) for s, d in more],
        in_specs=[SCALARS, SCALARS, hbm, hbm, vmem, hbm] + [vmem] * 7,
        out_specs=out_specs + [hbm] * 4 + [whole(r) for r in rows],
        scratch_shapes=scratch + [
            pltpu.VMEM((length, width), BF16), pltpu.VMEM((width, proj), BF16), pltpu.VMEM((inner, width), BF16),
            pltpu.VMEM((EDGE, TILE), F32), pltpu.VMEM((n, EDGE, TILE), F32), pltpu.VMEM((planes, PLANE, piece, width), BF16), dma((3,)),
            *(dma(d) for d in ((planes,), (planes,), (planes, PLANE), (planes, PLANE), (planes + 1,))), *(dma((n,)) for _ in range(4)), dma((2, planes, 2)), dma((2, planes)),
            dma((2, planes, 6)), dma((2, planes, 6)), dma((2, planes, 4)), dma((2, planes, 4)), dma((3,)),
        ],
        compiler_params=pltpu.CompilerParams(
            dimension_semantics=("arbitrary",), collective_id=0, has_side_effects=True, vmem_limit_bytes=LIMIT
        ),
    )(lengths, order, tokens, cotangent, in_weight, out_weight, *pieces, *heads)
    return results[:9], results[9:]


OUT_PARTS = ((1, 0, 384, 0), (1, 384, 384, 1))
IN_PARTS = ((0, 0, 768, 0), (0, 768, 768, 1), (0, 1536, 896, 0), (0, 2432, 920, 1))


SPREAD = (1, 6, 11, 16, 16)


def remote(src, dst, s, r, to):
    return pltpu.make_async_remote_copy(src_ref=src, dst_ref=dst, send_sem=s, recv_sem=r, device_id=to, device_id_type=MESH)


class Reduction:
    def __init__(self, n, parts, out, refs):
        self.n, self.parts, self.out = n, parts, out
        count = len(parts)
        self.bufs = [refs[i * 7 : (i + 1) * 7] for i in range(count)]
        self.sems = refs[count * 7 :]
        self.planes = n // PLANE
        me = lax.axis_index("shard")
        self.core = lax.axis_index("rep")
        self.z, self.y, self.x = me // PLANE, (me // 2) % 2, me % 2
        self.across = {"shard": me + 1 - 2 * self.x}
        self.along = {"shard": me + 2 - 4 * self.y}
        self.twin = {"rep": 1 - self.core}

    @staticmethod
    def scratch(n, parts, rows):
        planes, count, dma = n // PLANE, len(parts), pltpu.SemaphoreType.DMA
        out = []
        for _, _, size, _ in parts:
            full = (planes, 2, 2, rows, size)
            out += [
                pltpu.VMEM(full, F32), pltpu.VMEM(full, BF16), pltpu.VMEM(full, BF16), pltpu.VMEM(full, BF16),
                pltpu.VMEM((planes, 2, rows, size), BF16), pltpu.VMEM((planes, rows, size), BF16), pltpu.VMEM((planes, rows, size), BF16),
            ]
        return out + [dma((count,))] * 7 + [dma((count, planes))] * 2 + [dma((count,))] * 2

    def product(self, p, left, right):
        _, start, size, _ = self.parts[p]
        acc, s0 = self.bufs[p][0], self.bufs[p][1]
        first = self.core == 0
        rows = acc.shape[3]
        for c in range(0, size, 256):
            wide = min(256, size - c)
            total = mul(left[...], right[:, start + c : start + c + wide])
            total = total.reshape(self.planes, 2, 2, 2, rows, wide)
            acc[:, :, :, :, c : c + wide] = jnp.where(first, total[:, :, :, 0], total[:, :, :, 1])
            s0[:, :, :, :, c : c + wide] = jnp.where(first, total[:, :, :, 1], total[:, :, :, 0]).astype(BF16)

    def c0(self, p):
        own, s0s, s0r = self.sems[:3]
        return remote(self.bufs[p][1], self.bufs[p][2], s0s.at[p], s0r.at[p], self.twin)

    def c1(self, p):
        s1s, s1r = self.sems[3:5]
        sb, r1 = self.bufs[p][3], self.bufs[p][4]
        if self.parts[p][3] == 0:
            return remote(sb.at[:, 1 - self.y], r1, s1s.at[p], s1r.at[p], self.along)
        return remote(sb.at[:, :, 1 - self.x], r1, s1s.at[p], s1r.at[p], self.across)

    def c2(self, p):
        s2s, s2r = self.sems[5:7]
        sb, r2 = self.bufs[p][3], self.bufs[p][5]
        if self.parts[p][3] == 0:
            return remote(sb.at[:, self.y, 1 - self.x], r2, s2s.at[p], s2r.at[p], self.across)
        return remote(sb.at[:, 1 - self.y, self.x], r2, s2s.at[p], s2r.at[p], self.along)

    def c3(self, p, dest, source):
        s3s, s3r = self.sems[7:9]
        sb, r3 = self.bufs[p][3], self.bufs[p][6]
        to = {"shard": dest * PLANE + 2 * self.y + self.x}
        return remote(sb.at[dest, self.y, self.x], r3.at[source], s3s.at[p, dest], s3r.at[p, source], to)

    def into_half(self, p):
        acc, _, r0, sb = self.bufs[p][:4]
        self.c0(p).wait_recv()

        def step(i, carry):
            at = (i // PLANE, (i // 2) % 2, i % 2)
            value = acc[at] + r0[at].astype(F32)
            acc[at] = value
            sb[at] = value.astype(BF16)
            return carry

        lax.fori_loop(0, self.n, step, 0)
        self.c1(p).start()

    def after_first(self, p):
        acc, _, _, sb, r1 = self.bufs[p][:5]
        self.c1(p).wait_recv()
        self.c1(p).wait_send()

        def step(i, carry):
            zz, kk = i // 2, i % 2
            at = (zz, self.y, kk) if self.parts[p][3] == 0 else (zz, kk, self.x)
            value = acc[at] + r1[zz, kk].astype(F32)
            acc[at] = value
            sb[at] = value.astype(BF16)
            return carry

        lax.fori_loop(0, 2 * self.planes, step, 0)
        self.c2(p).start()

    def after_second(self, p):
        acc, _, _, sb, _, r2 = self.bufs[p][:6]
        z, y, x = self.z, self.y, self.x
        self.c2(p).wait_recv()
        self.c2(p).wait_send()
        for zz in range(self.planes):
            value = acc[zz, y, x] + r2[zz].astype(F32)
            acc[zz, y, x] = value
            sb[zz, y, x] = value.astype(BF16)
        for dest in range(self.planes):
            @pl.when(dest != z)
            def _():
                self.c3(p, dest, z).start()

    def results(self, p):
        own, s4s, s4r = self.sems[0], *self.sems[9:11]
        _, start, size, _ = self.parts[p]
        acc = self.bufs[p][0]
        rows = acc.shape[3]
        view = self.out.at[pl.ds(pl.multiple_of(self.core * rows, 8), rows), pl.ds(start, size)]
        mine = acc.at[self.z, self.y, self.x]
        return remote(mine, view, s4s.at[p], s4r.at[p], self.twin), pltpu.make_async_copy(mine, view, own.at[p])

    def finish(self, p):
        acc, r3 = self.bufs[p][0], self.bufs[p][6]
        for source in range(self.planes):
            @pl.when(source != self.z)
            def _():
                self.c3(p, source, source).wait_recv()
                acc[self.z, self.y, self.x] += r3[source].astype(F32)

        for copy in self.results(p):
            copy.start()

    def close(self, p):
        self.c0(p).wait_send()
        for dest in range(self.planes):
            @pl.when(dest != self.z)
            def _():
                self.c3(p, dest, self.z).wait_send()

        far, near = self.results(p)
        near.wait()
        far.wait()


def backward_exchange_kernel(n, *refs):
    len_ref, ord_ref, out_ref, glt_ref, cot_ref = refs[:5]
    blocks = refs[5:21]
    ig_ref, gp_ref, few_ref, slot_ref, gout_ref, out_stage = refs[21:27]
    scratch = refs[27:48]
    gb_v, out_s, out_r, out_fs, out_fr, out_l = refs[48:54]
    red = Reduction(n, OUT_PARTS, gout_ref, refs[54:])
    planes = n // PLANE
    step = pl.program_id(0)
    me = lax.axis_index("shard")
    z, quad = me // PLANE, me % PLANE
    piece = slot_ref.shape[1]
    width = cot_ref.shape[1]
    moves = ((out_stage, slot_ref, out_fs, out_fr, out_l),)

    def span(c):
        return pl.ds(pl.multiple_of(c * SPAN, SPAN), SPAN)

    def out_copy(to, source):
        return remote(
            out_ref.at[span(to)], out_stage.at[source], out_s.at[to], out_r.at[source], {"shard": to * PLANE + quad}
        )

    def own_out():
        return pltpu.make_async_copy(out_ref.at[span(z)], out_stage.at[z], out_l.at[planes])

    def pass_copy(m, zz, j, source):
        stage, dst, ss, sr, _ = moves[m]
        return remote(
            stage.at[zz, pl.ds(j * piece, piece)], dst.at[zz * PLANE + source], ss.at[zz, j], sr.at[zz, source],
            {"shard": z * PLANE + j},
        )

    def keep_copy(m, zz):
        stage, dst, _, _, sem = moves[m]
        rows = pl.ds(pl.multiple_of(quad * piece, piece), piece)
        return pltpu.make_async_copy(stage.at[zz, rows], dst.at[zz * PLANE + quad], sem.at[zz])

    def pass_on(m):
        for zz in range(planes):
            for j in range(PLANE):
                @pl.when(j != quad)
                def _():
                    pass_copy(m, zz, j, quad).start()

            keep_copy(m, zz).start()

    def landed(m):
        for zz in range(planes):
            for j in range(PLANE):
                @pl.when(j != quad)
                def _():
                    pass_copy(m, zz, j, quad).wait_send()
                    pass_copy(m, zz, j, j).wait_recv()

            keep_copy(m, zz).wait()

    @pl.when(step == 0)
    def _():
        barrier = pltpu.get_barrier_semaphore()
        for d in range(1, PLANE):
            near = z * PLANE + lax.rem(quad + d, PLANE)
            pl.semaphore_signal(barrier, inc=1, device_id={"shard": near}, device_id_type=MESH)
        for d in range(1, planes):
            far = lax.rem(z + d, planes) * PLANE + quad
            pl.semaphore_signal(barrier, inc=1, device_id={"shard": far}, device_id_type=MESH)
        pl.semaphore_signal(barrier, inc=1, device_id=red.twin, device_id_type=MESH)
        own_out().start()
        length = own_length(len_ref, ord_ref)
        for c in range(planes):
            positions = c * SPAN + lax.broadcasted_iota(jnp.int32, (SPAN, width), 0)
            rows = slice(c * SPAN, (c + 1) * SPAN)
            gb_v[rows, :] = jnp.where(positions < length, cot_ref[rows, :].astype(F32), 0.0).astype(BF16)
        pl.semaphore_wait(barrier, PLANE + planes - 1)
        for c in range(planes):
            @pl.when(c != z)
            def _():
                out_copy(c, z).start()

        for p in range(len(OUT_PARTS)):
            red.product(p, glt_ref, gb_v)
            red.c0(p).start()

    @pl.when(step == 1)
    def _():
        for p in range(len(OUT_PARTS)):
            red.into_half(p)

    @pl.when(step == 2)
    def _():
        for p in range(len(OUT_PARTS)):
            red.after_first(p)
        own_out().wait()
        for zz in range(planes):
            @pl.when(zz != z)
            def _():
                out_copy(zz, zz).wait_recv()

        pass_on(0)

    @pl.when(step == 3)
    def _():
        for p in range(len(OUT_PARTS)):
            red.after_second(p)

    rows = span(planes - 1 - step)
    backward_kernel(
        n, len_ref, ord_ref, cot_ref.at[rows], *blocks, ig_ref, gp_ref, gb_v.at[rows], few_ref, *scratch
    )

    @pl.when(step == planes - 1)
    def _():
        for p in range(len(OUT_PARTS)):
            red.finish(p)
        for c in range(planes):
            @pl.when(c != z)
            def _():
                out_copy(c, z).wait_send()

        landed(0)
        for p in range(len(OUT_PARTS)):
            red.close(p)


def run_backward_exchange(n, lengths, order, out, cot, tok, params, kept, glt):
    length, width = tok.shape
    count, piece, planes = length // SPAN, length // n, n // PLANE
    proj = DI + XBC + HEADS
    last = count - 1
    hbm = pl.BlockSpec(memory_space=pl.ANY)
    dma = pltpu.SemaphoreType.DMA
    shapes = [
        ((length, width), BF16), ((length, proj), BF16), ((n, EDGE, TILE), F32), ((n, piece, width), BF16),
        ((DI // n, width), F32), ((planes, SPAN, width), BF16),
    ]
    passes = [dma((planes,)), dma((planes,)), dma((planes, PLANE)), dma((planes, PLANE)), dma((planes + 1,))]
    return pl.pallas_call(
        functools.partial(backward_exchange_kernel, n),
        grid=(count,),
        out_shape=[jax.ShapeDtypeStruct(s, d) for s, d in shapes],
        in_specs=[
            SCALARS, SCALARS, hbm, whole((DI, length)), whole((length, width)), rows_of(width, last),
            *params_specs(width, params[0].shape[1]), *kept_blocks(last),
        ],
        out_specs=[rows_of(width, last), rows_of(proj, last), whole(shapes[2][0])] + [hbm] * 3,
        scratch_shapes=backward_scratch(width) + [
            pltpu.VMEM((length, width), BF16), *passes,
        ] + Reduction.scratch(n, OUT_PARTS, DI // n // REP),
        compiler_params=pltpu.CompilerParams(
            dimension_semantics=("arbitrary",), collective_id=2, has_side_effects=True, vmem_limit_bytes=LIMIT
        ),
    )(lengths, order, out, glt, cot, tok, *params, *kept)


def scatter_kernel(n, *refs):
    ig_ref, nl_ref, gp_ref, small_ref, slot_ref, gin_ref, sum_ref = refs[:7]
    nl_t, few, few_sib, ig_s, ig_r, few_s, few_r, pair_s, pair_r, own = refs[7:17]
    red = Reduction(n, IN_PARTS, gin_ref, refs[17:])
    me = lax.axis_index("shard")
    z = me // PLANE
    piece = slot_ref.shape[1]

    barrier = pltpu.get_barrier_semaphore()
    for d in range(1, n):
        pl.semaphore_signal(barrier, inc=1, device_id={"shard": lax.rem(me + d, n)}, device_id_type=MESH)
    pl.semaphore_signal(barrier, inc=1, device_id=red.twin, device_id_type=MESH)

    def ig_copy(d):
        to = lax.rem(me + d, n)
        src = ig_ref.at[pl.ds(pl.multiple_of(to * piece, piece), piece)]
        return remote(src, slot_ref.at[me], ig_s.at[d], ig_r.at[d], {"shard": to})

    def igs(first, last):
        for d in range(first, last):
            ig_copy(d).start()

    own_slot = pltpu.make_async_copy(ig_ref.at[pl.ds(pl.multiple_of(me * piece, piece), piece)], slot_ref.at[me], own)

    def few_copy(d):
        to = lax.rem(me + d, n)
        return remote(small_ref.at[to], few.at[me], few_s.at[d], few_r.at[d], {"shard": to})

    nl_t[...] = nl_ref[...].T
    for p in (0, 1):
        red.product(p, nl_t, gp_ref)
    pl.semaphore_wait(barrier, n)
    for p in (0, 1):
        red.c0(p).start()
    own_slot.start()
    igs(*SPREAD[0:2])
    for d in range(1, n):
        few_copy(d).start()
    for p in (2, 3):
        red.product(p, nl_t, gp_ref)
        red.c0(p).start()
    for p in (0, 1):
        red.into_half(p)
    igs(*SPREAD[1:3])
    for p in (2, 3):
        red.into_half(p)
    igs(*SPREAD[2:4])
    for p in (0, 1):
        red.after_first(p)
    igs(*SPREAD[3:5])
    for p in (0, 1):
        red.after_second(p)
    for p in (2, 3):
        red.after_first(p)
    for p in (0, 1):
        red.finish(p)
    few[me] = small_ref[me]
    for d in range(1, n):
        few_copy(d).wait()
    total = few[0]
    for k in range(1, n):
        total = total + few[k]
    few_sib[0] = total
    pair = remote(few_sib.at[0], few_sib.at[1], pair_s, pair_r, red.twin)
    pair.start()
    for p in (2, 3):
        red.after_second(p)
    for p in (2, 3):
        red.finish(p)
    pair.wait()
    sum_ref[...] = few_sib[0] + few_sib[1]
    own_slot.wait()
    for d in range(1, n):
        ig_copy(d).wait()
    for p in range(len(IN_PARTS)):
        red.close(p)


def run_scatter(n, ig, normed, gp, small):
    length, width = normed.shape
    piece = length // n
    few = small.shape[1:]
    vmem, hbm = pl.BlockSpec(memory_space=pltpu.VMEM), pl.BlockSpec(memory_space=pl.ANY)
    dma = pltpu.SemaphoreType.DMA
    shapes = [((n, piece, width), BF16), ((width // n, gp.shape[1]), F32), (few, F32)]
    return pl.pallas_call(
        functools.partial(scatter_kernel, n),
        out_shape=[jax.ShapeDtypeStruct(s, d) for s, d in shapes],
        in_specs=[hbm, vmem, vmem, vmem],
        out_specs=[hbm, hbm, vmem],
        scratch_shapes=[
            pltpu.VMEM((width, length), BF16), pltpu.VMEM((n, *few), F32), pltpu.VMEM((2, *few), F32),
            dma((n,)), dma((n,)), dma((n,)), dma((n,)), dma(()), dma(()), dma(()),
        ] + Reduction.scratch(n, IN_PARTS, width // n // REP),
        compiler_params=pltpu.CompilerParams(collective_id=1, has_side_effects=True, vmem_limit_bytes=LIMIT),
    )(ig, normed, gp, small)


def on_device(
    tokens, cotangent, lengths, order, norm_weight, in_weight, conv_weight, conv_bias,
    step_bias, decay_log, skip_gain, gate_norm_weight, out_weight,
):
    peers = lax.axis_size("shard")
    piece, width = tokens.shape[1:]

    def gather(x):
        return lax.all_gather(x, "shard", axis=0, tiled=True)

    def to_sequences(x):
        parts = x.reshape(peers, 1, piece, width)
        return lax.all_to_all(parts, "shard", split_axis=0, concat_axis=2, tiled=True).reshape(peers * piece, width)

    def to_slots(x):
        parts = x.reshape(peers, piece, width)
        return lax.all_to_all(parts, "shard", split_axis=0, concat_axis=0, tiled=True)

    direct = peers == PLANE * PLANE and lax.axis_size("rep") == REP and peers * piece == PLANE * SPAN
    if direct:
        pieces = (norm_weight[None], conv_weight.T, conv_bias[None], gate_norm_weight[None])
        heads = (step_bias[None], decay_log[None], skip_gain[None])
        forward, gathered = run_gather_forward(lengths, order, tokens, cotangent, in_weight, out_weight, pieces, heads)
        out, cin, gr, mx, st, sr, normed, gate_low, ar = forward
        tok, cot, params = gathered[0], gathered[1], gathered[2:]
    else:
        tok, cot = to_sequences(tokens), to_sequences(cotangent)
        params = prepare(
            gather(norm_weight), gather(in_weight), gather(conv_weight), gather(conv_bias),
            gather(gate_norm_weight), gather(out_weight), step_bias, decay_log, skip_gain,
        )
        out, cin, gr, mx, st, sr, normed, gate_low, ar = run_forward(lengths, order, tok, params)
    kept = (cin, gr, mx, st, sr, ar)
    if direct:
        results = run_backward_exchange(peers, lengths, order, out, cot, tok, params, kept, gate_low)
        ig, gp, few, output, grad_out = results[:5]
        input_grad, grad_in, few = run_scatter(peers, ig, normed, gp, few)
    else:
        output = to_slots(out)
        ig, gp, gb, few = run_backward(peers, lengths, order, cot, tok, params, kept)
        input_grad = to_slots(ig)

        def scatter(v):
            return lax.psum(lax.psum_scatter(v, "shard", scatter_dimension=0, tiled=True), "rep")

        grad_in, grad_out = scatter(mul_tn(normed, gp)), scatter(mul(gate_low, gb))
        parts = scatter(few[:, : EDGE - 1])
        few = jnp.concatenate([parts[0], lax.psum(few[0, EDGE - 1 :], ("rep", "shard"))])
    few, heads = run_split(few, norm_weight.size, conv_bias.size, gate_norm_weight.size)
    return (
        output, input_grad, few[0], grad_in, few[1], few[2], heads[0], heads[1], heads[2], few[3], grad_out,
    )


def solution(mesh):
    placed = (
        P("rep", "shard", None), P("rep", "shard", None), P("rep", None), P("rep", None), P("shard"),
        P("shard", None), P("shard", None), P("shard"), P(), P(), P(), P("shard"), P("shard", None),
    )
    outs = (
        P("rep", "shard", None), P("rep", "shard", None), P("shard"), P("shard", None), P("shard", None),
        P("shard"), P(), P(), P(), P("shard"), P("shard", None),
    )
    return jax.shard_map(on_device, mesh=mesh, in_specs=placed, out_specs=outs, check_vma=False)
```

```python
import functools

import jax
import jax.numpy as jnp
from jax import lax
from jax.experimental import pallas as pl
from jax.experimental.pallas import tpu as pltpu
from jax.sharding import PartitionSpec as P

HEADS = 24
HEADDIM = 64
STATE = 128
CONV = 4
SPAN = 256
DI = 1536
XBC = 1792
TILE = 128
PAIRS = DI // TILE
HALF = SPAN // 2
EDGE = 8
epsilon = 1e-05
LOG2E = 1.4426950408889634
F32 = jnp.float32
BF16 = jnp.bfloat16
FULL = lax.Precision.HIGHEST


def mul(a, b):
    return jnp.dot(a, b, preferred_element_type=F32)


def mul_nt(a, b):
    return lax.dot_general(a, b, (((1,), (1,)), ((), ())), preferred_element_type=F32)


def mul_tn(a, b):
    return lax.dot_general(a, b, (((0,), (0,)), ((), ())), preferred_element_type=F32)


def sigmoid(v):
    return 0.5 * jnp.tanh(0.5 * v) + 0.5


def softplus(v):
    return jnp.maximum(v, 0.0) + jnp.log1p(jnp.exp(-jnp.abs(v)))


def fold(v):
    return jnp.sum(v.reshape(v.shape[0] // EDGE, EDGE, v.shape[1]), axis=0)


def tile_at(j, base=0):
    return pl.ds(pl.multiple_of(base + j * TILE, TILE), TILE)


def lane_low(shape):
    return lax.broadcasted_iota(jnp.int32, shape, 1) < HEADDIM


def spread(column, h):
    return jnp.broadcast_to(column[:, h : h + 1], (column.shape[0], TILE))


def conv_argument(cin_ref, cw_ref, cb_ref, cols):
    total = cb_ref[:, cols]
    for tap in range(CONV):
        start = EDGE - CONV + 1 + tap
        total = total + cw_ref[tap : tap + 1, cols] * cin_ref[0, start : start + SPAN, cols]
    return total


def head_times(step_raw, step_bias, decay_log):
    shifted = step_raw + step_bias
    step = softplus(shifted)
    log_decay = -jnp.exp(decay_log) * step
    rows = lax.broadcasted_iota(jnp.int32, (SPAN, SPAN), 0)
    columns = lax.broadcasted_iota(jnp.int32, (SPAN, SPAN), 1)
    lower = (rows >= columns).astype(F32)
    cumul = jnp.dot(lower, log_decay, precision=FULL, preferred_element_type=F32)
    cumul = cumul * LOG2E
    return shifted, step, cumul, cumul - jnp.log2(step)


def own_length(len_ref, ord_ref):
    return len_ref[0, ord_ref[0, lax.axis_index("shard")]]


def causal_mask(flip):
    rows = lax.broadcasted_iota(jnp.int32, (HALF, HALF), 0)
    columns = lax.broadcasted_iota(jnp.int32, (HALF, HALF), 1)
    return columns >= rows if flip else rows >= columns


def forward_start(w_ref, ws, state, cin_ref):
    ws[...] = jnp.zeros_like(ws)
    ws[:, :HEADS] = w_ref[:, DI + XBC : DI + XBC + HEADS]
    state[...] = jnp.zeros_like(state)
    cin_ref[0, :EDGE, :] = jnp.zeros((EDGE, XBC), F32)


def forward_step(
    block, length, tok_ref, w_ref, ow_ref, nw_ref, cw_ref, cb_ref, sb_ref, dl_ref, sk_ref, gn_ref,
    out_ref, cin_ref, gr_ref, mx_ref, st_ref, sr_ref, nl_ref, gt_ref, ar_ref,
    ws, col_t, pair_s, row_s, state, scores, gated, gl_ref, hook=None,
):
    offset = block * SPAN

    @pl.when(block > 0)
    def _():
        cin_ref[0, :EDGE, :] = gated[:EDGE, :]

    for r in range(0, SPAN, 64):
        tok = tok_ref[r : r + 64, :].astype(F32)
        nrm = lax.rsqrt(jnp.mean(tok * tok, axis=-1, keepdims=True) + epsilon)
        nl_ref[r : r + 64, :] = (tok * nrm * nw_ref[...]).astype(BF16)
    low = nl_ref[...]
    sr_ref[...] = mul(low, ws[...])
    for n in range(0, XBC, 256):
        cin_ref[0, EDGE:, n : n + 256] = mul(low, w_ref[:, DI + n : DI + n + 256])
    for n in range(0, DI, 256):
        gr_ref[:, n : n + 256] = mul(low, w_ref[:, n : n + 256])

    _, _, cumul, shift = head_times(sr_ref[...], sb_ref[...], dl_ref[...])
    row_s[...] = shift.T
    low_lanes = lane_low((SPAN, TILE))
    for h in range(HEADS):
        col_t[h] = spread(cumul, h)
    for j in range(PAIRS):
        pair_s[j] = jnp.where(low_lanes, spread(shift, 2 * j), spread(shift, 2 * j + 1))

    def act(jt):
        cols = tile_at(jt)
        arg = conv_argument(cin_ref, cw_ref, cb_ref, cols)
        ar_ref[:, cols] = arg
        return arg * sigmoid(arg)

    key = act(PAIRS).astype(BF16)
    query = act(PAIRS + 1).astype(BF16)
    key_t = key.astype(F32).T.astype(BF16)
    scores[...] = mul_nt(query, key)
    st_ref[0] = state[...]
    mask = causal_mask(False)

    def pair(j, total):
        cols = tile_at(j)
        if hook is not None:
            hook(j)
        heads_in = act(j)
        heads_low = heads_in.astype(BF16)
        cum0, cum1 = col_t[2 * j], col_t[2 * j + 1]
        cum = jnp.where(low_lanes, cum0, cum1)
        last = cum[SPAN - 1 : SPAN, :]
        old = state[:, cols]
        across = mul(query, old.astype(BF16))
        weighted = (heads_low.astype(F32) * jnp.exp2(last - pair_s[j])).astype(BF16)
        state[:, cols] = jnp.exp2(last) * old + mul(key_t, weighted)
        zero = jnp.zeros_like(heads_low)
        parts = (jnp.where(low_lanes, heads_low, zero), jnp.where(low_lanes, zero, heads_low))
        top, bottom = [], []
        for h in range(2):
            col = (cum0, cum1)[h]
            row = row_s[pl.ds(2 * j + h, 1), :]
            first = jnp.where(mask, col[:HALF] - row[:, :HALF], -jnp.inf)
            top.append((scores[:HALF, :HALF] * jnp.exp2(first)).astype(BF16))
            full = col[HALF:] - row[:, :HALF]
            bottom.append((scores[HALF:, :HALF] * jnp.exp2(full)).astype(BF16))
            second = jnp.where(mask, col[HALF:] - row[:, HALF:], -jnp.inf)
            bottom.append((scores[HALF:, HALF:] * jnp.exp2(second)).astype(BF16))
        tops = jnp.concatenate([p[:HALF] for p in parts], axis=0)
        within = jnp.concatenate(
            [
                mul(jnp.concatenate(top, axis=1), tops),
                mul(jnp.concatenate(bottom, axis=1), jnp.concatenate(parts, axis=0)),
            ],
            axis=0,
        )
        mixed = within + jnp.exp2(cum) * across + sk_ref[:, cols] * heads_in
        mx_ref[:, cols] = mixed
        gate = gr_ref[:, cols]
        value = mixed * (gate * sigmoid(gate))
        gated[:, cols] = value
        return total + value * value

    total = lax.fori_loop(0, PAIRS, pair, jnp.zeros((SPAN, TILE), F32), unroll=3)
    rms = lax.rsqrt(jnp.sum(total, axis=-1, keepdims=True) * (1.0 / DI) + epsilon)

    def finish(j, carry):
        cols = tile_at(j)
        gl_ref[:, cols] = (gated[:, cols] * rms * gn_ref[:, cols]).astype(BF16)
        return carry

    lax.fori_loop(0, PAIRS, finish, 0)
    gt_ref[...] = gl_ref[...].T
    positions = offset + lax.broadcasted_iota(jnp.int32, (SPAN, 256), 0)
    valid = positions < length
    for n in range(0, tok_ref.shape[1], 256):
        branch = mul(gl_ref[...], ow_ref[:, n : n + 256])
        tok = tok_ref[:, n : n + 256].astype(F32)
        out_ref[:, n : n + 256] = (tok + jnp.where(valid, branch, 0.0)).astype(BF16)
    gated[:EDGE, :] = cin_ref[0, SPAN:, :]


def forward_kernel(
    len_ref, ord_ref, tok_ref, w_ref, ow_ref, nw_ref, cw_ref, cb_ref, sb_ref, dl_ref, sk_ref, gn_ref,
    out_ref, cin_ref, gr_ref, mx_ref, st_ref, sr_ref, nl_ref, gt_ref, ar_ref,
    ws, col_t, pair_s, row_s, state, scores, gated, gl_ref,
):
    block = pl.program_id(0)

    @pl.when(block == 0)
    def _():
        forward_start(w_ref, ws, state, cin_ref)

    forward_step(
        block, own_length(len_ref, ord_ref), tok_ref, w_ref, ow_ref, nw_ref, cw_ref, cb_ref, sb_ref, dl_ref, sk_ref, gn_ref,
        out_ref, cin_ref, gr_ref, mx_ref, st_ref, sr_ref, nl_ref, gt_ref, ar_ref,
        ws, col_t, pair_s, row_s, state, scores, gated, gl_ref,
    )


def backward_kernel(
    peers, len_ref, ord_ref, cot_ref, tok_ref, w_ref, ow_ref, nw_ref, cw_ref, cb_ref, sb_ref, dl_ref, sk_ref, gn_ref,
    cin_ref, gr_ref, mx_ref, st_ref, sr_ref, ar_ref,
    ig_ref, gp_ref, gb_ref, few_ref,
    taps_ref, gcb_ref, ggn_ref, gsk_ref, gnw_ref, ghd_ref,
    ws, col_s, pair_t, row_t, later, scores, grad_scores, gg, sig, gpre, acc_q, acc_k, acc_u, acc_v, acc_l,
):
    step_id = pl.program_id(0)
    count = pl.num_programs(0)
    offset = (count - 1 - step_id) * SPAN

    @pl.when(step_id == 0)
    def _():
        ws[...] = jnp.zeros_like(ws)
        ws[:, :HEADS] = w_ref[:, DI + XBC : DI + XBC + HEADS]
        later[...] = jnp.zeros_like(later)
        gpre[SPAN:, :] = jnp.zeros((EDGE, XBC), F32)
        for ref in (taps_ref, gcb_ref, ggn_ref, gsk_ref, gnw_ref, ghd_ref):
            ref[...] = jnp.zeros_like(ref)

    width = cot_ref.shape[1]
    positions = offset + lax.broadcasted_iota(jnp.int32, (SPAN, width), 0)
    grad_branch = jnp.where(positions < own_length(len_ref, ord_ref), cot_ref[...].astype(F32), 0.0).astype(BF16)
    gb_ref[...] = grad_branch
    for n in range(0, DI, 256):
        gg[:, n : n + 256] = mul_nt(grad_branch, ow_ref[n : n + 256, :])

    shifted, step, cumul, shift = head_times(sr_ref[...], sb_ref[...], dl_ref[...])
    row_t[...] = cumul.T
    low_lanes = lane_low((SPAN, TILE))
    for h in range(HEADS):
        col_s[h] = spread(shift, h)
    for j in range(PAIRS):
        pair_t[j] = jnp.where(low_lanes, spread(cumul, 2 * j), spread(cumul, 2 * j + 1))

    def sums(j, carry):
        squares, crossed = carry
        cols = tile_at(j)
        gate = gr_ref[:, cols]
        part = sigmoid(gate)
        sig[:, cols] = part
        value = mx_ref[:, cols] * (gate * part)
        return squares + value * value, crossed + (gg[:, cols] * gn_ref[:, cols]) * value

    nothing = jnp.zeros((SPAN, TILE), F32)
    squares, crossed = lax.fori_loop(0, PAIRS, sums, (nothing, nothing))
    rms = lax.rsqrt(jnp.sum(squares, axis=-1, keepdims=True) * (1.0 / DI) + epsilon)
    coef = rms * rms * (jnp.sum(crossed, axis=-1, keepdims=True) * (1.0 / DI))
    rms = jnp.broadcast_to(rms, (SPAN, TILE))
    coef = jnp.broadcast_to(coef, (SPAN, TILE))

    def act(jt):
        arg = ar_ref[:, jt * TILE : (jt + 1) * TILE]
        return (arg * sigmoid(arg)).astype(BF16)

    key = act(PAIRS)
    query = act(PAIRS + 1)
    query_t = query.astype(F32).T.astype(BF16)
    scores[...] = mul_nt(key, query)
    grad_scores[...] = jnp.zeros_like(grad_scores)
    for ref in (acc_q, acc_k, acc_u, acc_v, acc_l):
        ref[...] = jnp.zeros_like(ref)
    mask = causal_mask(True)
    lane = lax.broadcasted_iota(jnp.int32, (2 * TILE, TILE), 0) % TILE
    head = lax.broadcasted_iota(jnp.int32, (2 * TILE, TILE), 1)

    def by_head(value, pick):
        high = value.astype(BF16)
        rest = (value - high.astype(F32)).astype(BF16)
        return mul(jnp.concatenate([high, rest], axis=1), pick)

    def pair(j, carry):
        cols = tile_at(j)
        arg = ar_ref[:, cols]
        part_x = sigmoid(arg)
        heads_in = arg * part_x
        heads_low = heads_in.astype(BF16)
        heads_float = heads_low.astype(F32)
        gate, mixed, part, gain, back = (
            gr_ref[:, cols], mx_ref[:, cols], sig[:, cols], gn_ref[:, cols], gg[:, cols]
        )
        silu = gate * part
        value = mixed * silu
        ggn_ref[:, cols] += fold(back * value * rms)
        grad_gated = rms * (back * gain - value * coef)
        grad_scan = grad_gated * silu
        gp_ref[:, cols] = (grad_gated * mixed * (part * (1.0 + gate * (1.0 - part)))).astype(BF16)
        gsk_ref[:, cols] += fold(grad_scan * heads_in)
        cum = pair_t[j]
        growth = jnp.exp2(cum)
        last = cum[SPAN - 1 : SPAN, :]
        grad_low = grad_scan.astype(BF16)
        scaled = growth * grad_scan
        grad_across = scaled.astype(BF16)
        col0, col1 = col_s[2 * j], col_s[2 * j + 1]
        carry_weight = jnp.exp2(last - jnp.where(low_lanes, col0, col1))
        weighted = (heads_float * carry_weight).astype(BF16)
        after = later[:, cols]
        after_low = after.astype(BF16)
        before = st_ref[0, :, cols]
        before_low = before.astype(BF16)
        across = mul(query, before_low)
        acc_k[...] += mul_nt(weighted, after_low)
        acc_q[...] += mul_nt(grad_across, before_low)
        grow_last = jnp.exp2(last)
        carried = mul(key, after_low) * carry_weight
        last_sum = fold(carried * heads_float) + fold(after * before) * grow_last
        later[:, cols] = mul(query_t, grad_across) + grow_last * after
        zero = jnp.zeros_like(grad_low)
        parts = (jnp.where(low_lanes, grad_low, zero), jnp.where(low_lanes, zero, grad_low))
        top, bottom = [], []
        for h in range(2):
            col = (col0, col1)[h]
            row = row_t[pl.ds(2 * j + h, 1), :]
            mixed_top = mul_nt(heads_low[:HALF], parts[h])
            mixed_low = mul_nt(heads_low[HALF:], parts[h][HALF:])
            factor = jnp.exp2(jnp.where(mask, row[:, :HALF] - col[:HALF], -jnp.inf))
            top.append((scores[:HALF, :HALF] * factor).astype(BF16))
            grad_scores[:HALF, :HALF] += mixed_top[:, :HALF] * factor
            factor = jnp.exp2(row[:, HALF:] - col[:HALF])
            top.append((scores[:HALF, HALF:] * factor).astype(BF16))
            grad_scores[:HALF, HALF:] += mixed_top[:, HALF:] * factor
            factor = jnp.exp2(jnp.where(mask, row[:, HALF:] - col[HALF:], -jnp.inf))
            bottom.append((scores[HALF:, HALF:] * factor).astype(BF16))
            grad_scores[HALF:, HALF:] += mixed_low * factor
        lows = jnp.concatenate([p[HALF:] for p in parts], axis=0)
        grad_heads = carried + jnp.concatenate(
            [
                mul(jnp.concatenate(top, axis=1), jnp.concatenate(parts, axis=0)),
                mul(jnp.concatenate(bottom, axis=1), lows),
            ],
            axis=0,
        )
        gain_skip = sk_ref[:, cols]
        spanned = growth * across
        within = mixed - gain_skip * heads_in - spanned
        pick = (head == 2 * j + lane // HEADDIM).astype(F32)
        pick_low = pick.astype(BF16)
        acc_u[...] += by_head(grad_low.astype(F32) * within + grad_scan * spanned, pick_low)
        acc_v[...] += by_head(heads_float * grad_heads, pick_low)
        acc_l[...] += jnp.dot(last_sum, pick[:TILE], precision=FULL, preferred_element_type=F32)
        grad_conv = grad_heads + gain_skip * grad_scan
        gpre[:SPAN, cols] = grad_conv * (part_x * (1.0 + arg * (1.0 - part_x)))
        return carry

    lax.fori_loop(0, PAIRS, pair, 0, unroll=3)

    rows = lax.broadcasted_iota(jnp.int32, (SPAN, SPAN), 0)
    columns = lax.broadcasted_iota(jnp.int32, (SPAN, SPAN), 1)
    upper = (columns >= rows).astype(F32)
    at_end = lax.broadcasted_iota(jnp.int32, (SPAN, TILE), 0) == SPAN - 1
    to_step = acc_v[...]
    ends = jnp.sum(acc_l[...], axis=0, keepdims=True)
    grad_cumul = acc_u[...] - to_step + jnp.where(at_end, ends, 0.0)
    grad_log = jnp.dot(upper, grad_cumul, precision=FULL, preferred_element_type=F32)
    rate = jnp.exp(dl_ref[...])
    safe = jnp.where(step > 0.0, step, 1.0)
    grad_step = jnp.where(step > 0.0, to_step / safe, 0.0)
    grad_raw = (grad_step - rate * grad_log) * sigmoid(shifted)
    ghd_ref[:EDGE, :] += fold(grad_raw)
    ghd_ref[EDGE:, :] -= fold(rate * step * grad_log)
    raw_low = grad_raw.astype(BF16)
    gp_ref[:, DI + XBC :] = raw_low[:, :HEADS]

    scores_low = grad_scores[...].astype(BF16)
    scores_t = grad_scores[...].T.astype(BF16)
    for slot, grad in (
        (0, acc_k[...] + mul(scores_low, query)),
        (1, acc_q[...] + mul(scores_t, key)),
    ):
        arg = ar_ref[:, DI + slot * TILE : DI + (slot + 1) * TILE]
        part = sigmoid(arg)
        gpre[:SPAN, DI + slot * TILE : DI + (slot + 1) * TILE] = grad * (part * (1.0 + arg * (1.0 - part)))

    def through_conv(j, carry):
        cols = tile_at(j)
        here = gpre[:SPAN, cols]
        gcb_ref[:, cols] += fold(here)
        total = jnp.zeros_like(here)
        given = cin_ref[0, EDGE:, cols]
        for tap in range(CONV):
            ahead = CONV - 1 - tap
            later_grad = gpre[ahead : ahead + SPAN, cols]
            taps_ref[tap, :, cols] += fold(given * later_grad)
            total = total + cw_ref[tap : tap + 1, cols] * later_grad
        gp_ref[:, tile_at(j, DI)] = total.astype(BF16)
        return carry

    lax.fori_loop(0, PAIRS + 2, through_conv, 0)
    gpre[SPAN:, :] = gpre[:EDGE, :]

    for n in range(0, width, 256):
        grad = mul_nt(gp_ref[:, : DI + XBC], w_ref[n : n + 256, : DI + XBC])
        gg[:, n : n + 256] = grad + mul_nt(raw_low, ws[n : n + 256, :])
    for r in range(0, SPAN, 64):
        tok = tok_ref[r : r + 64, :].astype(F32)
        nrm = lax.rsqrt(jnp.mean(tok * tok, axis=-1, keepdims=True) + epsilon)
        grad = gg[r : r + 64, :width]
        gnw_ref[...] += fold(grad * tok * nrm)
        value = grad * nw_ref[...]
        centre = jnp.mean(value * tok, axis=-1, keepdims=True) * (nrm * nrm)
        grad_tok = nrm * (value - tok * centre)
        ig_ref[r : r + 64, :] = (cot_ref[r : r + 64, :].astype(F32) + grad_tok).astype(BF16)

    @pl.when(step_id == count - 1)
    def _():
        rows = lax.broadcasted_iota(jnp.int32, (DI, TILE), 0) // HEADDIM
        pick = (lax.broadcasted_iota(jnp.int32, (DI, TILE), 1) == rows + 2 * HEADS).astype(F32)
        skips = jnp.dot(gsk_ref[...], pick, precision=FULL, preferred_element_type=F32)
        heads = ghd_ref[:EDGE, :] + pltpu.roll(ghd_ref[EDGE:, :], HEADS, 1) + skips
        heads = jnp.sum(heads, axis=0, keepdims=True)
        few_ref[...] = jnp.zeros_like(few_ref)
        grads = [jnp.sum(gnw_ref[...], axis=0, keepdims=True)]
        grads += [jnp.sum(taps_ref[tap], axis=0, keepdims=True) for tap in range(CONV)]
        grads += [jnp.sum(ref[...], axis=0, keepdims=True) for ref in (gcb_ref, ggn_ref)]
        for r, grad in enumerate(grads):
            size = grad.shape[1] // peers
            for k in range(peers):
                few_ref[k, r : r + 1, :size] = grad[:, k * size : (k + 1) * size]
        for k in range(peers):
            few_ref[k, EDGE - 1 : EDGE, :] = heads


def split_kernel(sum_ref, *outs):
    rows = [0, 1, 1 + CONV, 2 + CONV] + [EDGE - 1] * 3
    for i, (ref, r) in enumerate(zip(outs, rows)):
        start = max(i - 4, 0) * HEADS
        ref[...] = sum_ref[r : r + ref.shape[0], start : start + ref.shape[1]]


def run_split(total, norm, taps, gate):
    shapes = [(1, norm), (CONV, taps), (1, taps), (1, gate)] + [(1, HEADS)] * 3
    outs = pl.pallas_call(split_kernel, out_shape=[jax.ShapeDtypeStruct(s, F32) for s in shapes])(total)
    return [outs[0][0], outs[1].T, outs[2][0], outs[3][0]], [o[0] for o in outs[4:]]


def whole(shape):
    return pl.BlockSpec(shape, lambda i: (0,) * len(shape), pipeline_mode=pl.Buffered(1))


def rows_of(width, last=None):
    if last is None:
        return pl.BlockSpec((SPAN, width), lambda i: (i, 0))
    return pl.BlockSpec((SPAN, width), lambda i: (last - i, 0))


def params_specs(width, proj):
    return [
        whole((width, proj)), whole((DI, width)), whole((1, width)), whole((CONV, XBC)), whole((1, XBC)),
        whole((1, TILE)), whole((1, TILE)), whole((1, DI)), whole((1, DI)),
    ]


LIMIT = 60 * 2**20
SCALARS = pl.BlockSpec(memory_space=pltpu.SMEM)


def forward_results(length, width):
    count = length // SPAN
    shapes = [
        ((length, width), BF16), ((count, SPAN + EDGE, XBC), F32), ((length, DI), F32), ((length, DI), F32),
        ((count, STATE, DI), F32), ((length, TILE), F32), ((length, width), BF16), ((DI, length), BF16), ((length, XBC), F32),
    ]
    out_specs = [
        rows_of(width), pl.BlockSpec((1, SPAN + EDGE, XBC), lambda i: (i, 0, 0)), rows_of(DI), rows_of(DI),
        pl.BlockSpec((1, STATE, DI), lambda i: (i, 0, 0)), rows_of(TILE), rows_of(width), pl.BlockSpec((DI, SPAN), lambda i: (0, i)), rows_of(XBC),
    ]
    scratch = [
        pltpu.VMEM((width, TILE), BF16), pltpu.VMEM((HEADS, SPAN, TILE), F32), pltpu.VMEM((PAIRS, SPAN, TILE), F32),
        pltpu.VMEM((TILE, SPAN), F32), pltpu.VMEM((STATE, DI), F32), pltpu.VMEM((SPAN, SPAN), F32), pltpu.VMEM((SPAN, XBC), F32), pltpu.VMEM((SPAN, DI), BF16),
    ]
    return [jax.ShapeDtypeStruct(s, d) for s, d in shapes], out_specs, scratch


def run_forward(lengths, order, tok, params):
    length, width = tok.shape
    shapes, out_specs, scratch = forward_results(length, width)
    return pl.pallas_call(
        forward_kernel,
        grid=(length // SPAN,),
        out_shape=shapes,
        in_specs=[SCALARS, SCALARS, rows_of(width), *params_specs(width, params[0].shape[1])],
        out_specs=out_specs,
        scratch_shapes=scratch,
        compiler_params=pltpu.CompilerParams(dimension_semantics=("arbitrary",), vmem_limit_bytes=LIMIT),
        cost_estimate=pl.CostEstimate(flops=20 * 10**9, bytes_accessed=60 * 10**6, transcendentals=10**7),
    )(lengths, order, tok, *params)


def backward_scratch(width):
    square, wide = pltpu.VMEM((SPAN, SPAN), F32), pltpu.VMEM((SPAN, DI), F32)
    narrow = pltpu.VMEM((SPAN, TILE), F32)
    return [
        *(pltpu.VMEM(s, F32) for s in ((CONV, EDGE, XBC), (EDGE, XBC), (EDGE, DI), (EDGE, DI), (EDGE, width), (2 * EDGE, TILE))),
        pltpu.VMEM((width, TILE), BF16), pltpu.VMEM((HEADS, SPAN, TILE), F32), pltpu.VMEM((PAIRS, SPAN, TILE), F32),
        pltpu.VMEM((TILE, SPAN), F32), pltpu.VMEM((STATE, DI), F32), square, square, wide, wide,
        pltpu.VMEM((SPAN + EDGE, XBC), F32),
        narrow, narrow, narrow, narrow, pltpu.VMEM((EDGE, TILE), F32),
    ]


def kept_blocks(last):
    return [
        pl.BlockSpec((1, SPAN + EDGE, XBC), lambda i: (last - i, 0, 0)), rows_of(DI, last), rows_of(DI, last),
        pl.BlockSpec((1, STATE, DI), lambda i: (last - i, 0, 0)), rows_of(TILE, last), rows_of(XBC, last),
    ]


def run_backward(peers, lengths, order, cot, tok, params, kept):
    length, width = tok.shape
    count = length // SPAN
    proj = DI + XBC + HEADS
    last = count - 1
    shapes = [((length, width), BF16), ((length, proj), BF16), ((length, width), BF16), ((peers, EDGE, TILE), F32)]
    out_specs = [rows_of(width, last), rows_of(proj, last), rows_of(width, last), whole(shapes[3][0])]
    kept_specs = kept_blocks(last)
    return pl.pallas_call(
        functools.partial(backward_kernel, peers),
        grid=(count,),
        out_shape=[jax.ShapeDtypeStruct(s, d) for s, d in shapes],
        in_specs=[SCALARS, SCALARS, rows_of(width, last), rows_of(width, last), *params_specs(width, params[0].shape[1]), *kept_specs],
        out_specs=out_specs,
        scratch_shapes=backward_scratch(width),
        compiler_params=pltpu.CompilerParams(dimension_semantics=("arbitrary",), vmem_limit_bytes=LIMIT),
        cost_estimate=pl.CostEstimate(flops=40 * 10**9, bytes_accessed=60 * 10**6, transcendentals=2 * 10**7),
    )(lengths, order, cot, tok, *params, *kept)


def prepare(norm_full, in_full, conv_full, shift_full, gate_full, out_full, step_bias, decay_log, skip_gain):
    pad = ((0, 0), (0, TILE - HEADS))
    return (
        in_full,
        out_full,
        norm_full.astype(F32)[None],
        conv_full.astype(F32).T,
        shift_full.astype(F32)[None],
        jnp.pad(step_bias[None], pad),
        jnp.pad(decay_log[None], pad),
        jnp.repeat(skip_gain, HEADDIM)[None],
        gate_full.astype(F32)[None],
    )


MESH = pl.DeviceIdType.MESH
PLANE = 4
REP = 2
COT_AT = 1


def lay_out(few, n, nw_ref, cw_ref, cb_ref, gn_ref):
    for ref, row in ((nw_ref, 0), (cw_ref, 1), (cb_ref, 1 + CONV), (gn_ref, 2 + CONV)):
        size = ref.shape[1] // n
        for k in range(n):
            ref[:, k * size : (k + 1) * size] = few[k, row : row + ref.shape[0], :size]


def gather_forward_kernel(n, *refs):
    len_ref, ord_ref, tok_ref, cot_ref, in_ref, ow_ref = refs[:6]
    pieces, (sb_in, dl_in, sk_in) = refs[6:10], refs[10:13]
    blocks = refs[13:22]
    seq_ref, cots_ref, inf_ref, owf_ref, nw_ref, cw_ref, cb_ref, sb_ref, dl_ref, sk_ref, gn_ref = refs[22:33]
    own_scratch = refs[33:41]
    (
        tok_v, w_v, ow_v, small_ref, few, tok_stage, own,
        tok_s, tok_r, tok_fs, tok_fr, tok_l, cot_s, cot_r, small_s, small_r, line_s, line_r, plane_s, plane_r, sib_s, sib_r, keep_s,
    ) = refs[41:]
    planes = n // PLANE
    block = pl.program_id(0)
    me = lax.axis_index("shard")
    core = lax.axis_index("rep")
    z, y, x = me // PLANE, (me // 2) % 2, me % 2
    across = me + 1 - 2 * x
    along = me + 2 - 4 * y
    piece = tok_ref.shape[1]
    arrays = ((in_ref, w_v), (ow_ref, ow_v))

    def region(a, k, part=None):
        src, dst = arrays[a]
        half = dst.shape[1] // REP
        first = pl.cdiv(half // TILE, 2) * TILE
        rows = pl.ds(pl.multiple_of(k * src.shape[0], src.shape[0]), src.shape[0])
        start, size = ((0, first), (first, half - first), (0, half))[2 if part is None else part]
        return dst.at[rows, pl.ds(pl.multiple_of(core * half + start, TILE), size)]

    def send(view, to, s, r):
        return pltpu.make_async_remote_copy(
            src_ref=view, dst_ref=view, send_sem=s, recv_sem=r, device_id=to, device_id_type=MESH
        )

    def line(a, origin, to):
        return send(region(a, origin), {"shard": to}, line_s.at[a, origin // PLANE, (to > me).astype(jnp.int32)], line_r.at[a, origin // PLANE])

    def hop(a, zz, kind):
        here = zz * PLANE + 2 * y + x
        side = zz * PLANE + 2 * y + 1 - x
        ahead = zz * PLANE + 2 * (1 - y) + x
        origin, part, to = (
            (here, 0, across), (here, 1, along), (here, 0, along), (here, 1, across), (side, 0, along), (ahead, 1, across),
        )[kind]
        return send(region(a, origin, part), {"shard": to}, plane_s.at[a, zz, kind], plane_r.at[a, zz, kind])

    def sibling(a, zz, kind):
        origin = zz * PLANE + (2 * y + x, 2 * y + 1 - x, 2 * (1 - y) + x, 2 * (1 - y) + 1 - x)[kind]
        return send(region(a, origin), {"rep": 1 - core}, sib_s.at[a, zz, kind], sib_r.at[a, zz, kind])

    def rows(k):
        return pl.ds(pl.multiple_of(k * piece, piece), piece)

    quad = me % PLANE
    moves = (
        (tok_ref, tok_stage, tok_v, tok_s, tok_r, tok_fs, tok_fr, tok_l),
    )

    def stage_copy(m, to, source):
        src, stage, _, ss, sr = moves[m][:5]
        return pltpu.make_async_remote_copy(
            src_ref=src.at[pl.ds(pl.multiple_of(to * PLANE, PLANE), PLANE)], dst_ref=stage.at[source],
            send_sem=ss.at[to], recv_sem=sr.at[source],
            device_id={"shard": to * PLANE + quad}, device_id_type=MESH,
        )

    def own_stage(m):
        src, stage = moves[m][:2]
        return pltpu.make_async_copy(src.at[pl.ds(pl.multiple_of(z * PLANE, PLANE), PLANE)], stage.at[z], moves[m][7].at[planes])

    def pass_copy(m, zz, j, source):
        _, stage, dst, _, _, ss, sr, _ = moves[m]
        return pltpu.make_async_remote_copy(
            src_ref=stage.at[zz, j], dst_ref=dst.at[rows(zz * PLANE + source)],
            send_sem=ss.at[zz, j], recv_sem=sr.at[zz, source],
            device_id={"shard": z * PLANE + j}, device_id_type=MESH,
        )

    def keep_copy(m, zz):
        _, stage, dst = moves[m][:3]
        return pltpu.make_async_copy(stage.at[zz, quad], dst.at[rows(zz * PLANE + quad)], moves[m][7].at[zz])

    def start_stage(m):
        for p in range(planes):
            @pl.when(p != z)
            def _():
                stage_copy(m, p, z).start()

    def pass_on(m, zz):
        @pl.when(zz != z)
        def _():
            stage_copy(m, zz, zz).wait_recv()

        for j in range(PLANE):
            @pl.when(j != quad)
            def _():
                pass_copy(m, zz, j, quad).start()

        keep_copy(m, zz).start()

    def landed(m, zz):
        for j in range(PLANE):
            @pl.when(j != quad)
            def _():
                pass_copy(m, zz, j, j).wait_recv()

        keep_copy(m, zz).wait()

    def gone(m):
        for zz in range(planes):
            @pl.when(zz != z)
            def _():
                stage_copy(m, zz, z).wait_send()

            for j in range(PLANE):
                @pl.when(j != quad)
                def _():
                    pass_copy(m, zz, j, quad).wait_send()

    def cot_copy(to, source):
        return pltpu.make_async_remote_copy(
            src_ref=cot_ref.at[to], dst_ref=cots_ref.at[rows(source)], send_sem=cot_s.at[to], recv_sem=cot_r.at[source],
            device_id={"shard": to}, device_id_type=MESH,
        )

    def small_copy(to, source):
        return pltpu.make_async_remote_copy(
            src_ref=small_ref, dst_ref=few.at[source], send_sem=small_s.at[to], recv_sem=small_r.at[source],
            device_id={"shard": to}, device_id_type=MESH,
        )

    def local_copies():
        src, dst = arrays[1]
        return [
            pltpu.make_async_copy(src, dst.at[pl.ds(pl.multiple_of(me * src.shape[0], 8), src.shape[0])], own.at[1]),
            pltpu.make_async_copy(small_ref, few.at[me], own.at[2]),
            own_stage(0),
            pltpu.make_async_copy(cot_ref.at[me], cots_ref.at[rows(me)], own.at[0]),
        ]

    def saves():
        return [
            pltpu.make_async_copy(w_v, inf_ref, keep_s.at[0]),
            pltpu.make_async_copy(ow_v, owf_ref, keep_s.at[1]),
        ]

    def launch(a, zz):
        for kind in range(4):
            hop(a, zz, kind).start()

    def relay(a, zz):
        hop(a, zz, 0).wait_recv()
        hop(a, zz, 4).start()
        hop(a, zz, 1).wait_recv()
        hop(a, zz, 5).start()

    def collect(a, zz):
        hop(a, zz, 3).wait_recv()
        sibling(a, zz, 1).start()
        hop(a, zz, 2).wait_recv()
        sibling(a, zz, 2).start()
        hop(a, zz, 4).wait_recv()
        hop(a, zz, 5).wait_recv()
        sibling(a, zz, 3).start()

    def each(d, step):
        @pl.when(z - d >= 0)
        def _():
            step(z - d, me - d * PLANE, me + PLANE, z + 1 < planes)

        @pl.when(z + d < planes)
        def _():
            step(z + d, me + d * PLANE, me - PLANE, z > 0)

    def start_line(a):
        @pl.when(z + 1 < planes)
        def _():
            line(a, me, me + PLANE).start()

        @pl.when(z > 0)
        def _():
            line(a, me, me - PLANE).start()

    def arrived(a):
        def step(zz, origin, to, more):
            line(a, origin, to).wait_recv()

            @pl.when(more)
            def _():
                line(a, origin, to).start()

            sibling(a, zz, 0).start()
            launch(a, zz)

        return step

    def send_pieces(copy, first, last):
        for d in range(first, last):
            copy(lax.rem(me + d, n), me).start()

    @pl.when(block == 0)
    def _():
        barrier = pltpu.get_barrier_semaphore()
        for d in range(1, n):
            pl.semaphore_signal(barrier, inc=1, device_id={"shard": lax.rem(me + d, n)}, device_id_type=MESH)
        pl.semaphore_signal(barrier, inc=1, device_id={"rep": 1 - core}, device_id_type=MESH)
        small_ref[...] = jnp.zeros_like(small_ref)
        for row, ref in zip((0, 1, 1 + CONV, 2 + CONV), pieces):
            small_ref[row : row + ref.shape[0], : ref.shape[1]] = ref[...].astype(F32)
        for ref, given in ((sb_ref, sb_in), (dl_ref, dl_in)):
            ref[...] = jnp.zeros_like(ref)
            ref[:, :HEADS] = given[...]
        for h in range(HEADS):
            sk_ref[:, h * HEADDIM : (h + 1) * HEADDIM] = jnp.broadcast_to(sk_in[:, h : h + 1], (1, HEADDIM))
        local = local_copies()
        for copy in local:
            copy.start()
        width = in_ref.shape[1]
        mine = pl.ds(pl.multiple_of(me * in_ref.shape[0], in_ref.shape[0]), in_ref.shape[0])
        w_v[mine, width // TILE * TILE :] = jnp.zeros((in_ref.shape[0], w_v.shape[1] - width // TILE * TILE), BF16)
        w_v[mine, :width] = in_ref[...]
        for copy in local[:1]:
            copy.wait()
        pl.semaphore_wait(barrier, n)
        for a in range(2):
            start_line(a)
        for a in range(2):
            launch(a, z)

        @pl.when(z == 0)
        def _():
            start_stage(0)

        send_pieces(small_copy, 1, n)
        for d in range(1, planes):
            for a in range(2):
                each(d, arrived(a))
                if d == 1:
                    relay(a, z)
                else:
                    each(d - 1, lambda zz, *_: relay(a, zz))

        @pl.when(z > 0)
        def _():
            start_stage(0)

        for a in range(2):
            collect(a, z)
            each(planes - 1, lambda zz, *_: relay(a, zz))
        for a in range(2):
            for d in range(1, planes):
                each(d, lambda zz, *_: collect(a, zz))
        for copy in local[1:]:
            copy.wait()
        for k in range(n):
            @pl.when(me != k)
            def _():
                small_copy(k, k).wait_recv()
        lay_out(few, n, nw_ref, cw_ref, cb_ref, gn_ref)
        for a in range(2):
            for d in range(planes):
                for kind in range(4):
                    if kind > 0:
                        sibling(a, d, kind).wait_recv()
                    else:
                        @pl.when(z != d)
                        def _():
                            sibling(a, d, kind).wait_recv()
        for copy in saves():
            copy.start()
        pass_on(0, 0)
        forward_start(w_v, own_scratch[0], own_scratch[4], blocks[1])

    @pl.when(block < 2)
    def _():
        pass_on(0, block + 1)

    @pl.when(block == 1)
    def _():
        for zz in range(3, planes):
            pass_on(0, zz)

    landed(0, block)

    @pl.when(block == COT_AT)
    def _():
        send_pieces(cot_copy, 1, n)

    forward_step(
        block, own_length(len_ref, ord_ref), tok_v.at[pl.ds(pl.multiple_of(block * SPAN, SPAN), SPAN)], w_v, ow_v,
        nw_ref, cw_ref, cb_ref, sb_ref, dl_ref, sk_ref, gn_ref, *blocks, *own_scratch,
    )

    @pl.when(block == pl.num_programs(0) - 1)
    def _():
        keep = pltpu.make_async_copy(tok_v, seq_ref, keep_s.at[2])
        keep.start()
        for copy in saves():
            copy.wait()
        gone(0)
        for k in range(n):
            @pl.when(me != k)
            def _():
                small_copy(k, k).wait_send()
                cot_copy(k, k).wait()
        for a in range(2):
            def sent(zz, origin, to, more):
                @pl.when(more)
                def _():
                    line(a, origin, to).wait_send()

            for d in range(1, planes):
                each(d, sent)

            @pl.when(z + 1 < planes)
            def _():
                line(a, me, me + PLANE).wait_send()

            @pl.when(z > 0)
            def _():
                line(a, me, me - PLANE).wait_send()

            for zz in range(planes):
                for kind in range(6):
                    hop(a, zz, kind).wait_send()
                for kind in range(4):
                    if kind > 0:
                        sibling(a, zz, kind).wait_send()
                    else:
                        @pl.when(z != zz)
                        def _():
                            sibling(a, zz, kind).wait_send()
        keep.wait()


def run_gather_forward(lengths, order, tokens, cotangent, in_weight, out_weight, pieces, heads):
    n, piece, width = tokens.shape
    length = n * piece
    planes = n // PLANE
    proj = pl.cdiv(in_weight.shape[1], 2 * REP * TILE) * 2 * REP * TILE
    inner = n * out_weight.shape[0]
    hbm = pl.BlockSpec(memory_space=pl.ANY)
    vmem = pl.BlockSpec(memory_space=pltpu.VMEM)
    dma = pltpu.SemaphoreType.DMA
    shapes, out_specs, scratch = forward_results(length, width)
    rows = [(1, width), (CONV, XBC), (1, XBC), (1, TILE), (1, TILE), (1, DI), (1, DI)]
    more = [((length, width), BF16)] * 2 + [((width, proj), BF16), ((inner, width), BF16)] + [(r, F32) for r in rows]
    results = pl.pallas_call(
        functools.partial(gather_forward_kernel, n),
        grid=(length // SPAN,),
        out_shape=shapes + [jax.ShapeDtypeStruct(s, d) for s, d in more],
        in_specs=[SCALARS, SCALARS, hbm, hbm, vmem, hbm] + [vmem] * 7,
        out_specs=out_specs + [hbm] * 4 + [whole(r) for r in rows],
        scratch_shapes=scratch + [
            pltpu.VMEM((length, width), BF16), pltpu.VMEM((width, proj), BF16), pltpu.VMEM((inner, width), BF16),
            pltpu.VMEM((EDGE, TILE), F32), pltpu.VMEM((n, EDGE, TILE), F32), pltpu.VMEM((planes, PLANE, piece, width), BF16), dma((3,)),
            *(dma(d) for d in ((planes,), (planes,), (planes, PLANE), (planes, PLANE), (planes + 1,))), *(dma((n,)) for _ in range(4)), dma((2, planes, 2)), dma((2, planes)),
            dma((2, planes, 6)), dma((2, planes, 6)), dma((2, planes, 4)), dma((2, planes, 4)), dma((3,)),
        ],
        compiler_params=pltpu.CompilerParams(
            dimension_semantics=("arbitrary",), collective_id=0, has_side_effects=True, vmem_limit_bytes=LIMIT
        ),
    )(lengths, order, tokens, cotangent, in_weight, out_weight, *pieces, *heads)
    return results[:9], results[9:]


OUT_PARTS = ((1, 0, 384, 0), (1, 384, 384, 1))
IN_PARTS = ((0, 0, 768, 0), (0, 768, 768, 1), (0, 1536, 896, 0), (0, 2432, 920, 1))


SPREAD = (1, 6, 11, 16, 16)


def remote(src, dst, s, r, to):
    return pltpu.make_async_remote_copy(src_ref=src, dst_ref=dst, send_sem=s, recv_sem=r, device_id=to, device_id_type=MESH)


class Reduction:
    def __init__(self, n, parts, out, refs):
        self.n, self.parts, self.out = n, parts, out
        count = len(parts)
        self.bufs = [refs[i * 7 : (i + 1) * 7] for i in range(count)]
        self.sems = refs[count * 7 :]
        self.planes = n // PLANE
        me = lax.axis_index("shard")
        self.core = lax.axis_index("rep")
        self.z, self.y, self.x = me // PLANE, (me // 2) % 2, me % 2
        self.across = {"shard": me + 1 - 2 * self.x}
        self.along = {"shard": me + 2 - 4 * self.y}
        self.twin = {"rep": 1 - self.core}

    @staticmethod
    def scratch(n, parts, rows):
        planes, count, dma = n // PLANE, len(parts), pltpu.SemaphoreType.DMA
        out = []
        for _, _, size, _ in parts:
            full = (planes, 2, 2, rows, size)
            out += [
                pltpu.VMEM(full, F32), pltpu.VMEM(full, BF16), pltpu.VMEM(full, BF16), pltpu.VMEM(full, BF16),
                pltpu.VMEM((planes, 2, rows, size), BF16), pltpu.VMEM((planes, rows, size), BF16), pltpu.VMEM((planes, rows, size), BF16),
            ]
        return out + [dma((count,))] * 7 + [dma((count, planes))] * 2 + [dma((count,))] * 2

    def product(self, p, left, right):
        _, start, size, _ = self.parts[p]
        acc, s0 = self.bufs[p][0], self.bufs[p][1]
        first = self.core == 0
        rows = acc.shape[3]
        for c in range(0, size, 256):
            wide = min(256, size - c)
            total = mul(left[...], right[:, start + c : start + c + wide])
            total = total.reshape(self.planes, 2, 2, 2, rows, wide)
            acc[:, :, :, :, c : c + wide] = jnp.where(first, total[:, :, :, 0], total[:, :, :, 1])
            s0[:, :, :, :, c : c + wide] = jnp.where(first, total[:, :, :, 1], total[:, :, :, 0]).astype(BF16)

    def c0(self, p):
        own, s0s, s0r = self.sems[:3]
        return remote(self.bufs[p][1], self.bufs[p][2], s0s.at[p], s0r.at[p], self.twin)

    def c1(self, p):
        s1s, s1r = self.sems[3:5]
        sb, r1 = self.bufs[p][3], self.bufs[p][4]
        if self.parts[p][3] == 0:
            return remote(sb.at[:, 1 - self.y], r1, s1s.at[p], s1r.at[p], self.along)
        return remote(sb.at[:, :, 1 - self.x], r1, s1s.at[p], s1r.at[p], self.across)

    def c2(self, p):
        s2s, s2r = self.sems[5:7]
        sb, r2 = self.bufs[p][3], self.bufs[p][5]
        if self.parts[p][3] == 0:
            return remote(sb.at[:, self.y, 1 - self.x], r2, s2s.at[p], s2r.at[p], self.across)
        return remote(sb.at[:, 1 - self.y, self.x], r2, s2s.at[p], s2r.at[p], self.along)

    def c3(self, p, dest, source):
        s3s, s3r = self.sems[7:9]
        sb, r3 = self.bufs[p][3], self.bufs[p][6]
        to = {"shard": dest * PLANE + 2 * self.y + self.x}
        return remote(sb.at[dest, self.y, self.x], r3.at[source], s3s.at[p, dest], s3r.at[p, source], to)

    def into_half(self, p):
        acc, _, r0, sb = self.bufs[p][:4]
        self.c0(p).wait_recv()

        def step(i, carry):
            at = (i // PLANE, (i // 2) % 2, i % 2)
            value = acc[at] + r0[at].astype(F32)
            acc[at] = value
            sb[at] = value.astype(BF16)
            return carry

        lax.fori_loop(0, self.n, step, 0)
        self.c1(p).start()

    def after_first(self, p):
        acc, _, _, sb, r1 = self.bufs[p][:5]
        self.c1(p).wait_recv()
        self.c1(p).wait_send()

        def step(i, carry):
            zz, kk = i // 2, i % 2
            at = (zz, self.y, kk) if self.parts[p][3] == 0 else (zz, kk, self.x)
            value = acc[at] + r1[zz, kk].astype(F32)
            acc[at] = value
            sb[at] = value.astype(BF16)
            return carry

        lax.fori_loop(0, 2 * self.planes, step, 0)
        self.c2(p).start()

    def after_second(self, p):
        acc, _, _, sb, _, r2 = self.bufs[p][:6]
        z, y, x = self.z, self.y, self.x
        self.c2(p).wait_recv()
        self.c2(p).wait_send()
        for zz in range(self.planes):
            value = acc[zz, y, x] + r2[zz].astype(F32)
            acc[zz, y, x] = value
            sb[zz, y, x] = value.astype(BF16)
        for dest in range(self.planes):
            @pl.when(dest != z)
            def _():
                self.c3(p, dest, z).start()

    def results(self, p):
        own, s4s, s4r = self.sems[0], *self.sems[9:11]
        _, start, size, _ = self.parts[p]
        acc = self.bufs[p][0]
        rows = acc.shape[3]
        view = self.out.at[pl.ds(pl.multiple_of(self.core * rows, 8), rows), pl.ds(start, size)]
        mine = acc.at[self.z, self.y, self.x]
        return remote(mine, view, s4s.at[p], s4r.at[p], self.twin), pltpu.make_async_copy(mine, view, own.at[p])

    def finish(self, p):
        acc, r3 = self.bufs[p][0], self.bufs[p][6]
        for source in range(self.planes):
            @pl.when(source != self.z)
            def _():
                self.c3(p, source, source).wait_recv()
                acc[self.z, self.y, self.x] += r3[source].astype(F32)

        for copy in self.results(p):
            copy.start()

    def close(self, p):
        self.c0(p).wait_send()
        for dest in range(self.planes):
            @pl.when(dest != self.z)
            def _():
                self.c3(p, dest, self.z).wait_send()

        far, near = self.results(p)
        near.wait()
        far.wait()


def backward_exchange_kernel(n, *refs):
    len_ref, ord_ref, out_ref, glt_ref, cot_ref = refs[:5]
    blocks = refs[5:21]
    ig_ref, gp_ref, few_ref, slot_ref, gout_ref, out_stage = refs[21:27]
    scratch = refs[27:48]
    gb_v, out_s, out_r, out_fs, out_fr, out_l = refs[48:54]
    red = Reduction(n, OUT_PARTS, gout_ref, refs[54:])
    planes = n // PLANE
    step = pl.program_id(0)
    me = lax.axis_index("shard")
    z, quad = me // PLANE, me % PLANE
    piece = slot_ref.shape[1]
    width = cot_ref.shape[1]
    moves = ((out_stage, slot_ref, out_fs, out_fr, out_l),)

    def span(c):
        return pl.ds(pl.multiple_of(c * SPAN, SPAN), SPAN)

    def out_copy(to, source):
        return remote(
            out_ref.at[span(to)], out_stage.at[source], out_s.at[to], out_r.at[source], {"shard": to * PLANE + quad}
        )

    def own_out():
        return pltpu.make_async_copy(out_ref.at[span(z)], out_stage.at[z], out_l.at[planes])

    def pass_copy(m, zz, j, source):
        stage, dst, ss, sr, _ = moves[m]
        return remote(
            stage.at[zz, pl.ds(j * piece, piece)], dst.at[zz * PLANE + source], ss.at[zz, j], sr.at[zz, source],
            {"shard": z * PLANE + j},
        )

    def keep_copy(m, zz):
        stage, dst, _, _, sem = moves[m]
        rows = pl.ds(pl.multiple_of(quad * piece, piece), piece)
        return pltpu.make_async_copy(stage.at[zz, rows], dst.at[zz * PLANE + quad], sem.at[zz])

    def pass_on(m):
        for zz in range(planes):
            for j in range(PLANE):
                @pl.when(j != quad)
                def _():
                    pass_copy(m, zz, j, quad).start()

            keep_copy(m, zz).start()

    def landed(m):
        for zz in range(planes):
            for j in range(PLANE):
                @pl.when(j != quad)
                def _():
                    pass_copy(m, zz, j, quad).wait_send()
                    pass_copy(m, zz, j, j).wait_recv()

            keep_copy(m, zz).wait()

    @pl.when(step == 0)
    def _():
        barrier = pltpu.get_barrier_semaphore()
        for d in range(1, PLANE):
            near = z * PLANE + lax.rem(quad + d, PLANE)
            pl.semaphore_signal(barrier, inc=1, device_id={"shard": near}, device_id_type=MESH)
        for d in range(1, planes):
            far = lax.rem(z + d, planes) * PLANE + quad
            pl.semaphore_signal(barrier, inc=1, device_id={"shard": far}, device_id_type=MESH)
        pl.semaphore_signal(barrier, inc=1, device_id=red.twin, device_id_type=MESH)
        own_out().start()
        length = own_length(len_ref, ord_ref)
        for c in range(planes):
            positions = c * SPAN + lax.broadcasted_iota(jnp.int32, (SPAN, width), 0)
            rows = slice(c * SPAN, (c + 1) * SPAN)
            gb_v[rows, :] = jnp.where(positions < length, cot_ref[rows, :].astype(F32), 0.0).astype(BF16)
        pl.semaphore_wait(barrier, PLANE + planes - 1)
        for c in range(planes):
            @pl.when(c != z)
            def _():
                out_copy(c, z).start()

        for p in range(len(OUT_PARTS)):
            red.product(p, glt_ref, gb_v)
            red.c0(p).start()

    @pl.when(step == 1)
    def _():
        for p in range(len(OUT_PARTS)):
            red.into_half(p)

    @pl.when(step == 2)
    def _():
        for p in range(len(OUT_PARTS)):
            red.after_first(p)
        own_out().wait()
        for zz in range(planes):
            @pl.when(zz != z)
            def _():
                out_copy(zz, zz).wait_recv()

        pass_on(0)

    @pl.when(step == 3)
    def _():
        for p in range(len(OUT_PARTS)):
            red.after_second(p)

    rows = span(planes - 1 - step)
    backward_kernel(
        n, len_ref, ord_ref, cot_ref.at[rows], *blocks, ig_ref, gp_ref, gb_v.at[rows], few_ref, *scratch
    )

    @pl.when(step == planes - 1)
    def _():
        for p in range(len(OUT_PARTS)):
            red.finish(p)
        for c in range(planes):
            @pl.when(c != z)
            def _():
                out_copy(c, z).wait_send()

        landed(0)
        for p in range(len(OUT_PARTS)):
            red.close(p)


def run_backward_exchange(n, lengths, order, out, cot, tok, params, kept, glt):
    length, width = tok.shape
    count, piece, planes = length // SPAN, length // n, n // PLANE
    proj = DI + XBC + HEADS
    last = count - 1
    hbm = pl.BlockSpec(memory_space=pl.ANY)
    dma = pltpu.SemaphoreType.DMA
    shapes = [
        ((length, width), BF16), ((length, proj), BF16), ((n, EDGE, TILE), F32), ((n, piece, width), BF16),
        ((DI // n, width), F32), ((planes, SPAN, width), BF16),
    ]
    passes = [dma((planes,)), dma((planes,)), dma((planes, PLANE)), dma((planes, PLANE)), dma((planes + 1,))]
    return pl.pallas_call(
        functools.partial(backward_exchange_kernel, n),
        grid=(count,),
        out_shape=[jax.ShapeDtypeStruct(s, d) for s, d in shapes],
        in_specs=[
            SCALARS, SCALARS, hbm, whole((DI, length)), whole((length, width)), rows_of(width, last),
            *params_specs(width, params[0].shape[1]), *kept_blocks(last),
        ],
        out_specs=[rows_of(width, last), rows_of(proj, last), whole(shapes[2][0])] + [hbm] * 3,
        scratch_shapes=backward_scratch(width) + [
            pltpu.VMEM((length, width), BF16), *passes,
        ] + Reduction.scratch(n, OUT_PARTS, DI // n // REP),
        compiler_params=pltpu.CompilerParams(
            dimension_semantics=("arbitrary",), collective_id=2, has_side_effects=True, vmem_limit_bytes=LIMIT
        ),
    )(lengths, order, out, glt, cot, tok, *params, *kept)


def scatter_kernel(n, *refs):
    ig_ref, nl_ref, gp_ref, small_ref, slot_ref, gin_ref, sum_ref = refs[:7]
    nl_t, few, few_sib, ig_s, ig_r, few_s, few_r, pair_s, pair_r, own = refs[7:17]
    red = Reduction(n, IN_PARTS, gin_ref, refs[17:])
    me = lax.axis_index("shard")
    z = me // PLANE
    piece = slot_ref.shape[1]

    barrier = pltpu.get_barrier_semaphore()
    for d in range(1, n):
        pl.semaphore_signal(barrier, inc=1, device_id={"shard": lax.rem(me + d, n)}, device_id_type=MESH)
    pl.semaphore_signal(barrier, inc=1, device_id=red.twin, device_id_type=MESH)

    def ig_copy(d):
        to = lax.rem(me + d, n)
        src = ig_ref.at[pl.ds(pl.multiple_of(to * piece, piece), piece)]
        return remote(src, slot_ref.at[me], ig_s.at[d], ig_r.at[d], {"shard": to})

    def igs(first, last):
        for d in range(first, last):
            ig_copy(d).start()

    own_slot = pltpu.make_async_copy(ig_ref.at[pl.ds(pl.multiple_of(me * piece, piece), piece)], slot_ref.at[me], own)

    def few_copy(d):
        to = lax.rem(me + d, n)
        return remote(small_ref.at[to], few.at[me], few_s.at[d], few_r.at[d], {"shard": to})

    nl_t[...] = nl_ref[...].T
    for p in (0, 1):
        red.product(p, nl_t, gp_ref)
    pl.semaphore_wait(barrier, n)
    for p in (0, 1):
        red.c0(p).start()
    own_slot.start()
    igs(*SPREAD[0:2])
    for d in range(1, n):
        few_copy(d).start()
    for p in (2, 3):
        red.product(p, nl_t, gp_ref)
        red.c0(p).start()
    for p in (0, 1):
        red.into_half(p)
    igs(*SPREAD[1:3])
    for p in (2, 3):
        red.into_half(p)
    igs(*SPREAD[2:4])
    for p in (0, 1):
        red.after_first(p)
    igs(*SPREAD[3:5])
    for p in (0, 1):
        red.after_second(p)
    for p in (2, 3):
        red.after_first(p)
    for p in (0, 1):
        red.finish(p)
    few[me] = small_ref[me]
    for d in range(1, n):
        few_copy(d).wait()
    total = few[0]
    for k in range(1, n):
        total = total + few[k]
    few_sib[0] = total
    pair = remote(few_sib.at[0], few_sib.at[1], pair_s, pair_r, red.twin)
    pair.start()
    for p in (2, 3):
        red.after_second(p)
    for p in (2, 3):
        red.finish(p)
    pair.wait()
    sum_ref[...] = few_sib[0] + few_sib[1]
    own_slot.wait()
    for d in range(1, n):
        ig_copy(d).wait()
    for p in range(len(IN_PARTS)):
        red.close(p)


def run_scatter(n, ig, normed, gp, small):
    length, width = normed.shape
    piece = length // n
    few = small.shape[1:]
    vmem, hbm = pl.BlockSpec(memory_space=pltpu.VMEM), pl.BlockSpec(memory_space=pl.ANY)
    dma = pltpu.SemaphoreType.DMA
    shapes = [((n, piece, width), BF16), ((width // n, gp.shape[1]), F32), (few, F32)]
    return pl.pallas_call(
        functools.partial(scatter_kernel, n),
        out_shape=[jax.ShapeDtypeStruct(s, d) for s, d in shapes],
        in_specs=[hbm, vmem, vmem, vmem],
        out_specs=[hbm, hbm, vmem],
        scratch_shapes=[
            pltpu.VMEM((width, length), BF16), pltpu.VMEM((n, *few), F32), pltpu.VMEM((2, *few), F32),
            dma((n,)), dma((n,)), dma((n,)), dma((n,)), dma(()), dma(()), dma(()),
        ] + Reduction.scratch(n, IN_PARTS, width // n // REP),
        compiler_params=pltpu.CompilerParams(collective_id=1, has_side_effects=True, vmem_limit_bytes=LIMIT),
    )(ig, normed, gp, small)


def on_device(
    tokens, cotangent, lengths, order, norm_weight, in_weight, conv_weight, conv_bias,
    step_bias, decay_log, skip_gain, gate_norm_weight, out_weight,
):
    peers = lax.axis_size("shard")
    piece, width = tokens.shape[1:]

    def gather(x):
        return lax.all_gather(x, "shard", axis=0, tiled=True)

    def to_sequences(x):
        parts = x.reshape(peers, 1, piece, width)
        return lax.all_to_all(parts, "shard", split_axis=0, concat_axis=2, tiled=True).reshape(peers * piece, width)

    def to_slots(x):
        parts = x.reshape(peers, piece, width)
        return lax.all_to_all(parts, "shard", split_axis=0, concat_axis=0, tiled=True)

    direct = peers == PLANE * PLANE and lax.axis_size("rep") == REP and peers * piece == PLANE * SPAN
    if direct:
        pieces = (norm_weight[None], conv_weight.T, conv_bias[None], gate_norm_weight[None])
        heads = (step_bias[None], decay_log[None], skip_gain[None])
        forward, gathered = run_gather_forward(lengths, order, tokens, cotangent, in_weight, out_weight, pieces, heads)
        out, cin, gr, mx, st, sr, normed, gate_low, ar = forward
        tok, cot, params = gathered[0], gathered[1], gathered[2:]
    else:
        tok, cot = to_sequences(tokens), to_sequences(cotangent)
        params = prepare(
            gather(norm_weight), gather(in_weight), gather(conv_weight), gather(conv_bias),
            gather(gate_norm_weight), gather(out_weight), step_bias, decay_log, skip_gain,
        )
        out, cin, gr, mx, st, sr, normed, gate_low, ar = run_forward(lengths, order, tok, params)
    kept = (cin, gr, mx, st, sr, ar)
    if direct:
        results = run_backward_exchange(peers, lengths, order, out, cot, tok, params, kept, gate_low)
        ig, gp, few, output, grad_out = results[:5]
        input_grad, grad_in, few = run_scatter(peers, ig, normed, gp, few)
    else:
        output = to_slots(out)
        ig, gp, gb, few = run_backward(peers, lengths, order, cot, tok, params, kept)
        input_grad = to_slots(ig)

        def scatter(v):
            return lax.psum(lax.psum_scatter(v, "shard", scatter_dimension=0, tiled=True), "rep")

        grad_in, grad_out = scatter(mul_tn(normed, gp)), scatter(mul(gate_low, gb))
        parts = scatter(few[:, : EDGE - 1])
        few = jnp.concatenate([parts[0], lax.psum(few[0, EDGE - 1 :], ("rep", "shard"))])
    few, heads = run_split(few, norm_weight.size, conv_bias.size, gate_norm_weight.size)
    return (
        output, input_grad, few[0], grad_in, few[1], few[2], heads[0], heads[1], heads[2], few[3], grad_out,
    )


def solution(mesh):
    placed = (
        P("rep", "shard", None), P("rep", "shard", None), P("rep", None), P("rep", None), P("shard"),
        P("shard", None), P("shard", None), P("shard"), P(), P(), P(), P("shard"), P("shard", None),
    )
    outs = (
        P("rep", "shard", None), P("rep", "shard", None), P("shard"), P("shard", None), P("shard", None),
        P("shard"), P(), P(), P(), P("shard"), P("shard", None),
    )
    return jax.shard_map(on_device, mesh=mesh, in_specs=placed, out_specs=outs, check_vma=False)
```
